128 devices in a mesh: rows: 8 (over y, x_hi), cols: 16 (over x_lo, z, core).
Axes of the slice: x: 4 (x_hi: 2, x_lo: 2; x = x_hi * 2 + x_lo), y: 4, z: 4, core: 2. Of those that a mesh axis runs over, the one named last changes fastest.
Arguments:
- object_field: float32 [2, 2048, 4096], P(None, 'rows', 'cols'), may hold values from -6 to 6
- probe: float32 [2, 256, 256], replicated, may hold values from -6 to 6
- positions: int32 [8, 16, 6, 2], P('rows', 'cols'), may hold values from 0 to 256
- counts: int32 [8, 16], P('rows', 'cols'), may hold values from 2 to 6
- intensity: int32 [8, 16, 6, 256, 256], P('rows', 'cols'), may hold values from 0 to 4000
Outputs:
- updated_field: float32 [2, 2048, 4096], P(None, 'rows', 'cols')
The draws below stay inside these ranges and needn't reach their ends.
Inputs may be any that keep to these rules, and one draw needn't show every extreme that they name: Only the first counts[a, b] entries of tile (a, b) in positions and intensity are used.
All inputs are finite; a program needn't handle non-finite values.
Results may differ from the reference program's by a relative error of at most 0.00029.
Values sent between devices are 32-bit elements; how exact they have to be, the bound alone decides.
No kernel may reach another device: no remote copies, remote signals or barrier semaphores. Data moves between devices by JAX's collectives and lax.ppermute only.
A program may use at most 64 MiB of HBM per device.

```python
import jax
import jax.numpy as jnp
from jax import lax

TILE = 256
MARGIN = 128
PATCH = 256
SLOTS = 6
ITERS = 2
IMG_R = 2048
IMG_C = 4096
N_ROWS = 8
N_COLS = 16


def with_ends(values, rng, low, high):
    dims = values.shape
    place = [jax.random.randint(jax.random.fold_in(rng, axis), (), 0, dims[axis]) for axis in range(len(dims))]
    values = values.at[tuple(place)].set(low)
    longest = dims.index(max(dims))
    place[longest] = (place[longest] + 1) % dims[longest]
    return values.at[tuple(place)].set(high)


def levels(rng, shape, pieces, least, high):
    def one(dim, parts):
        steps = jax.random.uniform(jax.random.fold_in(jax.random.fold_in(rng, 6), dim), (parts,), jnp.float32, least / len(pieces), high / len(pieces))
        return jnp.repeat(jnp.exp(steps), shape[dim] // parts).reshape((-1,) + (1,) * (len(shape) - dim - 1))

    loudness = one(*pieces[0])
    for cut in pieces[1:]:
        loudness = loudness * one(*cut)
    return loudness


def scatter_about(rng, extent, width, bound, split=(), kind=jnp.bfloat16):
    level = levels(rng, extent, split, -0.22, 0.18) if split else 1.0
    result = jax.random.normal(rng, extent, jnp.float32) * width * level
    return jnp.minimum(jnp.maximum(result, -bound), bound).astype(kind)


def setup_inputs(seed: int = 0) -> dict:
    keys = jax.random.split(jax.random.key(seed), 6)
    object_field = scatter_about(keys[0], (2, IMG_R, IMG_C), 1.0, 6.0, ((1, 8), (2, 16)), jnp.float32)
    probe = scatter_about(keys[1], (2, PATCH, PATCH), 1.0, 6.0, (), jnp.float32)
    positions = with_ends(jax.random.randint(keys[2], (N_ROWS, N_COLS, SLOTS, 2), 0, TILE + 2 * MARGIN - PATCH + 1), jax.random.fold_in(keys[2], 1), 0, TILE + 2 * MARGIN - PATCH).astype(jnp.int32)
    counts = with_ends(jax.random.randint(keys[3], (N_ROWS, N_COLS), 2, SLOTS + 1), jax.random.fold_in(keys[3], 1), 2, SLOTS).astype(jnp.int32)
    intensity = with_ends(jax.random.randint(keys[4], (N_ROWS, N_COLS, SLOTS, PATCH, PATCH), 0, 4001), jax.random.fold_in(keys[4], 1), 0, 4000).astype(jnp.int32)
    return {"object_field": object_field, "probe": probe, "positions": positions, "counts": counts, "intensity": intensity}


step_rate = 0.02
photon_unit = 0.001


def reference(object_field, probe, positions, counts, intensity):
    field = object_field
    probe_c = lax.complex(probe[0], probe[1])
    measured = intensity.astype(field.dtype) * photon_unit
    total = N_ROWS * N_COLS * SLOTS
    for step in range(ITERS):
        padded = jnp.pad(field, ((0, 0), (MARGIN, MARGIN), (MARGIN, MARGIN)))

        def one(item, grad):
            tile = item // SLOTS
            slot = item % SLOTS
            trow = tile // N_COLS
            tcol = tile % N_COLS
            srow = (positions[trow, tcol, slot, 0] + trow * TILE).astype(jnp.int32)
            scol = (positions[trow, tcol, slot, 1] + tcol * TILE).astype(jnp.int32)
            zero = jnp.zeros((), jnp.int32)
            patch = lax.dynamic_slice(padded, (zero, srow, scol), (2, PATCH, PATCH))
            exit_wave = probe_c * lax.complex(patch[0], patch[1])
            spectrum = jnp.fft.fft2(exit_wave, norm="ortho")
            misfit = jnp.real(spectrum) ** 2 + jnp.imag(spectrum) ** 2 - measured[trow, tcol, slot]
            back = jnp.fft.ifft2(misfit * spectrum, norm="ortho")
            term = jnp.conj(probe_c) * back
            live = (slot < counts[trow, tcol]).astype(field.dtype)
            stacked = jnp.stack([jnp.real(term), jnp.imag(term)]) * live
            old = lax.dynamic_slice(grad, (zero, srow, scol), (2, PATCH, PATCH))
            return lax.dynamic_update_slice(grad, old + stacked, (zero, srow, scol))

        grad = lax.fori_loop(0, total, one, jnp.zeros_like(padded))
        field = field - step_rate * grad[:, MARGIN:MARGIN + IMG_R, MARGIN:MARGIN + IMG_C]
    return field
```

```python
import functools

import jax
import jax.numpy as jnp
import numpy as np
from jax import lax
from jax.experimental import pallas as pl
from jax.experimental.pallas import tpu as pltpu
from jax.sharding import PartitionSpec as P

MARGIN = 128
HALF = 128


step_rate = 0.02
photon_unit = 0.001


def rotation_tables(length):
    half = length // 2
    index = np.arange(half, dtype=np.int64)
    angle = (index[:, None] * index[None, :] % half) * (2.0 * np.pi / half)
    norm = 1.0 / np.sqrt(length)
    cosine = np.cos(angle) * norm
    sine = np.sin(angle) * norm
    mixed = np.block([[cosine, -sine], [sine, cosine]]).astype(np.float32)
    turn = index * (2.0 * np.pi / length)
    twiddle = np.stack([np.cos(turn), -np.sin(turn)]).astype(np.float32)
    return mixed, twiddle


def split_order(length):
    half = length // 2
    order = np.concatenate([np.arange(half) * 2, np.arange(half) * 2 + 1])
    return (np.arange(length)[:, None] == order[None, :]).astype(np.float32)


def prepare_body(positions, intensity, probe, order, measured, rolled):
    slots = intensity.shape[0]
    size = probe.shape[1]
    half = size // 2
    moves = order[...]

    def one_slot(slot, carry):
        scol = positions[slot, 1]
        shift = lax.rem(scol, size)
        for part in range(2):
            rolled[slot, part] = pltpu.roll(probe[part], shift, 1)
        full = intensity[slot]
        for parity in range(2):
            counts = full.reshape(half, 2, size)[:, parity, :]
            upper = lax.shift_right_logical(counts, 8).astype(jnp.float32).astype(jnp.bfloat16)
            lower = lax.bitwise_and(counts, 255).astype(jnp.float32).astype(jnp.bfloat16)
            moved = 256.0 * jnp.dot(upper, moves, preferred_element_type=jnp.float32)
            moved = moved + jnp.dot(lower, moves, preferred_element_type=jnp.float32)
            measured[slot, parity] = moved * photon_unit
        return carry

    lax.fori_loop(0, slots, one_slot, 0)


def prepare(positions, intensity, probe, order):
    slots, size = intensity.shape[0], probe.shape[1]
    vmem = pl.BlockSpec(memory_space=pltpu.VMEM)
    return pl.pallas_call(
        prepare_body,
        out_shape=(
            jax.ShapeDtypeStruct((slots, 2, size // 2, size), jnp.float32),
            jax.ShapeDtypeStruct((slots, 2, size, size), jnp.float32),
        ),
        in_specs=[pl.BlockSpec(memory_space=pltpu.SMEM), vmem, vmem, vmem],
        out_specs=(vmem, vmem),
        compiler_params=pltpu.CompilerParams(vmem_limit_bytes=32 << 20),
        cost_estimate=pl.CostEstimate(flops=slots * 2**27, bytes_accessed=8 << 20, transcendentals=0),
    )(positions, intensity, probe, order)


def halves(value):
    upper = value.astype(jnp.bfloat16)
    lower = (value - upper.astype(jnp.float32)).astype(jnp.bfloat16)
    return upper, lower


def times_table(value, table):
    upper, lower = halves(value)
    packed = jnp.concatenate([upper, lower, upper], axis=1)
    return jnp.dot(packed, table, preferred_element_type=jnp.float32)


def table_times(table, value):
    upper, lower = halves(value)
    packed = jnp.concatenate([upper, lower, upper], axis=0)
    return jnp.dot(table, packed, preferred_element_type=jnp.float32)


def wide(left, right):
    return jnp.concatenate([left, right], axis=1)


def tall(upper, lower):
    return jnp.concatenate([upper, lower], axis=0)


def gradient_body(
    info, positions, counts, ext, strip_a, strip_b, measured, rolled, fore_lane, fore_row, back_row, back_lane,
    twist_lane, twist_row,    out_a, out_b, inner, sides, outer
):
    size = rolled.shape[2]
    half = size // 2
    odd_col = info[1]
    lanes = lax.broadcasted_iota(jnp.int32, (1, half), 1)
    inner[...] = jnp.zeros_like(inner)
    outer[...] = jnp.zeros_like(outer)
    sides[0] = jnp.where(info[4] == 1, 0.0, jnp.where(odd_col == 1, strip_a[0], strip_b[0]))
    sides[1] = jnp.where(info[5] == 1, 0.0, jnp.where(odd_col == 1, strip_b[1], strip_a[1]))

    def one_slot(slot, carry):
        srow = positions[slot, 0]
        scol = positions[slot, 1]
        rows = pl.ds(srow, size)
        near = [lanes + half * block >= scol for block in range(2)]
        blocks = [
            lambda part: sides[0, part, rows, :],
            lambda part: ext[part, 0, rows, :],
            lambda part: ext[part, 1, rows, :],
            lambda part: sides[1, part, rows, :],
        ]

        def patch(part, block):
            return jnp.where(near[block], blocks[block](part), blocks[block + 2](part))

        def probe(part, block):
            return rolled[slot, part, :, half * block : half * (block + 1)]

        lane_r, lane_i = twist_lane[0], twist_lane[1]
        row_r, row_i = twist_row[0], twist_row[1]
        waves = []
        for block in range(2):
            p_r, p_i = probe(0, block), probe(1, block)
            o_r, o_i = patch(0, block), patch(1, block)
            waves.append((p_r * o_r - p_i * o_i, p_r * o_i + p_i * o_r))
        (r0, i0), (r1, i1) = waves
        even = wide(r0 + r1, i0 + i1)
        d_r, d_i = r0 - r1, i0 - i1
        odd = wide(d_r * lane_r - d_i * lane_i, d_r * lane_i + d_i * lane_r)
        even = times_table(even, fore_lane[...])
        odd = times_table(odd, fore_lane[...])
        halves_r = wide(even[:, :half], odd[:, :half])
        halves_i = wide(even[:, half:], odd[:, half:])
        r0, r1 = halves_r[:half], halves_r[half:]
        i0, i1 = halves_i[:half], halves_i[half:]
        even = tall(r0 + r1, i0 + i1)
        d_r, d_i = r0 - r1, i0 - i1
        odd = tall(d_r * row_r - d_i * row_i, d_r * row_i + d_i * row_r)
        spectra = [table_times(fore_row[...], even), table_times(fore_row[...], odd)]
        scaled = []
        for parity, spectrum in enumerate(spectra):
            s_r, s_i = spectrum[:half], spectrum[half:]
            misfit = s_r * s_r + s_i * s_i - measured[slot, parity]
            scaled.append(tall(misfit * s_r, misfit * s_i))
        even = table_times(back_row[...], scaled[0])
        odd = table_times(back_row[...], scaled[1])
        e_r, e_i = even[:half], even[half:]
        o_r, o_i = odd[:half], odd[half:]
        t_r = o_r * row_r + o_i * row_i
        t_i = o_i * row_r - o_r * row_i
        full_r = tall(e_r + t_r, e_r - t_r)
        full_i = tall(e_i + t_i, e_i - t_i)
        even = times_table(wide(full_r[:, :half], full_i[:, :half]), back_lane[...])
        odd = times_table(wide(full_r[:, half:], full_i[:, half:]), back_lane[...])
        e_r, e_i = even[:, :half], even[:, half:]
        o_r, o_i = odd[:, :half], odd[:, half:]
        t_r = o_r * lane_r + o_i * lane_i
        t_i = o_i * lane_r - o_r * lane_i
        outs = [(e_r + t_r, e_i + t_i), (e_r - t_r, e_i - t_i)]
        for block, (b_r, b_i) in enumerate(outs):
            p_r, p_i = probe(0, block), probe(1, block)
            terms = (p_r * b_r + p_i * b_i, p_r * b_i - p_i * b_r)
            for part, term in enumerate(terms):
                low = jnp.where(near[block], term, 0.0)
                high = jnp.where(near[block], 0.0, term)
                if block == 0:
                    outer[0, part, rows, :] += low
                    inner[part, 1, rows, :] += high
                else:
                    inner[part, 0, rows, :] += low
                    outer[1, part, rows, :] += high
        return carry

    lax.fori_loop(0, counts[0, 0], one_slot, 0)
    out_a[...] = outer[1 - odd_col]
    out_b[...] = outer[odd_col]


VMEM = pl.BlockSpec(memory_space=pltpu.VMEM)
SMEM = pl.BlockSpec(memory_space=pltpu.SMEM)


def shaped(*dims):
    return jax.ShapeDtypeStruct(dims, jnp.float32)


def whole(body, outs, scalars, arrays, scratch=(), limit=40 << 20, flops=1 << 20):
    return pl.pallas_call(
        body,
        out_shape=outs,
        in_specs=[SMEM] * len(scalars) + [VMEM] * len(arrays),
        out_specs=tuple(VMEM for _ in outs),
        scratch_shapes=scratch,
        compiler_params=pltpu.CompilerParams(vmem_limit_bytes=limit),
        cost_estimate=pl.CostEstimate(flops=flops, bytes_accessed=8 << 20, transcendentals=0),
    )(*scalars, *arrays)


def gradient(info, positions, counts, ext, strip_a, strip_b, measured, rolled, tables):
    extent = ext.shape[2]
    strip = shaped(2, extent, HALF)
    return whole(
        gradient_body,
        (strip, strip, shaped(2, 2, extent, HALF)),
        (info, positions, counts),
        (ext, strip_a, strip_b, measured, rolled, *tables),
        [pltpu.VMEM((2, 2, extent, HALF), jnp.float32)] * 2,
        flops=6 * 8 * 3 * 2**25,
    )


def extend_body(info, tile, halo_a, halo_b, ext, out_a, out_b):
    size = tile.shape[1]
    odd_row, odd_col = info[0], info[1]
    top, bottom = info[2], info[3]
    above = jnp.where(top == 1, 0.0, jnp.where(odd_row == 1, halo_a[0], halo_b[0]))
    below = jnp.where(bottom == 1, 0.0, jnp.where(odd_row == 1, halo_b[1], halo_a[1]))
    for block in range(2):
        cut = slice(block * HALF, (block + 1) * HALF)
        ext[:, block, :MARGIN] = above[:, :, cut]
        ext[:, block, MARGIN : MARGIN + size] = tile[:, :, cut]
        ext[:, block, MARGIN + size :] = below[:, :, cut]
    for part in range(2):
        out_a[part] = ext[part, 1 - odd_col]
        out_b[part] = ext[part, odd_col]


def join_body(width, info, inner, strip_a, strip_b, total, out_a, out_b):
    extent = inner.shape[2]
    odd_row, odd_col = info[0], info[1]
    low = jnp.where(info[4] == 1, 0.0, jnp.where(odd_col == 1, strip_a[0], strip_b[0]))
    high = jnp.where(info[5] == 1, 0.0, jnp.where(odd_col == 1, strip_b[1], strip_a[1]))
    total[:, 0] = inner[:, 0] + low
    total[:, 1] = inner[:, 1] + high
    upper = pl.multiple_of((1 - odd_row) * (extent - width), 8)
    lower = pl.multiple_of(odd_row * (extent - width), 8)
    out_a[...] = total[:, :, pl.ds(upper, width), :]
    out_b[...] = total[:, :, pl.ds(lower, width), :]


def update_body(info, ext, total, halo_a, halo_b, out, out_a, out_b):
    middle = total.shape[2] // 2
    odd_row, odd_col = info[0], info[1]
    top, bottom = info[2], info[3]
    above = jnp.where(top == 1, 0.0, jnp.where(odd_row == 1, halo_a[0], halo_b[0]))
    below = jnp.where(bottom == 1, 0.0, jnp.where(odd_row == 1, halo_b[1], halo_a[1]))
    row = lax.broadcasted_iota(jnp.int32, (1, 1, middle, HALF), 2)
    above = jnp.where((top == 1) & (row < MARGIN), 0.0, total[:, :, :middle] + above)
    below = jnp.where((bottom == 1) & (row >= middle - MARGIN), 0.0, total[:, :, middle:] + below)
    out[:, :, :middle] = ext[:, :, :middle] - step_rate * above
    out[:, :, middle:] = ext[:, :, middle:] - step_rate * below
    for part in range(2):
        out_a[part] = out[part, 1 - odd_col]
        out_b[part] = out[part, odd_col]


def finish_body(info, ext, total, halo_a, halo_b, out):
    size = out.shape[1]
    half = size // 2
    odd_row = info[0]
    above = jnp.where(info[2] == 1, 0.0, jnp.where(odd_row == 1, halo_a[0], halo_b[0]))
    below = jnp.where(info[3] == 1, 0.0, jnp.where(odd_row == 1, halo_b[1], halo_a[1]))
    for block in range(2):
        cut = slice(block * HALF, (block + 1) * HALF)
        upper = slice(MARGIN, MARGIN + half)
        lower = slice(MARGIN + half, MARGIN + size)
        out[:, :half, cut] = ext[:, block, upper] - step_rate * (total[:, block, upper] + above[:, block])
        out[:, half:, cut] = ext[:, block, lower] - step_rate * (total[:, block, lower] + below[:, block])


def constants(size):
    half = size // 2
    mixed, twiddle = rotation_tables(size)
    upper = mixed.astype(jnp.bfloat16)
    lower = (mixed - upper.astype(np.float32)).astype(jnp.bfloat16)
    fore_lane = jnp.asarray(np.concatenate([upper, upper, lower], axis=0))
    back_row = jnp.asarray(np.concatenate([upper, upper, lower], axis=1))
    fore_row = jnp.asarray(np.concatenate([upper.T, upper.T, lower.T], axis=1))
    back_lane = jnp.asarray(np.concatenate([upper.T, upper.T, lower.T], axis=0))
    twist_lane = jnp.asarray(twiddle.reshape(2, 1, half))
    twist_row = jnp.asarray(np.ascontiguousarray(np.broadcast_to(twiddle[:, :, None], (2, half, size))))
    return fore_lane, fore_row, back_row, back_lane, twist_lane, twist_row


def pairs(count, first):
    return [[i, (i + 1) % count] for i in range(first, count, 2)]


def gathered(value_a, value_b, axis):
    count = lax.axis_size(axis)
    return tuple(
        lax.all_gather(value, axis, axis_index_groups=pairs(count, first))
        for first, value in enumerate((value_a, value_b))
    )


def on_device(object_field, probe, positions, counts, intensity):
    size = probe.shape[1]
    tile = object_field.shape[1]
    extent = tile + 2 * MARGIN
    row, col = lax.axis_index("rows"), lax.axis_index("cols")
    n_rows, n_cols = lax.axis_size("rows"), lax.axis_size("cols")
    info = jnp.stack(
        [row % 2, col % 2, row == 0, row == n_rows - 1, col == 0, col == n_cols - 1]
    ).astype(jnp.int32)
    tables = constants(size)
    order = jnp.asarray(split_order(size)).astype(jnp.bfloat16)
    positions, intensity = positions[0, 0], intensity[0, 0]
    strip = shaped(2, extent, HALF)
    block = shaped(2, 2, extent, HALF)

    edge = tile - MARGIN
    edge_a = lax.dynamic_slice_in_dim(object_field, (1 - row % 2) * edge, MARGIN, 1)
    edge_b = lax.dynamic_slice_in_dim(object_field, (row % 2) * edge, MARGIN, 1)
    halos = gathered(edge_a, edge_b, "rows")
    measured, rolled = prepare(positions, intensity, probe, order)
    ext, side_a, side_b = whole(extend_body, (block, strip, strip), (info,), (object_field, *halos))
    sides = gathered(side_a, side_b, "cols")
    side_a, side_b, inner = gradient(info, positions, counts, ext, *sides, measured, rolled, tables)
    sides = gathered(side_a, side_b, "cols")
    width = extent // 2
    part = shaped(2, 2, width, HALF)
    total, edge_a, edge_b = whole(
        functools.partial(join_body, width), (block, part, part), (info,), (inner, *sides)
    )
    halos = gathered(edge_a, edge_b, "rows")
    ext, side_a, side_b = whole(update_body, (block, strip, strip), (info,), (ext, total, *halos))
    sides = gathered(side_a, side_b, "cols")
    side_a, side_b, inner = gradient(info, positions, counts, ext, *sides, measured, rolled, tables)
    sides = gathered(side_a, side_b, "cols")
    part = shaped(2, 2, MARGIN, HALF)
    total, edge_a, edge_b = whole(
        functools.partial(join_body, MARGIN), (block, part, part), (info,), (inner, *sides)
    )
    halos = gathered(edge_a, edge_b, "rows")
    return whole(finish_body, (shaped(2, tile, tile),), (info,), (ext, total, *halos))[0]


def solution(mesh):
    placed = (
        P(None, "rows", "cols"),
        P(),
        P("rows", "cols", None, None),
        P("rows", "cols"),
        P("rows", "cols", None, None, None),
    )
    return jax.shard_map(
        on_device, mesh=mesh, in_specs=placed, out_specs=P(None, "rows", "cols"), check_vma=False
    )
```

```python
import functools

import jax
import jax.numpy as jnp
import numpy as np
from jax import lax
from jax.experimental import pallas as pl
from jax.experimental.pallas import tpu as pltpu
from jax.sharding import PartitionSpec as P

MARGIN = 128
HALF = 128


step_rate = 0.02
photon_unit = 0.001


def rotation_tables(length):
    half = length // 2
    index = np.arange(half, dtype=np.int64)
    angle = (index[:, None] * index[None, :] % half) * (2.0 * np.pi / half)
    norm = 1.0 / np.sqrt(length)
    cosine = np.cos(angle) * norm
    sine = np.sin(angle) * norm
    mixed = np.block([[cosine, -sine], [sine, cosine]]).astype(np.float32)
    turn = index * (2.0 * np.pi / length)
    twiddle = np.stack([np.cos(turn), -np.sin(turn)]).astype(np.float32)
    return mixed, twiddle


def split_order(length):
    half = length // 2
    order = np.concatenate([np.arange(half) * 2, np.arange(half) * 2 + 1])
    return (np.arange(length)[:, None] == order[None, :]).astype(np.float32)


def prepare_body(positions, intensity, probe, order, measured, rolled):
    slots = intensity.shape[0]
    size = probe.shape[1]
    half = size // 2
    moves = order[...]

    def one_slot(slot, carry):
        scol = positions[slot, 1]
        shift = lax.rem(scol, size)
        for part in range(2):
            rolled[slot, part] = pltpu.roll(probe[part], shift, 1)
        full = intensity[slot]
        for parity in range(2):
            counts = full.reshape(half, 2, size)[:, parity, :]
            upper = lax.shift_right_logical(counts, 8).astype(jnp.float32).astype(jnp.bfloat16)
            lower = lax.bitwise_and(counts, 255).astype(jnp.float32).astype(jnp.bfloat16)
            moved = 256.0 * jnp.dot(upper, moves, preferred_element_type=jnp.float32)
            moved = moved + jnp.dot(lower, moves, preferred_element_type=jnp.float32)
            measured[slot, parity] = moved * photon_unit
        return carry

    lax.fori_loop(0, slots, one_slot, 0)


def prepare(positions, intensity, probe, order):
    slots, size = intensity.shape[0], probe.shape[1]
    vmem = pl.BlockSpec(memory_space=pltpu.VMEM)
    return pl.pallas_call(
        prepare_body,
        out_shape=(
            jax.ShapeDtypeStruct((slots, 2, size // 2, size), jnp.float32),
            jax.ShapeDtypeStruct((slots, 2, size, size), jnp.float32),
        ),
        in_specs=[pl.BlockSpec(memory_space=pltpu.SMEM), vmem, vmem, vmem],
        out_specs=(vmem, vmem),
        compiler_params=pltpu.CompilerParams(vmem_limit_bytes=32 << 20),
        cost_estimate=pl.CostEstimate(flops=slots * 2**27, bytes_accessed=8 << 20, transcendentals=0),
    )(positions, intensity, probe, order)


def halves(value):
    upper = value.astype(jnp.bfloat16)
    lower = (value - upper.astype(jnp.float32)).astype(jnp.bfloat16)
    return upper, lower


def times_table(value, table):
    upper, lower = halves(value)
    packed = jnp.concatenate([upper, lower, upper], axis=1)
    return jnp.dot(packed, table, preferred_element_type=jnp.float32)


def table_times(table, value):
    upper, lower = halves(value)
    packed = jnp.concatenate([upper, lower, upper], axis=0)
    return jnp.dot(table, packed, preferred_element_type=jnp.float32)


def wide(left, right):
    return jnp.concatenate([left, right], axis=1)


def tall(upper, lower):
    return jnp.concatenate([upper, lower], axis=0)


def gradient_body(
    info, positions, counts, ext, strip_a, strip_b, measured, rolled, fore_lane, fore_row, back_row, back_lane,
    twist_lane, twist_row,    out_a, out_b, inner, sides, outer
):
    size = rolled.shape[2]
    half = size // 2
    odd_col = info[1]
    lanes = lax.broadcasted_iota(jnp.int32, (1, half), 1)
    inner[...] = jnp.zeros_like(inner)
    outer[...] = jnp.zeros_like(outer)
    sides[1 - odd_col] = strip_a[...]
    sides[odd_col] = strip_b[...]

    def one_slot(slot, carry):
        srow = positions[slot, 0]
        scol = positions[slot, 1]
        rows = pl.ds(srow, size)
        near = [lanes + half * block >= scol for block in range(2)]
        blocks = [
            lambda part: sides[0, part, rows, :],
            lambda part: ext[part, 0, rows, :],
            lambda part: ext[part, 1, rows, :],
            lambda part: sides[1, part, rows, :],
        ]

        def patch(part, block):
            return jnp.where(near[block], blocks[block](part), blocks[block + 2](part))

        def probe(part, block):
            return rolled[slot, part, :, half * block : half * (block + 1)]

        lane_r, lane_i = twist_lane[0], twist_lane[1]
        row_r, row_i = twist_row[0], twist_row[1]
        waves = []
        for block in range(2):
            p_r, p_i = probe(0, block), probe(1, block)
            o_r, o_i = patch(0, block), patch(1, block)
            waves.append((p_r * o_r - p_i * o_i, p_r * o_i + p_i * o_r))
        (r0, i0), (r1, i1) = waves
        even = wide(r0 + r1, i0 + i1)
        d_r, d_i = r0 - r1, i0 - i1
        odd = wide(d_r * lane_r - d_i * lane_i, d_r * lane_i + d_i * lane_r)
        even = times_table(even, fore_lane[...])
        odd = times_table(odd, fore_lane[...])
        halves_r = wide(even[:, :half], odd[:, :half])
        halves_i = wide(even[:, half:], odd[:, half:])
        r0, r1 = halves_r[:half], halves_r[half:]
        i0, i1 = halves_i[:half], halves_i[half:]
        even = tall(r0 + r1, i0 + i1)
        d_r, d_i = r0 - r1, i0 - i1
        odd = tall(d_r * row_r - d_i * row_i, d_r * row_i + d_i * row_r)
        spectra = [table_times(fore_row[...], even), table_times(fore_row[...], odd)]
        scaled = []
        for parity, spectrum in enumerate(spectra):
            s_r, s_i = spectrum[:half], spectrum[half:]
            misfit = s_r * s_r + s_i * s_i - measured[slot, parity]
            scaled.append(tall(misfit * s_r, misfit * s_i))
        even = table_times(back_row[...], scaled[0])
        odd = table_times(back_row[...], scaled[1])
        e_r, e_i = even[:half], even[half:]
        o_r, o_i = odd[:half], odd[half:]
        t_r = o_r * row_r + o_i * row_i
        t_i = o_i * row_r - o_r * row_i
        full_r = tall(e_r + t_r, e_r - t_r)
        full_i = tall(e_i + t_i, e_i - t_i)
        even = times_table(wide(full_r[:, :half], full_i[:, :half]), back_lane[...])
        odd = times_table(wide(full_r[:, half:], full_i[:, half:]), back_lane[...])
        e_r, e_i = even[:, :half], even[:, half:]
        o_r, o_i = odd[:, :half], odd[:, half:]
        t_r = o_r * lane_r + o_i * lane_i
        t_i = o_i * lane_r - o_r * lane_i
        outs = [(e_r + t_r, e_i + t_i), (e_r - t_r, e_i - t_i)]
        for block, (b_r, b_i) in enumerate(outs):
            p_r, p_i = probe(0, block), probe(1, block)
            terms = (p_r * b_r + p_i * b_i, p_r * b_i - p_i * b_r)
            for part, term in enumerate(terms):
                low = jnp.where(near[block], term, 0.0)
                high = jnp.where(near[block], 0.0, term)
                if block == 0:
                    outer[0, part, rows, :] += low
                    inner[part, 1, rows, :] += high
                else:
                    inner[part, 0, rows, :] += low
                    outer[1, part, rows, :] += high
        return carry

    lax.fori_loop(0, counts[0, 0], one_slot, 0)
    out_a[...] = outer[1 - odd_col]
    out_b[...] = outer[odd_col]


VMEM = pl.BlockSpec(memory_space=pltpu.VMEM)
SMEM = pl.BlockSpec(memory_space=pltpu.SMEM)


def shaped(*dims):
    return jax.ShapeDtypeStruct(dims, jnp.float32)


def whole(body, outs, scalars, arrays, scratch=(), limit=40 << 20, flops=1 << 20):
    return pl.pallas_call(
        body,
        out_shape=outs,
        in_specs=[SMEM] * len(scalars) + [VMEM] * len(arrays),
        out_specs=tuple(VMEM for _ in outs),
        scratch_shapes=scratch,
        compiler_params=pltpu.CompilerParams(vmem_limit_bytes=limit),
        cost_estimate=pl.CostEstimate(flops=flops, bytes_accessed=8 << 20, transcendentals=0),
    )(*scalars, *arrays)


def gradient(info, positions, counts, ext, strip_a, strip_b, measured, rolled, tables):
    extent = ext.shape[2]
    strip = shaped(2, extent, HALF)
    return whole(
        gradient_body,
        (strip, strip, shaped(2, 2, extent, HALF)),
        (info, positions, counts),
        (ext, strip_a, strip_b, measured, rolled, *tables),
        [pltpu.VMEM((2, 2, extent, HALF), jnp.float32)] * 2,
        flops=6 * 8 * 3 * 2**25,
    )


def extend_body(info, tile, halo_a, halo_b, ext, out_a, out_b):
    size = tile.shape[1]
    odd_row, odd_col = info[0], info[1]
    above = jnp.where(odd_row == 1, halo_a[...], halo_b[...])
    below = jnp.where(odd_row == 1, halo_b[...], halo_a[...])
    for block in range(2):
        cut = slice(block * HALF, (block + 1) * HALF)
        ext[:, block, :MARGIN] = above[:, :, cut]
        ext[:, block, MARGIN : MARGIN + size] = tile[:, :, cut]
        ext[:, block, MARGIN + size :] = below[:, :, cut]
    for part in range(2):
        out_a[part] = ext[part, 1 - odd_col]
        out_b[part] = ext[part, odd_col]


def join_body(width, info, inner, strip_a, strip_b, total, out_a, out_b):
    extent = inner.shape[2]
    odd_row, odd_col = info[0], info[1]
    low = jnp.where(odd_col == 1, strip_a[...], strip_b[...])
    high = jnp.where(odd_col == 1, strip_b[...], strip_a[...])
    total[:, 0] = inner[:, 0] + low
    total[:, 1] = inner[:, 1] + high
    upper = pl.multiple_of((1 - odd_row) * (extent - width), 8)
    lower = pl.multiple_of(odd_row * (extent - width), 8)
    out_a[...] = total[:, :, pl.ds(upper, width), :]
    out_b[...] = total[:, :, pl.ds(lower, width), :]


def update_body(info, ext, total, halo_a, halo_b, out, out_a, out_b):
    middle = total.shape[2] // 2
    odd_row, odd_col = info[0], info[1]
    above = jnp.where(odd_row == 1, halo_a[...], halo_b[...])
    below = jnp.where(odd_row == 1, halo_b[...], halo_a[...])
    row = lax.broadcasted_iota(jnp.int32, (1, 1, middle, HALF), 2)
    above = jnp.where((info[2] == 1) & (row < MARGIN), 0.0, total[:, :, :middle] + above)
    below = jnp.where((info[3] == 1) & (row >= middle - MARGIN), 0.0, total[:, :, middle:] + below)
    out[:, :, :middle] = ext[:, :, :middle] - step_rate * above
    out[:, :, middle:] = ext[:, :, middle:] - step_rate * below
    for part in range(2):
        out_a[part] = out[part, 1 - odd_col]
        out_b[part] = out[part, odd_col]


def finish_body(info, ext, total, halo_a, halo_b, out):
    size = out.shape[1]
    half = size // 2
    odd_row = info[0]
    above = jnp.where(odd_row == 1, halo_a[...], halo_b[...])
    below = jnp.where(odd_row == 1, halo_b[...], halo_a[...])
    for block in range(2):
        cut = slice(block * HALF, (block + 1) * HALF)
        upper = slice(MARGIN, MARGIN + half)
        lower = slice(MARGIN + half, MARGIN + size)
        out[:, :half, cut] = ext[:, block, upper] - step_rate * (total[:, block, upper] + above[:, block])
        out[:, half:, cut] = ext[:, block, lower] - step_rate * (total[:, block, lower] + below[:, block])


def constants(size):
    half = size // 2
    mixed, twiddle = rotation_tables(size)
    upper = mixed.astype(jnp.bfloat16)
    lower = (mixed - upper.astype(np.float32)).astype(jnp.bfloat16)
    fore_lane = jnp.asarray(np.concatenate([upper, upper, lower], axis=0))
    back_row = jnp.asarray(np.concatenate([upper, upper, lower], axis=1))
    fore_row = jnp.asarray(np.concatenate([upper.T, upper.T, lower.T], axis=1))
    back_lane = jnp.asarray(np.concatenate([upper.T, upper.T, lower.T], axis=0))
    twist_lane = jnp.asarray(twiddle.reshape(2, 1, half))
    twist_row = jnp.asarray(np.ascontiguousarray(np.broadcast_to(twiddle[:, :, None], (2, half, size))))
    return fore_lane, fore_row, back_row, back_lane, twist_lane, twist_row


def swapped(value, axis, first):
    count = lax.axis_size(axis)
    route = []
    for i in range(first, count - 1, 2):
        route += [(i, i + 1), (i + 1, i)]
    return lax.ppermute(value, axis, route)


def paired(value, axis):
    groups = [[i, i + 1] for i in range(0, lax.axis_size(axis), 2)]
    other = 1 - lax.axis_index(axis) % 2
    parts = []
    for part in range(value.shape[0]):
        both = lax.all_gather(value[part], axis, axis_index_groups=groups)
        parts.append(lax.dynamic_index_in_dim(both, other, 0, keepdims=False))
    return jnp.stack(parts)


def exchanged(value_a, value_b, axis):
    far = swapped(value_b, axis, 1)
    near = paired(value_a, axis) if axis == "cols" else swapped(value_a, axis, 0)
    return near, far


def on_device(object_field, probe, positions, counts, intensity):
    size = probe.shape[1]
    tile = object_field.shape[1]
    extent = tile + 2 * MARGIN
    row, col = lax.axis_index("rows"), lax.axis_index("cols")
    last = lax.axis_size("rows") - 1
    info = jnp.stack([row % 2, col % 2, row == 0, row == last]).astype(jnp.int32)
    tables = constants(size)
    order = jnp.asarray(split_order(size)).astype(jnp.bfloat16)
    positions, intensity = positions[0, 0], intensity[0, 0]
    strip = shaped(2, extent, HALF)
    block = shaped(2, 2, extent, HALF)

    edge = tile - MARGIN
    edge_a = lax.dynamic_slice_in_dim(object_field, (1 - row % 2) * edge, MARGIN, 1)
    edge_b = lax.dynamic_slice_in_dim(object_field, (row % 2) * edge, MARGIN, 1)
    halos = exchanged(edge_a, edge_b, "rows")
    measured, rolled = prepare(positions, intensity, probe, order)
    ext, side_a, side_b = whole(extend_body, (block, strip, strip), (info,), (object_field, *halos))
    sides = exchanged(side_a, side_b, "cols")
    side_a, side_b, inner = gradient(info, positions, counts, ext, *sides, measured, rolled, tables)
    sides = exchanged(side_a, side_b, "cols")
    width = extent // 2
    part = shaped(2, 2, width, HALF)
    total, edge_a, edge_b = whole(
        functools.partial(join_body, width), (block, part, part), (info,), (inner, *sides)
    )
    halos = exchanged(edge_a, edge_b, "rows")
    ext, side_a, side_b = whole(update_body, (block, strip, strip), (info,), (ext, total, *halos))
    sides = exchanged(side_a, side_b, "cols")
    side_a, side_b, inner = gradient(info, positions, counts, ext, *sides, measured, rolled, tables)
    sides = exchanged(side_a, side_b, "cols")
    part = shaped(2, 2, MARGIN, HALF)
    total, edge_a, edge_b = whole(
        functools.partial(join_body, MARGIN), (block, part, part), (info,), (inner, *sides)
    )
    halos = exchanged(edge_a, edge_b, "rows")
    return whole(finish_body, (shaped(2, tile, tile),), (info,), (ext, total, *halos))[0]


def solution(mesh):
    placed = (
        P(None, "rows", "cols"),
        P(),
        P("rows", "cols", None, None),
        P("rows", "cols"),
        P("rows", "cols", None, None, None),
    )
    return jax.shard_map(
        on_device, mesh=mesh, in_specs=placed, out_specs=P(None, "rows", "cols"), check_vma=False
    )
```

```python
import functools

import jax
import jax.numpy as jnp
import numpy as np
from jax import lax
from jax.experimental import pallas as pl
from jax.experimental.pallas import tpu as pltpu
from jax.sharding import PartitionSpec as P

MARGIN = 128
HALF = 128
GROUP = 2


step_rate = 0.02
photon_unit = 0.001


def rotation_tables(length):
    half = length // 2
    index = np.arange(half, dtype=np.int64)
    angle = (index[:, None] * index[None, :] % half) * (2.0 * np.pi / half)
    norm = 1.0 / np.sqrt(length)
    cosine = np.cos(angle) * norm
    sine = np.sin(angle) * norm
    mixed = np.block([[cosine, -sine], [sine, cosine]]).astype(np.float32)
    turn = index * (2.0 * np.pi / length)
    twiddle = np.stack([np.cos(turn), -np.sin(turn)]).astype(np.float32)
    return mixed, twiddle


def split_order(length):
    half = length // 2
    order = np.concatenate([np.arange(half) * 2, np.arange(half) * 2 + 1])
    return (np.arange(length)[:, None] == order[None, :]).astype(np.float32)


VMEM = pl.BlockSpec(memory_space=pltpu.VMEM)
SMEM = pl.BlockSpec(memory_space=pltpu.SMEM)


def shaped(*dims):
    return jax.ShapeDtypeStruct(dims, jnp.float32)


def whole(body, outs, scalars, arrays, scratch=(), limit=40 << 20, flops=1 << 20):
    return pl.pallas_call(
        body,
        out_shape=outs,
        in_specs=[SMEM] * len(scalars) + [VMEM] * len(arrays),
        out_specs=tuple(VMEM for _ in outs),
        scratch_shapes=scratch,
        compiler_params=pltpu.CompilerParams(vmem_limit_bytes=limit),
        cost_estimate=pl.CostEstimate(flops=flops, bytes_accessed=8 << 20, transcendentals=0),
    )(*scalars, *arrays)


def prepare_body(positions, intensity, probe, order, measured, rolled, held, arrived):
    slots, size = intensity.shape[0], probe.shape[1]
    half = size // 2
    moves = [order[:half], order[half:]]
    copies = [
        pltpu.make_async_copy(intensity.at[:, :, pl.ds(half * block, half)], held.at[block], arrived.at[block])
        for block in range(2)
    ]
    for copy in copies:
        copy.start()

    def turn(slot, carry):
        shift = lax.rem(positions[slot, 1], size)
        for part in range(2):
            rolled[slot, part] = pltpu.roll(probe[part], shift, 1)
        return carry

    lax.fori_loop(0, slots, turn, 0)
    for copy in copies:
        copy.wait()

    def reorder(slot, carry):
        for parity in range(2):
            moved = jnp.zeros((half, size), jnp.float32)
            for block in range(2):
                counts = held[block, slot, pl.ds(parity, half, stride=2), :]
                upper = lax.shift_right_logical(counts, 8).astype(jnp.float32).astype(jnp.bfloat16)
                lower = lax.bitwise_and(counts, 255).astype(jnp.float32).astype(jnp.bfloat16)
                high = jnp.dot(upper, moves[block], preferred_element_type=jnp.float32)
                low = jnp.dot(lower, moves[block], preferred_element_type=jnp.float32)
                moved = moved + (256.0 * high + low)
            measured[slot, parity] = moved * photon_unit
        return carry

    lax.fori_loop(0, slots, reorder, 0)


def prepare(positions, intensity, probe, order):
    slots, size = intensity.shape[0], probe.shape[1]
    half = size // 2
    return pl.pallas_call(
        prepare_body,
        out_shape=(shaped(slots, 2, half, size), shaped(slots, 2, size, size)),
        in_specs=[SMEM, pl.BlockSpec(memory_space=pl.ANY), VMEM, VMEM],
        out_specs=(VMEM, VMEM),
        scratch_shapes=[pltpu.VMEM((2, slots, size, half), jnp.int32), pltpu.SemaphoreType.DMA((2,))],
        compiler_params=pltpu.CompilerParams(vmem_limit_bytes=24 << 20),
        cost_estimate=pl.CostEstimate(flops=slots * 2**27, bytes_accessed=8 << 20, transcendentals=0),
    )(positions, intensity, probe, order)


def halves(value):
    upper = value.astype(jnp.bfloat16)
    lower = (value - upper.astype(jnp.float32)).astype(jnp.bfloat16)
    return upper, lower


def times_table(value, table):
    upper, lower = halves(value)
    packed = jnp.concatenate([upper, lower, upper], axis=1)
    return jnp.dot(packed, table, preferred_element_type=jnp.float32)


def table_times(table, value):
    upper, lower = halves(value)
    packed = jnp.concatenate([upper, lower, upper], axis=0)
    return jnp.dot(table, packed, preferred_element_type=jnp.float32)


def wide(left, right):
    return jnp.concatenate([left, right], axis=1)


def tall(upper, lower):
    return jnp.concatenate([upper, lower], axis=0)


def places(odd_col):
    return 3 - 3 * odd_col, 2 - odd_col, 1 + odd_col, 3 * odd_col


def gradient_body(
    first, info, positions, counts, ext_r, ext_i, ext_b, *refs
):
    if first:
        near_edge, near_corner, far_edge, far_corner, *refs = refs
    else:
        near_r, near_i, far_strip, *refs = refs
    measured, rolled, fore_lane, fore_row, back_row, back_lane, twist_lane, twist_row, *refs = refs
    out_r, out_i, out_b, in_a, in_b, field, sums = refs
    size = rolled.shape[2]
    half = size // 2
    extent = field.shape[2]
    odd_col = info[1]
    other = 1 - odd_col
    near_at, a_at, b_at, far_at = places(odd_col)
    lanes = lax.broadcasted_iota(jnp.int32, (1, half), 1)
    sums[...] = jnp.zeros_like(sums)
    field[a_at, 0] = ext_r[...]
    field[a_at, 1] = ext_i[...]
    field[b_at] = ext_b[...]
    if first:
        upper, middle, lower = slice(0, MARGIN), slice(MARGIN, extent - MARGIN), slice(extent - MARGIN, extent)
        field[near_at, :, middle] = near_edge[other]
        field[near_at, :, upper] = near_corner[other, 0]
        field[near_at, :, lower] = near_corner[other, 1]
        field[far_at, :, middle] = far_edge[...]
        field[far_at, :, upper] = far_corner[0]
        field[far_at, :, lower] = far_corner[1]
    else:
        field[near_at, 0] = near_r[other]
        field[near_at, 1] = near_i[other]
        field[far_at] = far_strip[...]
    lane_r, lane_i = twist_lane[0], twist_lane[1]
    row_r, row_i = twist_row[0], twist_row[1]

    def enter(slot):
        rows = pl.ds(positions[slot, 0], size)
        waves = []
        for block in range(2):
            near = lanes + half * block >= positions[slot, 1]
            cut = slice(half * block, half * (block + 1))
            p_r, p_i = rolled[slot, 0, :, cut], rolled[slot, 1, :, cut]
            o_r = jnp.where(near, field[block, 0, rows, :], field[block + 2, 0, rows, :])
            o_i = jnp.where(near, field[block, 1, rows, :], field[block + 2, 1, rows, :])
            waves.append((p_r * o_r - p_i * o_i, p_r * o_i + p_i * o_r))
        (r0, i0), (r1, i1) = waves
        d_r, d_i = r0 - r1, i0 - i1
        return [
            wide(r0 + r1, i0 + i1),
            wide(d_r * lane_r - d_i * lane_i, d_r * lane_i + d_i * lane_r),
        ]

    def cross(pair):
        even, odd = pair
        r_all = wide(even[:, :half], odd[:, :half])
        i_all = wide(even[:, half:], odd[:, half:])
        r0, r1 = r_all[:half], r_all[half:]
        i0, i1 = i_all[:half], i_all[half:]
        d_r, d_i = r0 - r1, i0 - i1
        return [
            tall(r0 + r1, i0 + i1),
            tall(d_r * row_r - d_i * row_i, d_r * row_i + d_i * row_r),
        ]

    def scale(slot, pair):
        scaled = []
        for parity, spectrum in enumerate(pair):
            s_r, s_i = spectrum[:half], spectrum[half:]
            misfit = s_r * s_r + s_i * s_i - measured[slot, parity]
            scaled.append(tall(misfit * s_r, misfit * s_i))
        return scaled

    def cross_back(pair):
        even, odd = pair
        e_r, e_i = even[:half], even[half:]
        o_r, o_i = odd[:half], odd[half:]
        t_r = o_r * row_r + o_i * row_i
        t_i = o_i * row_r - o_r * row_i
        full_r = tall(e_r + t_r, e_r - t_r)
        full_i = tall(e_i + t_i, e_i - t_i)
        return [
            wide(full_r[:, :half], full_i[:, :half]),
            wide(full_r[:, half:], full_i[:, half:]),
        ]

    def leave(slot, pair, keep):
        rows = pl.ds(positions[slot, 0], size)
        even, odd = pair
        e_r, e_i = even[:, :half], even[:, half:]
        o_r, o_i = odd[:, :half], odd[:, half:]
        t_r = o_r * lane_r + o_i * lane_i
        t_i = o_i * lane_r - o_r * lane_i
        outs = [(e_r + t_r, e_i + t_i), (e_r - t_r, e_i - t_i)]
        for block, (b_r, b_i) in enumerate(outs):
            place = lanes + half * block
            near = place >= positions[slot, 1]
            far = place < positions[slot, 1]
            if keep is not None:
                near, far = near & keep, far & keep
            cut = slice(half * block, half * (block + 1))
            p_r, p_i = rolled[slot, 0, :, cut], rolled[slot, 1, :, cut]
            terms = (p_r * b_r + p_i * b_i, p_r * b_i - p_i * b_r)
            for part, term in enumerate(terms):
                sums[block, part, rows, :] += jnp.where(near, term, 0.0)
                sums[block + 2, part, rows, :] += jnp.where(far, term, 0.0)

    def one_group(group, carry):
        slots = [GROUP * group + i for i in range(GROUP)]
        live = [None] + [slot < counts[0, 0] for slot in slots[1:]]
        pairs = [enter(slot) for slot in slots]
        pairs = [[times_table(half_, fore_lane[...]) for half_ in pair] for pair in pairs]
        pairs = [cross(pair) for pair in pairs]
        pairs = [[table_times(fore_row[...], half_) for half_ in pair] for pair in pairs]
        pairs = [scale(slot, pair) for slot, pair in zip(slots, pairs)]
        pairs = [[table_times(back_row[...], half_) for half_ in pair] for pair in pairs]
        pairs = [cross_back(pair) for pair in pairs]
        pairs = [[times_table(half_, back_lane[...]) for half_ in pair] for pair in pairs]
        for slot, pair, keep in zip(slots, pairs, live):
            leave(slot, pair, keep)
        return carry

    lax.fori_loop(0, (counts[0, 0] + GROUP - 1) // GROUP, one_group, 0)
    out_r[...] = sums[near_at, 0]
    out_i[...] = sums[near_at, 1]
    out_b[...] = sums[far_at]
    in_a[...] = sums[a_at]
    in_b[...] = sums[b_at]


def gradient(first, info, positions, counts, ext, sides, measured, rolled, tables):
    extent = ext[0].shape[0]
    plane, strip = shaped(extent, HALF), shaped(2, extent, HALF)
    return whole(
        functools.partial(gradient_body, first),
        (plane, plane, strip, strip, strip),
        (info, positions, counts),
        (*ext, *sides, measured, rolled, *tables),
        [pltpu.VMEM((4, 2, extent, HALF), jnp.float32)] * 2,
        flops=6 * 8 * 3 * 2**25,
    )


def extend_body(info, tile, halo_a, halo_b, ext_r, ext_i, ext_b, corner_a, corner_b):
    size = tile.shape[1]
    odd_row, odd_col = info[0], info[1]

    def fill(cut_a, cut_b):
        above = [jnp.where(odd_row == 1, halo_a[part], halo_b[part]) for part in range(2)]
        below = [jnp.where(odd_row == 1, halo_b[part], halo_a[part]) for part in range(2)]
        targets = [ext_r, ext_i]
        for part in range(2):
            corner_a[0, part] = above[part][:, cut_a]
            corner_a[1, part] = below[part][:, cut_a]
            corner_b[0, part] = above[part][:, cut_b]
            corner_b[1, part] = below[part][:, cut_b]
            targets[part][:MARGIN, :] = above[part][:, cut_a]
            targets[part][MARGIN : MARGIN + size, :] = tile[part, :, cut_a]
            targets[part][MARGIN + size :, :] = below[part][:, cut_a]
            ext_b[part, :MARGIN] = above[part][:, cut_b]
            ext_b[part, MARGIN : MARGIN + size] = tile[part, :, cut_b]
            ext_b[part, MARGIN + size :] = below[part][:, cut_b]

    left, right = slice(0, HALF), slice(HALF, 2 * HALF)

    @pl.when(odd_col == 1)
    def _():
        fill(left, right)

    @pl.when(odd_col == 0)
    def _():
        fill(right, left)


def outgoing(odd_row, total, width, out_a, out_b):
    extent = total.shape[1]
    out_a[...] = total[:, pl.ds(pl.multiple_of((1 - odd_row) * (extent - width), 8), width), :]
    out_b[...] = total[:, pl.ds(pl.multiple_of(odd_row * (extent - width), 8), width), :]


def join_near_body(width, info, inner, near_r, near_i, total, out_a, out_b):
    other = 1 - info[1]
    total[0] = inner[0] + near_r[other]
    total[1] = inner[1] + near_i[other]
    outgoing(info[0], total, width, out_a, out_b)


def join_far_body(width, info, inner, strip, total, out_a, out_b):
    total[...] = inner[...] + strip[...]
    outgoing(info[0], total, width, out_a, out_b)


def updated(info, part, ext, total, halo_a, halo_b):
    middle = total.shape[1] // 2
    above = total[part, :middle] + jnp.where(info[0] == 1, halo_a[part], halo_b[part])
    below = total[part, middle:] + jnp.where(info[0] == 1, halo_b[part], halo_a[part])
    row = lax.broadcasted_iota(jnp.int32, (middle, HALF), 0)
    above = jnp.where((info[2] == 1) & (row < MARGIN), 0.0, above)
    below = jnp.where((info[3] == 1) & (row >= middle - MARGIN), 0.0, below)
    return tall(ext[:middle] - step_rate * above, ext[middle:] - step_rate * below)


def update_near_body(info, ext_r, ext_i, total, halo_a, halo_b, out_r, out_i):
    out_r[...] = updated(info, 0, ext_r, total, halo_a, halo_b)
    out_i[...] = updated(info, 1, ext_i, total, halo_a, halo_b)


def update_far_body(info, ext_b, total, halo_a, halo_b, out):
    for part in range(2):
        out[part] = updated(info, part, ext_b.at[part], total, halo_a, halo_b)


def finish_body(info, ext_r, ext_i, ext_b, total_a, total_b, near_a, near_b, far_a, far_b, out):
    size = out.shape[1]
    half = size // 2
    upper, lower = slice(MARGIN, MARGIN + half), slice(MARGIN + half, MARGIN + size)

    def settle(cut, ext, total, halo_a, halo_b):
        for part in range(2):
            above = total[part, upper] + jnp.where(info[0] == 1, halo_a[part], halo_b[part])
            below = total[part, lower] + jnp.where(info[0] == 1, halo_b[part], halo_a[part])
            out[part, :half, cut] = ext[part][upper] - step_rate * above
            out[part, half:, cut] = ext[part][lower] - step_rate * below

    def place(cut_a, cut_b):
        settle(cut_a, [ext_r, ext_i], total_a, near_a, near_b)
        settle(cut_b, [ext_b.at[0], ext_b.at[1]], total_b, far_a, far_b)

    left, right = slice(0, HALF), slice(HALF, 2 * HALF)

    @pl.when(info[1] == 1)
    def _():
        place(left, right)

    @pl.when(info[1] == 0)
    def _():
        place(right, left)


def constants(size):
    half = size // 2
    mixed, twiddle = rotation_tables(size)
    upper = mixed.astype(jnp.bfloat16)
    lower = (mixed - upper.astype(np.float32)).astype(jnp.bfloat16)
    fore_lane = jnp.asarray(np.concatenate([upper, upper, lower], axis=0))
    back_row = jnp.asarray(np.concatenate([upper, upper, lower], axis=1))
    fore_row = jnp.asarray(np.concatenate([upper.T, upper.T, lower.T], axis=1))
    back_lane = jnp.asarray(np.concatenate([upper.T, upper.T, lower.T], axis=0))
    twist_lane = jnp.asarray(twiddle.reshape(2, 1, half))
    twist_row = jnp.asarray(np.ascontiguousarray(np.broadcast_to(twiddle[:, :, None], (2, half, size))))
    return fore_lane, fore_row, back_row, back_lane, twist_lane, twist_row


def swapped(value, axis, first):
    count = lax.axis_size(axis)
    route = []
    for i in range(first, count - 1, 2):
        route += [(i, i + 1), (i + 1, i)]
    return lax.ppermute(value, axis, route)


def paired(value):
    groups = [[i, i + 1] for i in range(0, lax.axis_size("cols"), 2)]
    return lax.all_gather(value, "cols", axis_index_groups=groups)


def both_rows(edge_a, edge_b):
    return swapped(edge_a, "rows", 0), swapped(edge_b, "rows", 1)


def summed(info, width, out_r, out_i, out_b, in_a, in_b):
    extent = in_a.shape[1]
    strip, piece = shaped(2, extent, HALF), shaped(2, width, HALF)
    far = swapped(out_b, "cols", 1)
    near = paired(out_r), paired(out_i)
    total_a, *edges = whole(functools.partial(join_near_body, width), (strip, piece, piece), (info,), (in_a, *near))
    halos_a = both_rows(*edges)
    total_b, *edges = whole(functools.partial(join_far_body, width), (strip, piece, piece), (info,), (in_b, far))
    halos_b = both_rows(*edges)
    return total_a, halos_a, total_b, halos_b


def on_device(object_field, probe, positions, counts, intensity):
    size = probe.shape[1]
    tile = object_field.shape[1]
    extent = tile + 2 * MARGIN
    row, col = lax.axis_index("rows"), lax.axis_index("cols")
    last = lax.axis_size("rows") - 1
    info = jnp.stack([row % 2, col % 2, row == 0, row == last]).astype(jnp.int32)
    tables = constants(size)
    order = jnp.asarray(split_order(size)).astype(jnp.bfloat16)
    positions, intensity = positions[0, 0], intensity[0, 0]
    plane, strip = shaped(extent, HALF), shaped(2, extent, HALF)
    corner = shaped(2, 2, MARGIN, HALF)

    edge = tile - MARGIN
    odd_row, odd_col = row % 2, col % 2
    halos = both_rows(
        lax.dynamic_slice_in_dim(object_field, (1 - odd_row) * edge, MARGIN, 1),
        lax.dynamic_slice_in_dim(object_field, odd_row * edge, MARGIN, 1),
    )
    far_edge = swapped(lax.dynamic_slice_in_dim(object_field, odd_col * edge, MARGIN, 2), "cols", 1)
    near_edge = paired(lax.dynamic_slice_in_dim(object_field, (1 - odd_col) * edge, MARGIN, 2))
    measured, rolled = prepare(positions, intensity, probe, order)
    *ext, corner_a, corner_b = whole(
        extend_body, (plane, plane, strip, corner, corner), (info,), (object_field, *halos)
    )
    far_corner = swapped(corner_b, "cols", 1)
    sides = near_edge, paired(corner_a), far_edge, far_corner
    parts = gradient(True, info, positions, counts, ext, sides, measured, rolled, tables)
    total_a, halos_a, total_b, halos_b = summed(info, extent // 2, *parts)
    near_ext = whole(update_near_body, (plane, plane), (info,), (*ext[:2], total_a, *halos_a))
    far_ext = whole(update_far_body, (strip,), (info,), (ext[2], total_b, *halos_b))
    ext = (*near_ext, *far_ext)
    sides = paired(ext[0]), paired(ext[1]), swapped(ext[2], "cols", 1)
    parts = gradient(False, info, positions, counts, ext, sides, measured, rolled, tables)
    total_a, halos_a, total_b, halos_b = summed(info, MARGIN, *parts)
    return whole(
        finish_body, (shaped(2, tile, tile),), (info,), (*ext, total_a, total_b, *halos_a, *halos_b)
    )[0]


def solution(mesh):
    placed = (
        P(None, "rows", "cols"),
        P(),
        P("rows", "cols", None, None),
        P("rows", "cols"),
        P("rows", "cols", None, None, None),
    )
    return jax.shard_map(
        on_device, mesh=mesh, in_specs=placed, out_specs=P(None, "rows", "cols"), check_vma=False
    )
```

```python
import functools

import jax
import jax.numpy as jnp
import numpy as np
from jax import lax
from jax.experimental import pallas as pl
from jax.experimental.pallas import tpu as pltpu
from jax.sharding import PartitionSpec as P

MARGIN = 128
HALF = 128
GROUP = 2


step_rate = 0.02
photon_unit = 0.001


def rotation_tables(length):
    half = length // 2
    index = np.arange(half, dtype=np.int64)
    angle = (index[:, None] * index[None, :] % half) * (2.0 * np.pi / half)
    norm = 1.0 / np.sqrt(length)
    cosine = np.cos(angle) * norm
    sine = np.sin(angle) * norm
    mixed = np.block([[cosine, -sine], [sine, cosine]]).astype(np.float32)
    turn = index * (2.0 * np.pi / length)
    twiddle = np.stack([np.cos(turn), -np.sin(turn)]).astype(np.float32)
    return mixed, twiddle


def split_order(length):
    half = length // 2
    order = np.concatenate([np.arange(half) * 2, np.arange(half) * 2 + 1])
    return (np.arange(length)[:, None] == order[None, :]).astype(np.float32)


VMEM = pl.BlockSpec(memory_space=pltpu.VMEM)
SMEM = pl.BlockSpec(memory_space=pltpu.SMEM)


def shaped(*dims):
    return jax.ShapeDtypeStruct(dims, jnp.float32)


def whole(body, outs, scalars, arrays, scratch=(), limit=40 << 20, flops=1 << 20):
    return pl.pallas_call(
        body,
        out_shape=outs,
        in_specs=[SMEM] * len(scalars) + [VMEM] * len(arrays),
        out_specs=tuple(VMEM for _ in outs),
        scratch_shapes=scratch,
        compiler_params=pltpu.CompilerParams(vmem_limit_bytes=limit),
        cost_estimate=pl.CostEstimate(flops=flops, bytes_accessed=8 << 20, transcendentals=0),
    )(*scalars, *arrays)


def split_columns(odd_col, tile, side_a, side_b):
    size = tile.shape[2]
    left, right = slice(0, MARGIN), slice(size - MARGIN, size)

    @pl.when(odd_col == 1)
    def _():
        side_a[...] = tile[:, :, left]
        side_b[...] = tile[:, :, right]

    @pl.when(odd_col == 0)
    def _():
        side_a[...] = tile[:, :, right]
        side_b[...] = tile[:, :, left]


def cut_rows_body(info, tile, edge_a, edge_b):
    edge = tile.shape[1] - MARGIN
    edge_a[...] = tile[:, pl.ds(pl.multiple_of((1 - info[0]) * edge, 8), MARGIN), :]
    edge_b[...] = tile[:, pl.ds(pl.multiple_of(info[0] * edge, 8), MARGIN), :]


def prepare_body(
    info, positions, intensity, probe, order, tile, measured, rolled, edge_a, edge_b, held, arrived
):
    slots, size = intensity.shape[0], probe.shape[1]
    half = size // 2
    moves = [order[:half], order[half:]]
    copies = [
        pltpu.make_async_copy(intensity.at[:, :, pl.ds(half * block, half)], held.at[block], arrived.at[block])
        for block in range(2)
    ]
    for copy in copies:
        copy.start()
    split_columns(info[1], tile, edge_a, edge_b)

    def turn(slot, carry):
        shift = lax.rem(positions[slot, 1], size)
        for part in range(2):
            rolled[slot, part] = pltpu.roll(probe[part], shift, 1)
        return carry

    lax.fori_loop(0, slots, turn, 0)
    for copy in copies:
        copy.wait()

    def reorder(slot, carry):
        for parity in range(2):
            moved = jnp.zeros((half, size), jnp.float32)
            for block in range(2):
                counts = held[block, slot, pl.ds(parity, half, stride=2), :]
                upper = lax.shift_right_logical(counts, 8).astype(jnp.float32).astype(jnp.bfloat16)
                lower = lax.bitwise_and(counts, 255).astype(jnp.float32).astype(jnp.bfloat16)
                high = jnp.dot(upper, moves[block], preferred_element_type=jnp.float32)
                low = jnp.dot(lower, moves[block], preferred_element_type=jnp.float32)
                moved = moved + (256.0 * high + low)
            measured[slot, parity] = moved * photon_unit
        return carry

    lax.fori_loop(0, slots, reorder, 0)


def prepare(info, positions, intensity, probe, order, tile):
    slots, size = intensity.shape[0], probe.shape[1]
    edge = shaped(2, tile.shape[1], MARGIN)
    half = size // 2
    return pl.pallas_call(
        prepare_body,
        out_shape=(shaped(slots, 2, half, size), shaped(slots, 2, size, size), edge, edge),
        in_specs=[SMEM, SMEM, pl.BlockSpec(memory_space=pl.ANY), VMEM, VMEM, VMEM],
        out_specs=(VMEM,) * 4,
        scratch_shapes=[pltpu.VMEM((2, slots, size, half), jnp.int32), pltpu.SemaphoreType.DMA((2,))],
        compiler_params=pltpu.CompilerParams(vmem_limit_bytes=24 << 20),
        cost_estimate=pl.CostEstimate(flops=slots * 2**27, bytes_accessed=8 << 20, transcendentals=0),
    )(info, positions, intensity, probe, order, tile)


def halves(value):
    upper = value.astype(jnp.bfloat16)
    lower = (value - upper.astype(jnp.float32)).astype(jnp.bfloat16)
    return upper, lower


def times_table(value, table):
    upper, lower = halves(value)
    packed = jnp.concatenate([upper, lower, upper], axis=1)
    return jnp.dot(packed, table, preferred_element_type=jnp.float32)


def table_times(table, value):
    upper, lower = halves(value)
    packed = jnp.concatenate([upper, lower, upper], axis=0)
    return jnp.dot(table, packed, preferred_element_type=jnp.float32)


def wide(left, right):
    return jnp.concatenate([left, right], axis=1)


def tall(upper, lower):
    return jnp.concatenate([upper, lower], axis=0)


def places(odd_col):
    return 3 - 3 * odd_col, 2 - odd_col, 1 + odd_col, 3 * odd_col


def gradient_body(first, info, positions, counts, ext_r, ext_i, ext_b, *refs):
    if first:
        near_edge, near_corner, far_edge, far_corner, *refs = refs
    else:
        near_r, near_i, far_strip, *refs = refs
    measured, rolled, fore_lane, fore_row, back_row, back_lane, twist_lane, twist_row, *refs = refs
    *outs, in_a, in_b, field, sums = refs
    size = rolled.shape[2]
    half = size // 2
    extent = field.shape[2]
    odd_col = info[1]
    other = 1 - odd_col
    near_at, a_at, b_at, far_at = places(odd_col)
    lanes = lax.broadcasted_iota(jnp.int32, (1, half), 1)
    sums[...] = jnp.zeros_like(sums)
    field[a_at, 0] = ext_r[...]
    field[a_at, 1] = ext_i[...]
    field[b_at] = ext_b[...]
    upper, middle, lower = slice(0, MARGIN), slice(MARGIN, extent - MARGIN), slice(extent - MARGIN, extent)
    if first:
        field[near_at, :, middle] = near_edge[other]
        field[near_at, :, upper] = near_corner[other, 0]
        field[near_at, :, lower] = near_corner[other, 1]
        field[far_at, :, middle] = far_edge[...]
        field[far_at, :, upper] = far_corner[0]
        field[far_at, :, lower] = far_corner[1]
    else:
        field[near_at, 0] = near_r[other]
        field[near_at, 1] = near_i[other]
        field[far_at] = far_strip[...]
    lane_r, lane_i = twist_lane[0], twist_lane[1]
    row_r, row_i = twist_row[0], twist_row[1]

    def enter(slot):
        rows = pl.ds(positions[slot, 0], size)
        waves = []
        for block in range(2):
            near = lanes + half * block >= positions[slot, 1]
            cut = slice(half * block, half * (block + 1))
            p_r, p_i = rolled[slot, 0, :, cut], rolled[slot, 1, :, cut]
            o_r = jnp.where(near, field[block, 0, rows, :], field[block + 2, 0, rows, :])
            o_i = jnp.where(near, field[block, 1, rows, :], field[block + 2, 1, rows, :])
            waves.append((p_r * o_r - p_i * o_i, p_r * o_i + p_i * o_r))
        (r0, i0), (r1, i1) = waves
        d_r, d_i = r0 - r1, i0 - i1
        return [
            wide(r0 + r1, i0 + i1),
            wide(d_r * lane_r - d_i * lane_i, d_r * lane_i + d_i * lane_r),
        ]

    def cross(pair):
        even, odd = pair
        r_all = wide(even[:, :half], odd[:, :half])
        i_all = wide(even[:, half:], odd[:, half:])
        r0, r1 = r_all[:half], r_all[half:]
        i0, i1 = i_all[:half], i_all[half:]
        d_r, d_i = r0 - r1, i0 - i1
        return [
            tall(r0 + r1, i0 + i1),
            tall(d_r * row_r - d_i * row_i, d_r * row_i + d_i * row_r),
        ]

    def scale(slot, pair):
        scaled = []
        for parity, spectrum in enumerate(pair):
            s_r, s_i = spectrum[:half], spectrum[half:]
            misfit = s_r * s_r + s_i * s_i - measured[slot, parity]
            scaled.append(tall(misfit * s_r, misfit * s_i))
        return scaled

    def cross_back(pair):
        even, odd = pair
        e_r, e_i = even[:half], even[half:]
        o_r, o_i = odd[:half], odd[half:]
        t_r = o_r * row_r + o_i * row_i
        t_i = o_i * row_r - o_r * row_i
        full_r = tall(e_r + t_r, e_r - t_r)
        full_i = tall(e_i + t_i, e_i - t_i)
        return [
            wide(full_r[:, :half], full_i[:, :half]),
            wide(full_r[:, half:], full_i[:, half:]),
        ]

    def leave(slot, pair, keep):
        rows = pl.ds(positions[slot, 0], size)
        even, odd = pair
        e_r, e_i = even[:, :half], even[:, half:]
        o_r, o_i = odd[:, :half], odd[:, half:]
        t_r = o_r * lane_r + o_i * lane_i
        t_i = o_i * lane_r - o_r * lane_i
        outs = [(e_r + t_r, e_i + t_i), (e_r - t_r, e_i - t_i)]
        for block, (b_r, b_i) in enumerate(outs):
            place = lanes + half * block
            near = place >= positions[slot, 1]
            far = place < positions[slot, 1]
            if keep is not None:
                near, far = near & keep, far & keep
            cut = slice(half * block, half * (block + 1))
            p_r, p_i = rolled[slot, 0, :, cut], rolled[slot, 1, :, cut]
            terms = (p_r * b_r + p_i * b_i, p_r * b_i - p_i * b_r)
            for part, term in enumerate(terms):
                sums[block, part, rows, :] += jnp.where(near, term, 0.0)
                sums[block + 2, part, rows, :] += jnp.where(far, term, 0.0)

    def one_group(group, carry):
        slots = [GROUP * group + i for i in range(GROUP)]
        live = [None] + [slot < counts[0, 0] for slot in slots[1:]]
        pairs = [enter(slot) for slot in slots]
        pairs = [[times_table(half_, fore_lane[...]) for half_ in pair] for pair in pairs]
        pairs = [cross(pair) for pair in pairs]
        pairs = [[table_times(fore_row[...], half_) for half_ in pair] for pair in pairs]
        pairs = [scale(slot, pair) for slot, pair in zip(slots, pairs)]
        pairs = [[table_times(back_row[...], half_) for half_ in pair] for pair in pairs]
        pairs = [cross_back(pair) for pair in pairs]
        pairs = [[times_table(half_, back_lane[...]) for half_ in pair] for pair in pairs]
        for slot, pair, keep in zip(slots, pairs, live):
            leave(slot, pair, keep)
        return carry

    lax.fori_loop(0, (counts[0, 0] + GROUP - 1) // GROUP, one_group, 0)
    if first:
        out_r, out_i, out_b = outs
        out_r[...] = sums[near_at, 0]
        out_i[...] = sums[near_at, 1]
        out_b[...] = sums[far_at]
    else:
        for at, corner, edge in ((near_at, *outs[:2]), (far_at, *outs[2:])):
            corner[0] = sums[at, :, upper]
            corner[1] = sums[at, :, lower]
            edge[...] = sums[at, :, middle]
    in_a[...] = sums[a_at]
    in_b[...] = sums[b_at]


def gradient(first, info, positions, counts, ext, sides, measured, rolled, tables):
    extent = ext[0].shape[0]
    plane, strip = shaped(extent, HALF), shaped(2, extent, HALF)
    corner, edge = shaped(2, 2, MARGIN, HALF), shaped(2, extent - 2 * MARGIN, HALF)
    outs = (plane, plane, strip) if first else (corner, edge, corner, edge)
    return whole(
        functools.partial(gradient_body, first),
        (*outs, strip, strip),
        (info, positions, counts),
        (*ext, *sides, measured, rolled, *tables),
        [pltpu.VMEM((4, 2, extent, HALF), jnp.float32)] * 2,
        flops=6 * 8 * 3 * 2**25,
    )


def extend_body(info, tile, halo_a, halo_b, ext_r, ext_i, ext_b, corner_a, corner_b):
    size = tile.shape[1]
    odd_row, odd_col = info[0], info[1]

    def fill(cut_a, cut_b):
        above = [jnp.where(odd_row == 1, halo_a[part], halo_b[part]) for part in range(2)]
        below = [jnp.where(odd_row == 1, halo_b[part], halo_a[part]) for part in range(2)]
        targets = [ext_r, ext_i]
        for part in range(2):
            corner_a[0, part] = above[part][:, cut_a]
            corner_a[1, part] = below[part][:, cut_a]
            corner_b[0, part] = above[part][:, cut_b]
            corner_b[1, part] = below[part][:, cut_b]
            targets[part][:MARGIN, :] = above[part][:, cut_a]
            targets[part][MARGIN : MARGIN + size, :] = tile[part, :, cut_a]
            targets[part][MARGIN + size :, :] = below[part][:, cut_a]
            ext_b[part, :MARGIN] = above[part][:, cut_b]
            ext_b[part, MARGIN : MARGIN + size] = tile[part, :, cut_b]
            ext_b[part, MARGIN + size :] = below[part][:, cut_b]

    left, right = slice(0, HALF), slice(HALF, 2 * HALF)

    @pl.when(odd_col == 1)
    def _():
        fill(left, right)

    @pl.when(odd_col == 0)
    def _():
        fill(right, left)


def outgoing(odd_row, total, width, out_a, out_b):
    extent = total.shape[1]
    out_a[...] = total[:, pl.ds(pl.multiple_of((1 - odd_row) * (extent - width), 8), width), :]
    out_b[...] = total[:, pl.ds(pl.multiple_of(odd_row * (extent - width), 8), width), :]


def join_near_body(info, inner, near_r, near_i, total, out_a, out_b):
    other = 1 - info[1]
    total[0] = inner[0] + near_r[other]
    total[1] = inner[1] + near_i[other]
    outgoing(info[0], total, total.shape[1] // 2, out_a, out_b)


def join_far_body(info, inner, strip, waiting, total, out_a, out_b, passed):
    total[...] = inner[...] + strip[...]
    outgoing(info[0], total, total.shape[1] // 2, out_a, out_b)
    passed[...] = waiting[...]


def corner_near_body(info, inner, corner, out_a, out_b):
    add_corner(info, inner, corner.at[1 - info[1]], out_a, out_b)


def corner_far_body(info, inner, corner, earlier, waiting, out_a, out_b, passed):
    add_corner(info, inner, corner, out_a, out_b)
    passed[...] = waiting[...]


def add_corner(info, inner, corner, out_a, out_b):
    last = inner.shape[1] - MARGIN
    lower, upper = 1 - info[0], info[0]
    out_a[...] = inner[:, pl.ds(pl.multiple_of(lower * last, 8), MARGIN), :] + corner[lower]
    out_b[...] = inner[:, pl.ds(pl.multiple_of(upper * last, 8), MARGIN), :] + corner[upper]


def updated(info, part, ext, total, halo_a, halo_b):
    middle = total.shape[1] // 2
    above = total[part, :middle] + jnp.where(info[0] == 1, halo_a[part], halo_b[part])
    below = total[part, middle:] + jnp.where(info[0] == 1, halo_b[part], halo_a[part])
    row = lax.broadcasted_iota(jnp.int32, (middle, HALF), 0)
    above = jnp.where((info[2] == 1) & (row < MARGIN), 0.0, above)
    below = jnp.where((info[3] == 1) & (row >= middle - MARGIN), 0.0, below)
    return tall(ext[:middle] - step_rate * above, ext[middle:] - step_rate * below)


def update_near_body(info, ext_r, ext_i, total, halo_a, halo_b, out_r, out_i):
    out_r[...] = updated(info, 0, ext_r, total, halo_a, halo_b)
    out_i[...] = updated(info, 1, ext_i, total, halo_a, halo_b)


def update_far_body(info, ext_b, total, halo_a, halo_b, out):
    for part in range(2):
        out[part] = updated(info, part, ext_b.at[part], total, halo_a, halo_b)


def finish_body(
    info, ext_r, ext_i, ext_b, inner_a, inner_b, edge_a, edge_b, near_a, near_b, far_a, far_b, out
):
    size = out.shape[1]
    half = size // 2
    upper, lower = slice(MARGIN, MARGIN + half), slice(MARGIN + half, MARGIN + size)

    def settle(cut, ext, inner, edge, halo_a, halo_b):
        for part in range(2):
            above = jnp.where(info[0] == 1, halo_a[part], halo_b[part])
            below = jnp.where(info[0] == 1, halo_b[part], halo_a[part])
            above = inner[part, upper] + edge[part, :half] + above
            below = inner[part, lower] + edge[part, half:] + below
            out[part, :half, cut] = ext[part][upper] - step_rate * above
            out[part, half:, cut] = ext[part][lower] - step_rate * below

    def place(cut_a, cut_b):
        settle(cut_a, [ext_r, ext_i], inner_a, edge_a.at[1 - info[1]], near_a, near_b)
        settle(cut_b, [ext_b.at[0], ext_b.at[1]], inner_b, edge_b, far_a, far_b)

    left, right = slice(0, HALF), slice(HALF, 2 * HALF)

    @pl.when(info[1] == 1)
    def _():
        place(left, right)

    @pl.when(info[1] == 0)
    def _():
        place(right, left)


def constants(size):
    half = size // 2
    mixed, twiddle = rotation_tables(size)
    upper = mixed.astype(jnp.bfloat16)
    lower = (mixed - upper.astype(np.float32)).astype(jnp.bfloat16)
    fore_lane = jnp.asarray(np.concatenate([upper, upper, lower], axis=0))
    back_row = jnp.asarray(np.concatenate([upper, upper, lower], axis=1))
    fore_row = jnp.asarray(np.concatenate([upper.T, upper.T, lower.T], axis=1))
    back_lane = jnp.asarray(np.concatenate([upper.T, upper.T, lower.T], axis=0))
    twist_lane = jnp.asarray(twiddle.reshape(2, 1, half))
    twist_row = jnp.asarray(np.ascontiguousarray(np.broadcast_to(twiddle[:, :, None], (2, half, size))))
    return fore_lane, fore_row, back_row, back_lane, twist_lane, twist_row


def swapped(value, axis, first):
    count = lax.axis_size(axis)
    route = []
    for i in range(first, count - 1, 2):
        route += [(i, i + 1), (i + 1, i)]
    return lax.ppermute(value, axis, route)


def paired(value):
    groups = [[i, i + 1] for i in range(0, lax.axis_size("cols"), 2)]
    return lax.all_gather(value, "cols", axis_index_groups=groups)


def both_rows(edge_a, edge_b):
    return swapped(edge_a, "rows", 0), swapped(edge_b, "rows", 1)


def on_device(object_field, probe, positions, counts, intensity):
    size = probe.shape[1]
    tile = object_field.shape[1]
    extent = tile + 2 * MARGIN
    row, col = lax.axis_index("rows"), lax.axis_index("cols")
    last = lax.axis_size("rows") - 1
    info = jnp.stack([row % 2, col % 2, row == 0, row == last]).astype(jnp.int32)
    tables = constants(size)
    order = jnp.asarray(split_order(size)).astype(jnp.bfloat16)
    positions, intensity = positions[0, 0], intensity[0, 0]
    plane, strip = shaped(extent, HALF), shaped(2, extent, HALF)
    corner = shaped(2, 2, MARGIN, HALF)

    edge = shaped(2, MARGIN, tile)
    halos = both_rows(*whole(cut_rows_body, (edge, edge), (info,), (object_field,)))
    measured, rolled, edge_a, edge_b = prepare(info, positions, intensity, probe, order, object_field)
    far_edge, near_edge = swapped(edge_b, "cols", 1), paired(edge_a)
    *ext, corner_a, corner_b = whole(
        extend_body, (plane, plane, strip, corner, corner), (info,), (object_field, *halos)
    )
    far_corner = swapped(corner_b, "cols", 1)
    sides = near_edge, paired(corner_a), far_edge, far_corner
    out_r, out_i, out_b, in_a, in_b = gradient(
        True, info, positions, counts, ext, sides, measured, rolled, tables
    )

    far = swapped(out_b, "cols", 1)
    near = paired(out_r), paired(out_i)
    piece = shaped(2, extent // 2, HALF)
    total_a, edge_a, edge_b = whole(join_near_body, (strip, piece, piece), (info,), (in_a, *near))
    near_halo_a = swapped(edge_a, "rows", 0)
    total_b, far_a, far_b, edge_b = whole(
        join_far_body, (strip, piece, piece, piece), (info,), (in_b, far, edge_b)
    )
    far_halos = both_rows(far_a, far_b)
    near_halos = near_halo_a, swapped(edge_b, "rows", 1)
    far_ext = whole(update_far_body, (strip,), (info,), (ext[2], total_b, *far_halos))
    near_ext = whole(update_near_body, (plane, plane), (info,), (*ext[:2], total_a, *near_halos))
    ext = (*near_ext, *far_ext)
    sides = paired(ext[0]), paired(ext[1]), swapped(ext[2], "cols", 1)
    corner_a, edge_a, corner_b, edge_b, in_a, in_b = gradient(
        False, info, positions, counts, ext, sides, measured, rolled, tables
    )

    piece = shaped(2, MARGIN, HALF)
    far_corner = swapped(corner_b, "cols", 1)
    near_corner = paired(corner_a)
    rows_a, rows_b = whole(corner_near_body, (piece, piece), (info,), (in_a, near_corner))
    near_halos = both_rows(rows_a, rows_b)
    edge = shaped(2, tile, HALF)
    far_a, far_b, edge_b = whole(
        corner_far_body, (piece, piece, edge), (info,), (in_b, far_corner, rows_b, edge_b)
    )
    far_halos = both_rows(far_a, far_b)
    sides = paired(edge_a), swapped(edge_b, "cols", 1)
    return whole(
        finish_body, (shaped(2, tile, tile),), (info,), (*ext, in_a, in_b, *sides, *near_halos, *far_halos)
    )[0]


def solution(mesh):
    placed = (
        P(None, "rows", "cols"),
        P(),
        P("rows", "cols", None, None),
        P("rows", "cols"),
        P("rows", "cols", None, None, None),
    )
    return jax.shard_map(
        on_device, mesh=mesh, in_specs=placed, out_specs=P(None, "rows", "cols"), check_vma=False
    )
```

```python
import functools

import jax
import jax.numpy as jnp
import numpy as np
from jax import lax
from jax.experimental import pallas as pl
from jax.experimental.pallas import tpu as pltpu
from jax.sharding import PartitionSpec as P

MARGIN = 128
HALF = 128
GROUP = 2


step_rate = 0.02
photon_unit = 0.001


def rotation_tables(length):
    half = length // 2
    index = np.arange(half, dtype=np.int64)
    angle = (index[:, None] * index[None, :] % half) * (2.0 * np.pi / half)
    norm = 1.0 / np.sqrt(length)
    cosine = np.cos(angle) * norm
    sine = np.sin(angle) * norm
    mixed = np.block([[cosine, -sine], [sine, cosine]]).astype(np.float32)
    turn = index * (2.0 * np.pi / length)
    twiddle = np.stack([np.cos(turn), -np.sin(turn)]).astype(np.float32)
    return mixed, twiddle


def split_order(length):
    half = length // 2
    order = np.concatenate([np.arange(half) * 2, np.arange(half) * 2 + 1])
    return (np.arange(length)[:, None] == order[None, :]).astype(np.float32)


VMEM = pl.BlockSpec(memory_space=pltpu.VMEM)
SMEM = pl.BlockSpec(memory_space=pltpu.SMEM)


def shaped(*dims):
    return jax.ShapeDtypeStruct(dims, jnp.float32)


def whole(body, outs, scalars, arrays, scratch=(), limit=40 << 20, flops=1 << 20):
    return pl.pallas_call(
        body,
        out_shape=outs,
        in_specs=[SMEM] * len(scalars) + [VMEM] * len(arrays),
        out_specs=tuple(VMEM for _ in outs),
        scratch_shapes=scratch,
        compiler_params=pltpu.CompilerParams(vmem_limit_bytes=limit),
        cost_estimate=pl.CostEstimate(flops=flops, bytes_accessed=8 << 20, transcendentals=0),
    )(*scalars, *arrays)


def split_columns(odd_col, tile, side_a, side_b):
    size = tile.shape[2]
    left, right = slice(0, MARGIN), slice(size - MARGIN, size)

    @pl.when(odd_col == 1)
    def _():
        side_a[...] = tile[:, :, left]
        side_b[...] = tile[:, :, right]

    @pl.when(odd_col == 0)
    def _():
        side_a[...] = tile[:, :, right]
        side_b[...] = tile[:, :, left]


def cut_body(info, tile, edge_a, edge_b, side_a, side_b):
    edge = tile.shape[1] - MARGIN
    edge_a[...] = tile[:, pl.ds(pl.multiple_of((1 - info[0]) * edge, 8), MARGIN), :]
    edge_b[...] = tile[:, pl.ds(pl.multiple_of(info[0] * edge, 8), MARGIN), :]
    split_columns(info[1], tile, side_a, side_b)


def prepare_body(positions, intensity, probe, order, measured, rolled, held, arrived):
    slots, size = intensity.shape[0], probe.shape[1]
    half = size // 2
    moves = [order[:half], order[half:]]
    copies = [
        pltpu.make_async_copy(intensity.at[:, :, pl.ds(half * block, half)], held.at[block], arrived.at[block])
        for block in range(2)
    ]
    for copy in copies:
        copy.start()

    def turn(slot, carry):
        shift = lax.rem(positions[slot, 1], size)
        for part in range(2):
            rolled[slot, part] = pltpu.roll(probe[part], shift, 1)
        return carry

    lax.fori_loop(0, slots, turn, 0)
    for copy in copies:
        copy.wait()

    def reorder(slot, carry):
        for parity in range(2):
            moved = jnp.zeros((half, size), jnp.float32)
            for block in range(2):
                counts = held[block, slot, pl.ds(parity, half, stride=2), :]
                upper = lax.shift_right_logical(counts, 8).astype(jnp.float32).astype(jnp.bfloat16)
                lower = lax.bitwise_and(counts, 255).astype(jnp.float32).astype(jnp.bfloat16)
                high = jnp.dot(upper, moves[block], preferred_element_type=jnp.float32)
                low = jnp.dot(lower, moves[block], preferred_element_type=jnp.float32)
                moved = moved + (256.0 * high + low)
            measured[slot, parity] = moved * photon_unit
        return carry

    lax.fori_loop(0, slots, reorder, 0)


def prepare(positions, intensity, probe, order):
    slots, size = intensity.shape[0], probe.shape[1]
    half = size // 2
    return pl.pallas_call(
        prepare_body,
        out_shape=(shaped(slots, 2, half, size), shaped(slots, 2, size, size)),
        in_specs=[SMEM, pl.BlockSpec(memory_space=pl.ANY), VMEM, VMEM],
        out_specs=(VMEM, VMEM),
        scratch_shapes=[pltpu.VMEM((2, slots, size, half), jnp.int32), pltpu.SemaphoreType.DMA((2,))],
        compiler_params=pltpu.CompilerParams(vmem_limit_bytes=24 << 20),
        cost_estimate=pl.CostEstimate(flops=slots * 2**27, bytes_accessed=8 << 20, transcendentals=0),
    )(positions, intensity, probe, order)


def halves(value):
    upper = value.astype(jnp.bfloat16)
    lower = (value - upper.astype(jnp.float32)).astype(jnp.bfloat16)
    return upper, lower


def times_table(value, table):
    upper, lower = halves(value)
    packed = jnp.concatenate([upper, lower, upper], axis=1)
    return jnp.dot(packed, table, preferred_element_type=jnp.float32)


def table_times(table, value):
    upper, lower = halves(value)
    packed = jnp.concatenate([upper, lower, upper], axis=0)
    return jnp.dot(table, packed, preferred_element_type=jnp.float32)


def wide(left, right):
    return jnp.concatenate([left, right], axis=1)


def tall(upper, lower):
    return jnp.concatenate([upper, lower], axis=0)


def places(odd_col):
    return 3 - 3 * odd_col, 2 - odd_col, 1 + odd_col, 3 * odd_col


def gradient_body(first, info, positions, counts, ext_r, ext_i, ext_b, *refs):
    if first:
        near_edge, near_corner, far_edge, far_corner, *refs = refs
    else:
        near_r, near_i, far_strip, *refs = refs
    measured, rolled, fore_lane, fore_row, back_row, back_lane, twist_lane, twist_row, *refs = refs
    *outs, in_a, in_b, field, sums = refs
    size = rolled.shape[2]
    half = size // 2
    extent = field.shape[2]
    odd_col = info[1]
    other = 1 - odd_col
    near_at, a_at, b_at, far_at = places(odd_col)
    lanes = lax.broadcasted_iota(jnp.int32, (1, half), 1)
    sums[...] = jnp.zeros_like(sums)
    field[a_at, 0] = ext_r[...]
    field[a_at, 1] = ext_i[...]
    field[b_at] = ext_b[...]
    upper, middle, lower = slice(0, MARGIN), slice(MARGIN, extent - MARGIN), slice(extent - MARGIN, extent)
    if first:
        field[near_at, :, middle] = near_edge[other]
        field[near_at, :, upper] = near_corner[other, 0]
        field[near_at, :, lower] = near_corner[other, 1]
        field[far_at, :, middle] = far_edge[...]
        field[far_at, :, upper] = far_corner[0]
        field[far_at, :, lower] = far_corner[1]
    else:
        field[near_at, 0] = near_r[other]
        field[near_at, 1] = near_i[other]
        field[far_at] = far_strip[...]
    lane_r, lane_i = twist_lane[0], twist_lane[1]
    row_r, row_i = twist_row[0], twist_row[1]

    def enter(slot):
        rows = pl.ds(positions[slot, 0], size)
        waves = []
        for block in range(2):
            near = lanes + half * block >= positions[slot, 1]
            cut = slice(half * block, half * (block + 1))
            p_r, p_i = rolled[slot, 0, :, cut], rolled[slot, 1, :, cut]
            o_r = jnp.where(near, field[block, 0, rows, :], field[block + 2, 0, rows, :])
            o_i = jnp.where(near, field[block, 1, rows, :], field[block + 2, 1, rows, :])
            waves.append((p_r * o_r - p_i * o_i, p_r * o_i + p_i * o_r))
        (r0, i0), (r1, i1) = waves
        d_r, d_i = r0 - r1, i0 - i1
        return [
            wide(r0 + r1, i0 + i1),
            wide(d_r * lane_r - d_i * lane_i, d_r * lane_i + d_i * lane_r),
        ]

    def cross(pair):
        even, odd = pair
        r_all = wide(even[:, :half], odd[:, :half])
        i_all = wide(even[:, half:], odd[:, half:])
        r0, r1 = r_all[:half], r_all[half:]
        i0, i1 = i_all[:half], i_all[half:]
        d_r, d_i = r0 - r1, i0 - i1
        return [
            tall(r0 + r1, i0 + i1),
            tall(d_r * row_r - d_i * row_i, d_r * row_i + d_i * row_r),
        ]

    def scale(slot, pair):
        scaled = []
        for parity, spectrum in enumerate(pair):
            s_r, s_i = spectrum[:half], spectrum[half:]
            misfit = s_r * s_r + s_i * s_i - measured[slot, parity]
            scaled.append(tall(misfit * s_r, misfit * s_i))
        return scaled

    def cross_back(pair):
        even, odd = pair
        e_r, e_i = even[:half], even[half:]
        o_r, o_i = odd[:half], odd[half:]
        t_r = o_r * row_r + o_i * row_i
        t_i = o_i * row_r - o_r * row_i
        full_r = tall(e_r + t_r, e_r - t_r)
        full_i = tall(e_i + t_i, e_i - t_i)
        return [
            wide(full_r[:, :half], full_i[:, :half]),
            wide(full_r[:, half:], full_i[:, half:]),
        ]

    def leave(slot, pair, keep):
        rows = pl.ds(positions[slot, 0], size)
        even, odd = pair
        e_r, e_i = even[:, :half], even[:, half:]
        o_r, o_i = odd[:, :half], odd[:, half:]
        t_r = o_r * lane_r + o_i * lane_i
        t_i = o_i * lane_r - o_r * lane_i
        outs = [(e_r + t_r, e_i + t_i), (e_r - t_r, e_i - t_i)]
        for block, (b_r, b_i) in enumerate(outs):
            place = lanes + half * block
            near = place >= positions[slot, 1]
            far = place < positions[slot, 1]
            if keep is not None:
                near, far = near & keep, far & keep
            cut = slice(half * block, half * (block + 1))
            p_r, p_i = rolled[slot, 0, :, cut], rolled[slot, 1, :, cut]
            terms = (p_r * b_r + p_i * b_i, p_r * b_i - p_i * b_r)
            for part, term in enumerate(terms):
                sums[block, part, rows, :] += jnp.where(near, term, 0.0)
                sums[block + 2, part, rows, :] += jnp.where(far, term, 0.0)

    def one_group(group, carry):
        slots = [GROUP * group + i for i in range(GROUP)]
        live = [None] + [slot < counts[0, 0] for slot in slots[1:]]
        pairs = [enter(slot) for slot in slots]
        pairs = [[times_table(half_, fore_lane[...]) for half_ in pair] for pair in pairs]
        pairs = [cross(pair) for pair in pairs]
        pairs = [[table_times(fore_row[...], half_) for half_ in pair] for pair in pairs]
        pairs = [scale(slot, pair) for slot, pair in zip(slots, pairs)]
        pairs = [[table_times(back_row[...], half_) for half_ in pair] for pair in pairs]
        pairs = [cross_back(pair) for pair in pairs]
        pairs = [[times_table(half_, back_lane[...]) for half_ in pair] for pair in pairs]
        for slot, pair, keep in zip(slots, pairs, live):
            leave(slot, pair, keep)
        return carry

    lax.fori_loop(0, (counts[0, 0] + GROUP - 1) // GROUP, one_group, 0)
    if first:
        out_r, out_i, out_b = outs
        out_r[...] = sums[near_at, 0]
        out_i[...] = sums[near_at, 1]
        out_b[...] = sums[far_at]
    else:
        for at, corner, edge in ((near_at, *outs[:2]), (far_at, *outs[2:])):
            corner[0] = sums[at, :, upper]
            corner[1] = sums[at, :, lower]
            edge[...] = sums[at, :, middle]
    in_a[...] = sums[a_at]
    in_b[...] = sums[b_at]


def gradient(first, info, positions, counts, ext, sides, measured, rolled, tables):
    extent = ext[0].shape[0]
    plane, strip = shaped(extent, HALF), shaped(2, extent, HALF)
    corner, edge = shaped(2, 2, MARGIN, HALF), shaped(2, extent - 2 * MARGIN, HALF)
    outs = (plane, plane, strip) if first else (corner, edge, corner, edge)
    return whole(
        functools.partial(gradient_body, first),
        (*outs, strip, strip),
        (info, positions, counts),
        (*ext, *sides, measured, rolled, *tables),
        [pltpu.VMEM((4, 2, extent, HALF), jnp.float32)] * 2,
        flops=6 * 8 * 3 * 2**25,
    )


def extend_body(info, tile, halo_a, halo_b, ext_r, ext_i, ext_b, corner_a, corner_b):
    size = tile.shape[1]
    odd_row, odd_col = info[0], info[1]

    def fill(cut_a, cut_b):
        above = [jnp.where(odd_row == 1, halo_a[part], halo_b[part]) for part in range(2)]
        below = [jnp.where(odd_row == 1, halo_b[part], halo_a[part]) for part in range(2)]
        targets = [ext_r, ext_i]
        for part in range(2):
            corner_a[0, part] = above[part][:, cut_a]
            corner_a[1, part] = below[part][:, cut_a]
            corner_b[0, part] = above[part][:, cut_b]
            corner_b[1, part] = below[part][:, cut_b]
            targets[part][:MARGIN, :] = above[part][:, cut_a]
            targets[part][MARGIN : MARGIN + size, :] = tile[part, :, cut_a]
            targets[part][MARGIN + size :, :] = below[part][:, cut_a]
            ext_b[part, :MARGIN] = above[part][:, cut_b]
            ext_b[part, MARGIN : MARGIN + size] = tile[part, :, cut_b]
            ext_b[part, MARGIN + size :] = below[part][:, cut_b]

    left, right = slice(0, HALF), slice(HALF, 2 * HALF)

    @pl.when(odd_col == 1)
    def _():
        fill(left, right)

    @pl.when(odd_col == 0)
    def _():
        fill(right, left)


def join_body(info, inner_a, inner_b, near_r, near_i, far, total, out_a, out_b):
    other = 1 - info[1]
    total[0, 0] = inner_a[0] + near_r[other]
    total[0, 1] = inner_a[1] + near_i[other]
    total[1] = inner_b[...] + far[...]
    middle = total.shape[2] // 2
    out_a[...] = total[:, :, pl.ds(pl.multiple_of((1 - info[0]) * middle, 8), middle), :]
    out_b[...] = total[:, :, pl.ds(pl.multiple_of(info[0] * middle, 8), middle), :]


def corner_body(info, inner_a, inner_b, near, far, edge, out_a, out_b, passed):
    last = inner_a.shape[1] - MARGIN
    for out, side in ((out_a, 1 - info[0]), (out_b, info[0])):
        rows = pl.ds(pl.multiple_of(side * last, 8), MARGIN)
        out[0] = inner_a[:, rows, :] + near[1 - info[1], side]
        out[1] = inner_b[:, rows, :] + far[side]
    passed[...] = edge[...]


def updated(info, part, ext, total, halo_a, halo_b):
    middle = total.shape[1] // 2
    above = total[part, :middle] + jnp.where(info[0] == 1, halo_a[part], halo_b[part])
    below = total[part, middle:] + jnp.where(info[0] == 1, halo_b[part], halo_a[part])
    row = lax.broadcasted_iota(jnp.int32, (middle, HALF), 0)
    above = jnp.where((info[2] == 1) & (row < MARGIN), 0.0, above)
    below = jnp.where((info[3] == 1) & (row >= middle - MARGIN), 0.0, below)
    return tall(ext[:middle] - step_rate * above, ext[middle:] - step_rate * below)


def update_body(info, ext_r, ext_i, ext_b, total, halo_a, halo_b, out_r, out_i, out_b):
    out_r[...] = updated(info, 0, ext_r, total.at[0], halo_a.at[0], halo_b.at[0])
    out_i[...] = updated(info, 1, ext_i, total.at[0], halo_a.at[0], halo_b.at[0])
    for part in range(2):
        out_b[part] = updated(info, part, ext_b.at[part], total.at[1], halo_a.at[1], halo_b.at[1])


def finish_body(
    info, ext_r, ext_i, ext_b, inner_a, inner_b, edge_a, edge_b, halo_a, halo_b, out
):
    size = out.shape[1]
    half = size // 2
    upper, lower = slice(MARGIN, MARGIN + half), slice(MARGIN + half, MARGIN + size)

    def settle(cut, ext, inner, edge, halo_a, halo_b):
        for part in range(2):
            above = jnp.where(info[0] == 1, halo_a[part], halo_b[part])
            below = jnp.where(info[0] == 1, halo_b[part], halo_a[part])
            above = inner[part, upper] + edge[part, :half] + above
            below = inner[part, lower] + edge[part, half:] + below
            out[part, :half, cut] = ext[part][upper] - step_rate * above
            out[part, half:, cut] = ext[part][lower] - step_rate * below

    def place(cut_a, cut_b):
        settle(cut_a, [ext_r, ext_i], inner_a, edge_a.at[1 - info[1]], halo_a.at[0], halo_b.at[0])
        settle(cut_b, [ext_b.at[0], ext_b.at[1]], inner_b, edge_b, halo_a.at[1], halo_b.at[1])

    left, right = slice(0, HALF), slice(HALF, 2 * HALF)

    @pl.when(info[1] == 1)
    def _():
        place(left, right)

    @pl.when(info[1] == 0)
    def _():
        place(right, left)


def constants(size):
    half = size // 2
    mixed, twiddle = rotation_tables(size)
    upper = mixed.astype(jnp.bfloat16)
    lower = (mixed - upper.astype(np.float32)).astype(jnp.bfloat16)
    fore_lane = jnp.asarray(np.concatenate([upper, upper, lower], axis=0))
    back_row = jnp.asarray(np.concatenate([upper, upper, lower], axis=1))
    fore_row = jnp.asarray(np.concatenate([upper.T, upper.T, lower.T], axis=1))
    back_lane = jnp.asarray(np.concatenate([upper.T, upper.T, lower.T], axis=0))
    twist_lane = jnp.asarray(twiddle.reshape(2, 1, half))
    twist_row = jnp.asarray(np.ascontiguousarray(np.broadcast_to(twiddle[:, :, None], (2, half, size))))
    return fore_lane, fore_row, back_row, back_lane, twist_lane, twist_row


def swapped(value, axis, first):
    count = lax.axis_size(axis)
    route = []
    for i in range(first, count - 1, 2):
        route += [(i, i + 1), (i + 1, i)]
    return lax.ppermute(value, axis, route)


def paired(value):
    groups = [[i, i + 1] for i in range(0, lax.axis_size("cols"), 2)]
    return lax.all_gather(value, "cols", axis_index_groups=groups)


def both_rows(edge_a, edge_b):
    return swapped(edge_a, "rows", 0), swapped(edge_b, "rows", 1)


def on_device(object_field, probe, positions, counts, intensity):
    size = probe.shape[1]
    tile = object_field.shape[1]
    extent = tile + 2 * MARGIN
    row, col = lax.axis_index("rows"), lax.axis_index("cols")
    last = lax.axis_size("rows") - 1
    info = jnp.stack([row % 2, col % 2, row == 0, row == last]).astype(jnp.int32)
    tables = constants(size)
    order = jnp.asarray(split_order(size)).astype(jnp.bfloat16)
    positions, intensity = positions[0, 0], intensity[0, 0]
    plane, strip = shaped(extent, HALF), shaped(2, extent, HALF)
    corner = shaped(2, 2, MARGIN, HALF)

    edge, side = shaped(2, MARGIN, tile), shaped(2, tile, MARGIN)
    edge_a, edge_b, side_a, side_b = whole(cut_body, (edge, edge, side, side), (info,), (object_field,))
    halos = both_rows(edge_a, edge_b)
    far_edge, near_edge = swapped(side_b, "cols", 1), paired(side_a)
    measured, rolled = prepare(positions, intensity, probe, order)
    *ext, corner_a, corner_b = whole(
        extend_body, (plane, plane, strip, corner, corner), (info,), (object_field, *halos)
    )
    far_corner = swapped(corner_b, "cols", 1)
    sides = near_edge, paired(corner_a), far_edge, far_corner
    out_r, out_i, out_b, in_a, in_b = gradient(
        True, info, positions, counts, ext, sides, measured, rolled, tables
    )

    far = swapped(out_b, "cols", 1)
    near = paired(out_r), paired(out_i)
    piece = shaped(2, 2, extent // 2, HALF)
    total, edge_a, edge_b = whole(
        join_body, (shaped(2, 2, extent, HALF), piece, piece), (info,), (in_a, in_b, *near, far)
    )
    halos = both_rows(edge_a, edge_b)
    ext = whole(update_body, (plane, plane, strip), (info,), (*ext, total, *halos))
    sides = paired(ext[0]), paired(ext[1]), swapped(ext[2], "cols", 1)
    corner_a, edge_a, corner_b, edge_b, in_a, in_b = gradient(
        False, info, positions, counts, ext, sides, measured, rolled, tables
    )

    piece = shaped(2, 2, MARGIN, HALF)
    far_corner = swapped(corner_b, "cols", 1)
    rows_a, rows_b, edge_b = whole(
        corner_body, (piece, piece, side), (info,), (in_a, in_b, paired(corner_a), far_corner, edge_b)
    )
    halos = both_rows(rows_a, rows_b)
    sides = paired(edge_a), swapped(edge_b, "cols", 1)
    return whole(finish_body, (shaped(2, tile, tile),), (info,), (*ext, in_a, in_b, *sides, *halos))[0]


def solution(mesh):
    placed = (
        P(None, "rows", "cols"),
        P(),
        P("rows", "cols", None, None),
        P("rows", "cols"),
        P("rows", "cols", None, None, None),
    )
    return jax.shard_map(
        on_device, mesh=mesh, in_specs=placed, out_specs=P(None, "rows", "cols"), check_vma=False
    )
```

```python
import functools

import jax
import jax.numpy as jnp
import numpy as np
from jax import lax
from jax.experimental import pallas as pl
from jax.experimental.pallas import tpu as pltpu
from jax.sharding import PartitionSpec as P

MARGIN = 128
HALF = 128
GROUP = 2


step_rate = 0.02
photon_unit = 0.001


def rotation_tables(length):
    half = length // 2
    index = np.arange(half, dtype=np.int64)
    angle = (index[:, None] * index[None, :] % half) * (2.0 * np.pi / half)
    norm = 1.0 / np.sqrt(length)
    cosine = np.cos(angle) * norm
    sine = np.sin(angle) * norm
    mixed = np.block([[cosine, -sine], [sine, cosine]]).astype(np.float32)
    turn = index * (2.0 * np.pi / length)
    twiddle = np.stack([np.cos(turn), -np.sin(turn)]).astype(np.float32)
    return mixed, twiddle


def split_order(length):
    half = length // 2
    order = np.concatenate([np.arange(half) * 2, np.arange(half) * 2 + 1])
    return (np.arange(length)[:, None] == order[None, :]).astype(np.float32)


VMEM = pl.BlockSpec(memory_space=pltpu.VMEM)
SMEM = pl.BlockSpec(memory_space=pltpu.SMEM)
ANY = pl.BlockSpec(memory_space=pl.ANY)


def shaped(*dims):
    return jax.ShapeDtypeStruct(dims, jnp.float32)


def whole(body, outs, scalars, arrays, scratch=(), limit=40 << 20, flops=1 << 20, unread=()):
    return pl.pallas_call(
        body,
        out_shape=outs,
        in_specs=[SMEM] * len(scalars) + [VMEM] * len(arrays) + [ANY] * len(unread),
        out_specs=tuple(VMEM for _ in outs),
        scratch_shapes=scratch,
        compiler_params=pltpu.CompilerParams(vmem_limit_bytes=limit),
        cost_estimate=pl.CostEstimate(flops=flops, bytes_accessed=8 << 20, transcendentals=0),
    )(*scalars, *arrays, *unread)


def cut_body(info, tile, edge_a, edge_b, side_a, side_b):
    last = tile.shape[1] - MARGIN
    edge_a[...] = tile[:, pl.ds(pl.multiple_of((1 - info[0]) * last, 8), MARGIN), :]
    edge_b[...] = tile[:, pl.ds(pl.multiple_of(info[0] * last, 8), MARGIN), :]
    left, right = slice(0, MARGIN), slice(last, last + MARGIN)

    @pl.when(info[1] == 1)
    def _():
        side_a[...] = tile[:, :, left]
        side_b[...] = tile[:, :, right]

    @pl.when(info[1] == 0)
    def _():
        side_a[...] = tile[:, :, right]
        side_b[...] = tile[:, :, left]


def prepare_body(positions, intensity, probe, order, earlier, measured, rolled, held, arrived):
    slots, size = intensity.shape[0], probe.shape[1]
    half = size // 2
    moves = [order[:half], order[half:]]
    copies = [
        pltpu.make_async_copy(intensity.at[:, :, pl.ds(half * block, half)], held.at[block], arrived.at[block])
        for block in range(2)
    ]
    for copy in copies:
        copy.start()

    def turn(slot, carry):
        shift = lax.rem(positions[slot, 1], size)
        for part in range(2):
            rolled[slot, part] = pltpu.roll(probe[part], shift, 1)
        return carry

    lax.fori_loop(0, slots, turn, 0)
    for copy in copies:
        copy.wait()

    def reorder(slot, carry):
        for parity in range(2):
            moved = jnp.zeros((half, size), jnp.float32)
            for block in range(2):
                counts = held[block, slot, pl.ds(parity, half, stride=2), :]
                upper = lax.shift_right_logical(counts, 8).astype(jnp.float32).astype(jnp.bfloat16)
                lower = lax.bitwise_and(counts, 255).astype(jnp.float32).astype(jnp.bfloat16)
                high = jnp.dot(upper, moves[block], preferred_element_type=jnp.float32)
                low = jnp.dot(lower, moves[block], preferred_element_type=jnp.float32)
                moved = moved + (256.0 * high + low)
            measured[slot, parity] = moved * photon_unit
        return carry

    lax.fori_loop(0, slots, reorder, 0)


def prepare(positions, intensity, probe, order, earlier):
    slots, size = intensity.shape[0], probe.shape[1]
    half = size // 2
    return pl.pallas_call(
        prepare_body,
        out_shape=(shaped(slots, 2, half, size), shaped(slots, 2, size, size)),
        in_specs=[SMEM, ANY, VMEM, VMEM, ANY],
        out_specs=(VMEM, VMEM),
        scratch_shapes=[pltpu.VMEM((2, slots, size, half), jnp.int32), pltpu.SemaphoreType.DMA((2,))],
        compiler_params=pltpu.CompilerParams(vmem_limit_bytes=24 << 20),
        cost_estimate=pl.CostEstimate(flops=slots * 2**27, bytes_accessed=8 << 20, transcendentals=0),
    )(positions, intensity, probe, order, earlier)


def halves(value):
    upper = value.astype(jnp.bfloat16)
    lower = (value - upper.astype(jnp.float32)).astype(jnp.bfloat16)
    return upper, lower


def times_table(value, table):
    upper, lower = halves(value)
    packed = jnp.concatenate([upper, lower, upper], axis=1)
    return jnp.dot(packed, table, preferred_element_type=jnp.float32)


def table_times(table, value):
    upper, lower = halves(value)
    packed = jnp.concatenate([upper, lower, upper], axis=0)
    return jnp.dot(table, packed, preferred_element_type=jnp.float32)


def wide(left, right):
    return jnp.concatenate([left, right], axis=1)


def tall(upper, lower):
    return jnp.concatenate([upper, lower], axis=0)


def places(odd_col):
    return 3 - 3 * odd_col, 2 - odd_col, 1 + odd_col, 3 * odd_col


def gradient_body(
    first, info, positions, counts, ext_r, ext_i, ext_b, *refs
):
    if first:
        near_edge, near_corner, far_edge, far_corner, *refs = refs
    else:
        near_r, near_i, far_strip, *refs = refs
    measured, rolled, fore_lane, fore_row, back_row, back_lane, twist_lane, twist_row, *refs = refs
    out_r, out_i, out_b, in_a, in_b, field, sums = refs
    size = rolled.shape[2]
    half = size // 2
    extent = field.shape[2]
    odd_col = info[1]
    other = 1 - odd_col
    near_at, a_at, b_at, far_at = places(odd_col)
    lanes = lax.broadcasted_iota(jnp.int32, (1, half), 1)
    sums[...] = jnp.zeros_like(sums)
    field[a_at, 0] = ext_r[...]
    field[a_at, 1] = ext_i[...]
    field[b_at] = ext_b[...]
    if first:
        upper, middle, lower = slice(0, MARGIN), slice(MARGIN, extent - MARGIN), slice(extent - MARGIN, extent)
        field[near_at, :, middle] = near_edge[other]
        field[near_at, :, upper] = near_corner[other, 0]
        field[near_at, :, lower] = near_corner[other, 1]
        field[far_at, :, middle] = jnp.where(info[4] == 1, 0.0, far_edge[odd_col])
        field[far_at, :, upper] = far_corner[0]
        field[far_at, :, lower] = far_corner[1]
    else:
        field[near_at, 0] = near_r[other]
        field[near_at, 1] = near_i[other]
        field[far_at] = far_strip[...]
    lane_r, lane_i = twist_lane[0], twist_lane[1]
    row_r, row_i = twist_row[0], twist_row[1]

    def enter(slot):
        rows = pl.ds(positions[slot, 0], size)
        waves = []
        for block in range(2):
            near = lanes + half * block >= positions[slot, 1]
            cut = slice(half * block, half * (block + 1))
            p_r, p_i = rolled[slot, 0, :, cut], rolled[slot, 1, :, cut]
            o_r = jnp.where(near, field[block, 0, rows, :], field[block + 2, 0, rows, :])
            o_i = jnp.where(near, field[block, 1, rows, :], field[block + 2, 1, rows, :])
            waves.append((p_r * o_r - p_i * o_i, p_r * o_i + p_i * o_r))
        (r0, i0), (r1, i1) = waves
        d_r, d_i = r0 - r1, i0 - i1
        return [
            wide(r0 + r1, i0 + i1),
            wide(d_r * lane_r - d_i * lane_i, d_r * lane_i + d_i * lane_r),
        ]

    def cross(pair):
        even, odd = pair
        r_all = wide(even[:, :half], odd[:, :half])
        i_all = wide(even[:, half:], odd[:, half:])
        r0, r1 = r_all[:half], r_all[half:]
        i0, i1 = i_all[:half], i_all[half:]
        d_r, d_i = r0 - r1, i0 - i1
        return [
            tall(r0 + r1, i0 + i1),
            tall(d_r * row_r - d_i * row_i, d_r * row_i + d_i * row_r),
        ]

    def scale(slot, pair):
        scaled = []
        for parity, spectrum in enumerate(pair):
            s_r, s_i = spectrum[:half], spectrum[half:]
            misfit = s_r * s_r + s_i * s_i - measured[slot, parity]
            scaled.append(tall(misfit * s_r, misfit * s_i))
        return scaled

    def cross_back(pair):
        even, odd = pair
        e_r, e_i = even[:half], even[half:]
        o_r, o_i = odd[:half], odd[half:]
        t_r = o_r * row_r + o_i * row_i
        t_i = o_i * row_r - o_r * row_i
        full_r = tall(e_r + t_r, e_r - t_r)
        full_i = tall(e_i + t_i, e_i - t_i)
        return [
            wide(full_r[:, :half], full_i[:, :half]),
            wide(full_r[:, half:], full_i[:, half:]),
        ]

    def leave(slot, pair, keep):
        rows = pl.ds(positions[slot, 0], size)
        even, odd = pair
        e_r, e_i = even[:, :half], even[:, half:]
        o_r, o_i = odd[:, :half], odd[:, half:]
        t_r = o_r * lane_r + o_i * lane_i
        t_i = o_i * lane_r - o_r * lane_i
        outs = [(e_r + t_r, e_i + t_i), (e_r - t_r, e_i - t_i)]
        for block, (b_r, b_i) in enumerate(outs):
            place = lanes + half * block
            near = place >= positions[slot, 1]
            far = place < positions[slot, 1]
            if keep is not None:
                near, far = near & keep, far & keep
            cut = slice(half * block, half * (block + 1))
            p_r, p_i = rolled[slot, 0, :, cut], rolled[slot, 1, :, cut]
            terms = (p_r * b_r + p_i * b_i, p_r * b_i - p_i * b_r)
            for part, term in enumerate(terms):
                sums[block, part, rows, :] += jnp.where(near, term, 0.0)
                sums[block + 2, part, rows, :] += jnp.where(far, term, 0.0)

    def one_group(group, carry):
        slots = [GROUP * group + i for i in range(GROUP)]
        live = [None] + [slot < counts[0, 0] for slot in slots[1:]]
        pairs = [enter(slot) for slot in slots]
        pairs = [[times_table(half_, fore_lane[...]) for half_ in pair] for pair in pairs]
        pairs = [cross(pair) for pair in pairs]
        pairs = [[table_times(fore_row[...], half_) for half_ in pair] for pair in pairs]
        pairs = [scale(slot, pair) for slot, pair in zip(slots, pairs)]
        pairs = [[table_times(back_row[...], half_) for half_ in pair] for pair in pairs]
        pairs = [cross_back(pair) for pair in pairs]
        pairs = [[times_table(half_, back_lane[...]) for half_ in pair] for pair in pairs]
        for slot, pair, keep in zip(slots, pairs, live):
            leave(slot, pair, keep)
        return carry

    lax.fori_loop(0, (counts[0, 0] + GROUP - 1) // GROUP, one_group, 0)
    out_r[...] = sums[near_at, 0]
    out_i[...] = sums[near_at, 1]
    out_b[...] = sums[far_at]
    in_a[...] = sums[a_at]
    in_b[...] = sums[b_at]


def gradient(first, info, positions, counts, ext, sides, measured, rolled, tables):
    extent = ext[0].shape[0]
    plane, strip = shaped(extent, HALF), shaped(2, extent, HALF)
    return whole(
        functools.partial(gradient_body, first),
        (plane, plane, strip, strip, strip),
        (info, positions, counts),
        (*ext, *sides, measured, rolled, *tables),
        [pltpu.VMEM((4, 2, extent, HALF), jnp.float32)] * 2,
        flops=6 * 8 * 3 * 2**25,
    )


def extend_body(info, tile, halo_a, halo_b, near, far, ext_r, ext_i, ext_b, corner_a, corner_b):
    size = tile.shape[1]
    odd_row, odd_col = info[0], info[1]

    def fill(cut_a, cut_b):
        above = [jnp.where(odd_row == 1, halo_a[part], halo_b[part]) for part in range(2)]
        below = [jnp.where(odd_row == 1, halo_b[part], halo_a[part]) for part in range(2)]
        targets = [ext_r, ext_i]
        for part in range(2):
            corner_a[0, part] = above[part][:, cut_a]
            corner_a[1, part] = below[part][:, cut_a]
            corner_b[0, part] = above[part][:, cut_b]
            corner_b[1, part] = below[part][:, cut_b]
            targets[part][:MARGIN, :] = above[part][:, cut_a]
            targets[part][MARGIN : MARGIN + size, :] = tile[part, :, cut_a]
            targets[part][MARGIN + size :, :] = below[part][:, cut_a]
            ext_b[part, :MARGIN] = above[part][:, cut_b]
            ext_b[part, MARGIN : MARGIN + size] = tile[part, :, cut_b]
            ext_b[part, MARGIN + size :] = below[part][:, cut_b]

    left, right = slice(0, HALF), slice(HALF, 2 * HALF)

    @pl.when(odd_col == 1)
    def _():
        fill(left, right)

    @pl.when(odd_col == 0)
    def _():
        fill(right, left)


def outgoing(odd_row, total, width, out_a, out_b):
    extent = total.shape[1]
    out_a[...] = total[:, pl.ds(pl.multiple_of((1 - odd_row) * (extent - width), 8), width), :]
    out_b[...] = total[:, pl.ds(pl.multiple_of(odd_row * (extent - width), 8), width), :]


def join_near_body(width, info, inner, near_r, near_i, total, out_a, out_b):
    other = 1 - info[1]
    total[0] = inner[0] + near_r[other]
    total[1] = inner[1] + near_i[other]
    outgoing(info[0], total, width, out_a, out_b)


def join_far_body(width, info, inner, strip, total, out_a, out_b):
    total[...] = inner[...] + strip[...]
    outgoing(info[0], total, width, out_a, out_b)


def updated(info, part, ext, total, halo_a, halo_b):
    middle = total.shape[1] // 2
    above = total[part, :middle] + jnp.where(info[0] == 1, halo_a[part], halo_b[part])
    below = total[part, middle:] + jnp.where(info[0] == 1, halo_b[part], halo_a[part])
    row = lax.broadcasted_iota(jnp.int32, (middle, HALF), 0)
    above = jnp.where((info[2] == 1) & (row < MARGIN), 0.0, above)
    below = jnp.where((info[3] == 1) & (row >= middle - MARGIN), 0.0, below)
    return tall(ext[:middle] - step_rate * above, ext[middle:] - step_rate * below)


def update_near_body(info, ext_r, ext_i, total, halo_a, halo_b, out_r, out_i):
    out_r[...] = updated(info, 0, ext_r, total, halo_a, halo_b)
    out_i[...] = updated(info, 1, ext_i, total, halo_a, halo_b)


def update_far_body(info, ext_b, total, halo_a, halo_b, out):
    for part in range(2):
        out[part] = updated(info, part, ext_b.at[part], total, halo_a, halo_b)


def finish_body(info, ext_r, ext_i, ext_b, total_a, total_b, near_a, near_b, far_a, far_b, out):
    size = out.shape[1]
    half = size // 2
    upper, lower = slice(MARGIN, MARGIN + half), slice(MARGIN + half, MARGIN + size)

    def settle(cut, ext, total, halo_a, halo_b):
        for part in range(2):
            above = total[part, upper] + jnp.where(info[0] == 1, halo_a[part], halo_b[part])
            below = total[part, lower] + jnp.where(info[0] == 1, halo_b[part], halo_a[part])
            out[part, :half, cut] = ext[part][upper] - step_rate * above
            out[part, half:, cut] = ext[part][lower] - step_rate * below

    def place(cut_a, cut_b):
        settle(cut_a, [ext_r, ext_i], total_a, near_a, near_b)
        settle(cut_b, [ext_b.at[0], ext_b.at[1]], total_b, far_a, far_b)

    left, right = slice(0, HALF), slice(HALF, 2 * HALF)

    @pl.when(info[1] == 1)
    def _():
        place(left, right)

    @pl.when(info[1] == 0)
    def _():
        place(right, left)


def constants(size):
    half = size // 2
    mixed, twiddle = rotation_tables(size)
    upper = mixed.astype(jnp.bfloat16)
    lower = (mixed - upper.astype(np.float32)).astype(jnp.bfloat16)
    fore_lane = jnp.asarray(np.concatenate([upper, upper, lower], axis=0))
    back_row = jnp.asarray(np.concatenate([upper, upper, lower], axis=1))
    fore_row = jnp.asarray(np.concatenate([upper.T, upper.T, lower.T], axis=1))
    back_lane = jnp.asarray(np.concatenate([upper.T, upper.T, lower.T], axis=0))
    twist_lane = jnp.asarray(twiddle.reshape(2, 1, half))
    twist_row = jnp.asarray(np.ascontiguousarray(np.broadcast_to(twiddle[:, :, None], (2, half, size))))
    return fore_lane, fore_row, back_row, back_lane, twist_lane, twist_row


def swapped(value, axis, first):
    count = lax.axis_size(axis)
    route = []
    for i in range(first, count - 1, 2):
        route += [(i, i + 1), (i + 1, i)]
    return lax.ppermute(value, axis, route)


def paired(value, first=0):
    count = lax.axis_size("cols")
    groups = [[i, (i + 1) % count] for i in range(first, count, 2)]
    return lax.all_gather(value, "cols", axis_index_groups=groups)


def both_rows(edge_a, edge_b):
    return swapped(edge_a, "rows", 0), swapped(edge_b, "rows", 1)


def summed(info, width, out_r, out_i, out_b, in_a, in_b):
    extent = in_a.shape[1]
    strip, piece = shaped(2, extent, HALF), shaped(2, width, HALF)
    far = swapped(out_b, "cols", 1)
    near = paired(out_r), paired(out_i)
    total_a, *edges = whole(functools.partial(join_near_body, width), (strip, piece, piece), (info,), (in_a, *near))
    halos_a = both_rows(*edges)
    total_b, *edges = whole(functools.partial(join_far_body, width), (strip, piece, piece), (info,), (in_b, far))
    halos_b = both_rows(*edges)
    return total_a, halos_a, total_b, halos_b


def on_device(object_field, probe, positions, counts, intensity):
    size = probe.shape[1]
    tile = object_field.shape[1]
    extent = tile + 2 * MARGIN
    row, col = lax.axis_index("rows"), lax.axis_index("cols")
    last, end = lax.axis_size("rows") - 1, lax.axis_size("cols") - 1
    info = jnp.stack(
        [row % 2, col % 2, row == 0, row == last, (col == 0) | (col == end)]
    ).astype(jnp.int32)
    tables = constants(size)
    order = jnp.asarray(split_order(size)).astype(jnp.bfloat16)
    positions, intensity = positions[0, 0], intensity[0, 0]
    plane, strip = shaped(extent, HALF), shaped(2, extent, HALF)
    corner = shaped(2, 2, MARGIN, HALF)

    edge, side = shaped(2, MARGIN, tile), shaped(2, tile, MARGIN)
    edge_a, edge_b, side_a, side_b = whole(cut_body, (edge, edge, side, side), (info,), (object_field,))
    halos = both_rows(edge_a, edge_b)
    far_edge, near_edge = paired(side_b, 1), paired(side_a)
    *ext, corner_a, corner_b = whole(
        extend_body,
        (plane, plane, strip, corner, corner),
        (info,),
        (object_field, *halos),
        unread=(near_edge, far_edge),
    )
    measured, rolled = prepare(positions, intensity, probe, order, corner_a)
    far_corner = swapped(corner_b, "cols", 1)
    sides = near_edge, paired(corner_a), far_edge, far_corner
    parts = gradient(True, info, positions, counts, ext, sides, measured, rolled, tables)
    total_a, halos_a, total_b, halos_b = summed(info, extent // 2, *parts)
    near_ext = whole(update_near_body, (plane, plane), (info,), (*ext[:2], total_a, *halos_a))
    far_ext = whole(update_far_body, (strip,), (info,), (ext[2], total_b, *halos_b))
    ext = (*near_ext, *far_ext)
    sides = paired(ext[0]), paired(ext[1]), swapped(ext[2], "cols", 1)
    parts = gradient(False, info, positions, counts, ext, sides, measured, rolled, tables)
    total_a, halos_a, total_b, halos_b = summed(info, MARGIN, *parts)
    return whole(
        finish_body, (shaped(2, tile, tile),), (info,), (*ext, total_a, total_b, *halos_a, *halos_b)
    )[0]


def solution(mesh):
    placed = (
        P(None, "rows", "cols"),
        P(),
        P("rows", "cols", None, None),
        P("rows", "cols"),
        P("rows", "cols", None, None, None),
    )
    return jax.shard_map(
        on_device, mesh=mesh, in_specs=placed, out_specs=P(None, "rows", "cols"), check_vma=False
    )
```

```python
import functools

import jax
import jax.numpy as jnp
import numpy as np
from jax import lax
from jax.experimental import pallas as pl
from jax.experimental.pallas import tpu as pltpu
from jax.sharding import PartitionSpec as P

MARGIN = 128
HALF = 128
GROUP = 2


step_rate = 0.02
photon_unit = 0.001


def rotation_tables(length):
    half = length // 2
    index = np.arange(half, dtype=np.int64)
    angle = (index[:, None] * index[None, :] % half) * (2.0 * np.pi / half)
    norm = 1.0 / np.sqrt(length)
    cosine = np.cos(angle) * norm
    sine = np.sin(angle) * norm
    mixed = np.block([[cosine, -sine], [sine, cosine]]).astype(np.float32)
    turn = index * (2.0 * np.pi / length)
    twiddle = np.stack([np.cos(turn), -np.sin(turn)]).astype(np.float32)
    return mixed, twiddle


def split_order(length):
    half = length // 2
    order = np.concatenate([np.arange(half) * 2, np.arange(half) * 2 + 1])
    return (np.arange(length)[:, None] == order[None, :]).astype(np.float32)


VMEM = pl.BlockSpec(memory_space=pltpu.VMEM)
SMEM = pl.BlockSpec(memory_space=pltpu.SMEM)
ANY = pl.BlockSpec(memory_space=pl.ANY)


def shaped(*dims):
    return jax.ShapeDtypeStruct(dims, jnp.float32)


def whole(body, outs, scalars, arrays, scratch=(), limit=40 << 20, flops=1 << 20, unread=()):
    return pl.pallas_call(
        body,
        out_shape=outs,
        in_specs=[SMEM] * len(scalars) + [VMEM] * len(arrays) + [ANY] * len(unread),
        out_specs=tuple(VMEM for _ in outs),
        scratch_shapes=scratch,
        compiler_params=pltpu.CompilerParams(vmem_limit_bytes=limit),
        cost_estimate=pl.CostEstimate(flops=flops, bytes_accessed=8 << 20, transcendentals=0),
    )(*scalars, *arrays, *unread)


def cut_body(info, tile, edge_a, edge_b, side_a, side_b):
    last = tile.shape[1] - MARGIN
    edge_a[...] = tile[:, pl.ds(pl.multiple_of((1 - info[0]) * last, 8), MARGIN), :]
    edge_b[...] = tile[:, pl.ds(pl.multiple_of(info[0] * last, 8), MARGIN), :]
    left, right = slice(0, MARGIN), slice(last, last + MARGIN)

    @pl.when(info[1] == 1)
    def _():
        side_a[...] = tile[:, :, left]
        side_b[...] = tile[:, :, right]

    @pl.when(info[1] == 0)
    def _():
        side_a[...] = tile[:, :, right]
        side_b[...] = tile[:, :, left]


def prepare_body(positions, intensity, probe, order, earlier, measured, rolled, held, arrived):
    slots, size = intensity.shape[0], probe.shape[1]
    half = size // 2
    moves = [order[:half], order[half:]]
    copies = [
        pltpu.make_async_copy(intensity.at[:, :, pl.ds(half * block, half)], held.at[block], arrived.at[block])
        for block in range(2)
    ]
    for copy in copies:
        copy.start()

    def turn(slot, carry):
        shift = lax.rem(positions[slot, 1], size)
        for part in range(2):
            rolled[slot, part] = pltpu.roll(probe[part], shift, 1)
        return carry

    lax.fori_loop(0, slots, turn, 0)
    for copy in copies:
        copy.wait()

    def reorder(slot, carry):
        for parity in range(2):
            moved = jnp.zeros((half, size), jnp.float32)
            for block in range(2):
                counts = held[block, slot, pl.ds(parity, half, stride=2), :]
                upper = lax.shift_right_logical(counts, 8).astype(jnp.float32).astype(jnp.bfloat16)
                lower = lax.bitwise_and(counts, 255).astype(jnp.float32).astype(jnp.bfloat16)
                high = jnp.dot(upper, moves[block], preferred_element_type=jnp.float32)
                low = jnp.dot(lower, moves[block], preferred_element_type=jnp.float32)
                moved = moved + (256.0 * high + low)
            measured[slot, parity] = moved * photon_unit
        return carry

    lax.fori_loop(0, slots, reorder, 0)


def prepare(positions, intensity, probe, order, earlier):
    slots, size = intensity.shape[0], probe.shape[1]
    half = size // 2
    return pl.pallas_call(
        prepare_body,
        out_shape=(shaped(slots, 2, half, size), shaped(slots, 2, size, size)),
        in_specs=[SMEM, ANY, VMEM, VMEM, ANY],
        out_specs=(VMEM, VMEM),
        scratch_shapes=[pltpu.VMEM((2, slots, size, half), jnp.int32), pltpu.SemaphoreType.DMA((2,))],
        compiler_params=pltpu.CompilerParams(vmem_limit_bytes=24 << 20),
        cost_estimate=pl.CostEstimate(flops=slots * 2**27, bytes_accessed=8 << 20, transcendentals=0),
    )(positions, intensity, probe, order, earlier)


def halves(value):
    upper = value.astype(jnp.bfloat16)
    lower = (value - upper.astype(jnp.float32)).astype(jnp.bfloat16)
    return upper, lower


def times_table(value, table):
    upper, lower = halves(value)
    packed = jnp.concatenate([upper, lower, upper], axis=1)
    return jnp.dot(packed, table, preferred_element_type=jnp.float32)


def table_times(table, value):
    upper, lower = halves(value)
    packed = jnp.concatenate([upper, lower, upper], axis=0)
    return jnp.dot(table, packed, preferred_element_type=jnp.float32)


def wide(left, right):
    return jnp.concatenate([left, right], axis=1)


def tall(upper, lower):
    return jnp.concatenate([upper, lower], axis=0)


def places(odd_col):
    return 3 - 3 * odd_col, 2 - odd_col, 1 + odd_col, 3 * odd_col


def gradient_body(
    first, info, positions, counts, ext_r, ext_i, ext_b, *refs
):
    if first:
        near_edge, near_corner, far_edge, far_corner, *refs = refs
    else:
        near_r, near_i, far_strip, *refs = refs
    measured, rolled, fore_lane, fore_row, back_row, back_lane, twist_lane, twist_row, *refs = refs
    out_r, out_i, out_b, sums, field = refs
    size = rolled.shape[2]
    half = size // 2
    extent = field.shape[2]
    odd_col = info[1]
    other = 1 - odd_col
    near_at, a_at, b_at, far_at = places(odd_col)
    lanes = lax.broadcasted_iota(jnp.int32, (1, half), 1)
    sums[...] = jnp.zeros_like(sums)
    field[a_at, 0] = ext_r[...]
    field[a_at, 1] = ext_i[...]
    field[b_at] = ext_b[...]
    if first:
        upper, middle, lower = slice(0, MARGIN), slice(MARGIN, extent - MARGIN), slice(extent - MARGIN, extent)
        field[near_at, :, middle] = near_edge[other]
        field[near_at, :, upper] = near_corner[other, 0]
        field[near_at, :, lower] = near_corner[other, 1]
        field[far_at, :, middle] = far_edge[...]
        field[far_at, :, upper] = far_corner[0]
        field[far_at, :, lower] = far_corner[1]
    else:
        field[near_at, 0] = near_r[other]
        field[near_at, 1] = near_i[other]
        field[far_at] = far_strip[...]
    lane_r, lane_i = twist_lane[0], twist_lane[1]
    row_r, row_i = twist_row[0], twist_row[1]

    def enter(slot):
        rows = pl.ds(positions[slot, 0], size)
        waves = []
        for block in range(2):
            near = lanes + half * block >= positions[slot, 1]
            cut = slice(half * block, half * (block + 1))
            p_r, p_i = rolled[slot, 0, :, cut], rolled[slot, 1, :, cut]
            o_r = jnp.where(near, field[block, 0, rows, :], field[block + 2, 0, rows, :])
            o_i = jnp.where(near, field[block, 1, rows, :], field[block + 2, 1, rows, :])
            waves.append((p_r * o_r - p_i * o_i, p_r * o_i + p_i * o_r))
        (r0, i0), (r1, i1) = waves
        d_r, d_i = r0 - r1, i0 - i1
        return [
            wide(r0 + r1, i0 + i1),
            wide(d_r * lane_r - d_i * lane_i, d_r * lane_i + d_i * lane_r),
        ]

    def cross(pair):
        even, odd = pair
        r_all = wide(even[:, :half], odd[:, :half])
        i_all = wide(even[:, half:], odd[:, half:])
        r0, r1 = r_all[:half], r_all[half:]
        i0, i1 = i_all[:half], i_all[half:]
        d_r, d_i = r0 - r1, i0 - i1
        return [
            tall(r0 + r1, i0 + i1),
            tall(d_r * row_r - d_i * row_i, d_r * row_i + d_i * row_r),
        ]

    def scale(slot, pair):
        scaled = []
        for parity, spectrum in enumerate(pair):
            s_r, s_i = spectrum[:half], spectrum[half:]
            misfit = s_r * s_r + s_i * s_i - measured[slot, parity]
            scaled.append(tall(misfit * s_r, misfit * s_i))
        return scaled

    def cross_back(pair):
        even, odd = pair
        e_r, e_i = even[:half], even[half:]
        o_r, o_i = odd[:half], odd[half:]
        t_r = o_r * row_r + o_i * row_i
        t_i = o_i * row_r - o_r * row_i
        full_r = tall(e_r + t_r, e_r - t_r)
        full_i = tall(e_i + t_i, e_i - t_i)
        return [
            wide(full_r[:, :half], full_i[:, :half]),
            wide(full_r[:, half:], full_i[:, half:]),
        ]

    def leave(slot, pair, keep):
        rows = pl.ds(positions[slot, 0], size)
        even, odd = pair
        e_r, e_i = even[:, :half], even[:, half:]
        o_r, o_i = odd[:, :half], odd[:, half:]
        t_r = o_r * lane_r + o_i * lane_i
        t_i = o_i * lane_r - o_r * lane_i
        outs = [(e_r + t_r, e_i + t_i), (e_r - t_r, e_i - t_i)]
        for block, (b_r, b_i) in enumerate(outs):
            place = lanes + half * block
            near = place >= positions[slot, 1]
            far = place < positions[slot, 1]
            if keep is not None:
                near, far = near & keep, far & keep
            cut = slice(half * block, half * (block + 1))
            p_r, p_i = rolled[slot, 0, :, cut], rolled[slot, 1, :, cut]
            terms = (p_r * b_r + p_i * b_i, p_r * b_i - p_i * b_r)
            for part, term in enumerate(terms):
                sums[block, part, rows, :] += jnp.where(near, term, 0.0)
                sums[block + 2, part, rows, :] += jnp.where(far, term, 0.0)

    def one_group(group, carry):
        slots = [GROUP * group + i for i in range(GROUP)]
        live = [None] + [slot < counts[0, 0] for slot in slots[1:]]
        pairs = [enter(slot) for slot in slots]
        pairs = [[times_table(half_, fore_lane[...]) for half_ in pair] for pair in pairs]
        pairs = [cross(pair) for pair in pairs]
        pairs = [[table_times(fore_row[...], half_) for half_ in pair] for pair in pairs]
        pairs = [scale(slot, pair) for slot, pair in zip(slots, pairs)]
        pairs = [[table_times(back_row[...], half_) for half_ in pair] for pair in pairs]
        pairs = [cross_back(pair) for pair in pairs]
        pairs = [[times_table(half_, back_lane[...]) for half_ in pair] for pair in pairs]
        for slot, pair, keep in zip(slots, pairs, live):
            leave(slot, pair, keep)
        return carry

    lax.fori_loop(0, (counts[0, 0] + GROUP - 1) // GROUP, one_group, 0)
    out_r[...] = sums[near_at, 0]
    out_i[...] = sums[near_at, 1]
    out_b[...] = sums[far_at]


def gradient(first, info, positions, counts, ext, sides, measured, rolled, tables):
    extent = ext[0].shape[0]
    plane, strip = shaped(extent, HALF), shaped(2, extent, HALF)
    return whole(
        functools.partial(gradient_body, first),
        (plane, plane, strip, shaped(4, 2, extent, HALF)),
        (info, positions, counts),
        (*ext, *sides, measured, rolled, *tables),
        [pltpu.VMEM((4, 2, extent, HALF), jnp.float32)],
        flops=6 * 8 * 3 * 2**25,
    )


def extend_body(info, tile, halo_a, halo_b, near, ext_r, ext_i, ext_b, corner_a, corner_b):
    size = tile.shape[1]
    odd_row, odd_col = info[0], info[1]

    def fill(cut_a, cut_b):
        above = [jnp.where(odd_row == 1, halo_a[part], halo_b[part]) for part in range(2)]
        below = [jnp.where(odd_row == 1, halo_b[part], halo_a[part]) for part in range(2)]
        targets = [ext_r, ext_i]
        for part in range(2):
            corner_a[0, part] = above[part][:, cut_a]
            corner_a[1, part] = below[part][:, cut_a]
            corner_b[0, part] = above[part][:, cut_b]
            corner_b[1, part] = below[part][:, cut_b]
            targets[part][:MARGIN, :] = above[part][:, cut_a]
            targets[part][MARGIN : MARGIN + size, :] = tile[part, :, cut_a]
            targets[part][MARGIN + size :, :] = below[part][:, cut_a]
            ext_b[part, :MARGIN] = above[part][:, cut_b]
            ext_b[part, MARGIN : MARGIN + size] = tile[part, :, cut_b]
            ext_b[part, MARGIN + size :] = below[part][:, cut_b]

    left, right = slice(0, HALF), slice(HALF, 2 * HALF)

    @pl.when(odd_col == 1)
    def _():
        fill(left, right)

    @pl.when(odd_col == 0)
    def _():
        fill(right, left)


def outgoing(odd_row, total, width, out_a, out_b):
    extent = total.shape[1]
    out_a[...] = total[:, pl.ds(pl.multiple_of((1 - odd_row) * (extent - width), 8), width), :]
    out_b[...] = total[:, pl.ds(pl.multiple_of(odd_row * (extent - width), 8), width), :]


def join_near_body(width, info, sums, near_r, near_i, total, out_a, out_b):
    other = 1 - info[1]
    block = places(info[1])[1]
    total[0] = sums[block, 0] + near_r[other]
    total[1] = sums[block, 1] + near_i[other]
    outgoing(info[0], total, width, out_a, out_b)


def join_far_body(width, info, sums, strip, total, out_a, out_b):
    total[...] = sums[places(info[1])[2]] + strip[...]
    outgoing(info[0], total, width, out_a, out_b)


def updated(info, part, ext, total, halo_a, halo_b):
    middle = total.shape[1] // 2
    above = total[part, :middle] + jnp.where(info[0] == 1, halo_a[part], halo_b[part])
    below = total[part, middle:] + jnp.where(info[0] == 1, halo_b[part], halo_a[part])
    row = lax.broadcasted_iota(jnp.int32, (middle, HALF), 0)
    above = jnp.where((info[2] == 1) & (row < MARGIN), 0.0, above)
    below = jnp.where((info[3] == 1) & (row >= middle - MARGIN), 0.0, below)
    return tall(ext[:middle] - step_rate * above, ext[middle:] - step_rate * below)


def update_near_body(info, ext_r, ext_i, total, halo_a, halo_b, out_r, out_i):
    out_r[...] = updated(info, 0, ext_r, total, halo_a, halo_b)
    out_i[...] = updated(info, 1, ext_i, total, halo_a, halo_b)


def update_far_body(info, ext_b, total, halo_a, halo_b, out):
    for part in range(2):
        out[part] = updated(info, part, ext_b.at[part], total, halo_a, halo_b)


def finish_body(info, ext_r, ext_i, ext_b, total_a, total_b, near_a, near_b, far_a, far_b, out):
    size = out.shape[1]
    half = size // 2
    upper, lower = slice(MARGIN, MARGIN + half), slice(MARGIN + half, MARGIN + size)

    def settle(cut, ext, total, halo_a, halo_b):
        for part in range(2):
            above = total[part, upper] + jnp.where(info[0] == 1, halo_a[part], halo_b[part])
            below = total[part, lower] + jnp.where(info[0] == 1, halo_b[part], halo_a[part])
            out[part, :half, cut] = ext[part][upper] - step_rate * above
            out[part, half:, cut] = ext[part][lower] - step_rate * below

    def place(cut_a, cut_b):
        settle(cut_a, [ext_r, ext_i], total_a, near_a, near_b)
        settle(cut_b, [ext_b.at[0], ext_b.at[1]], total_b, far_a, far_b)

    left, right = slice(0, HALF), slice(HALF, 2 * HALF)

    @pl.when(info[1] == 1)
    def _():
        place(left, right)

    @pl.when(info[1] == 0)
    def _():
        place(right, left)


def constants(size):
    half = size // 2
    mixed, twiddle = rotation_tables(size)
    upper = mixed.astype(jnp.bfloat16)
    lower = (mixed - upper.astype(np.float32)).astype(jnp.bfloat16)
    fore_lane = jnp.asarray(np.concatenate([upper, upper, lower], axis=0))
    back_row = jnp.asarray(np.concatenate([upper, upper, lower], axis=1))
    fore_row = jnp.asarray(np.concatenate([upper.T, upper.T, lower.T], axis=1))
    back_lane = jnp.asarray(np.concatenate([upper.T, upper.T, lower.T], axis=0))
    twist_lane = jnp.asarray(twiddle.reshape(2, 1, half))
    twist_row = jnp.asarray(np.ascontiguousarray(np.broadcast_to(twiddle[:, :, None], (2, half, size))))
    return fore_lane, fore_row, back_row, back_lane, twist_lane, twist_row


def swapped(value, axis, first):
    count = lax.axis_size(axis)
    route = []
    for i in range(first, count - 1, 2):
        route += [(i, i + 1), (i + 1, i)]
    return lax.ppermute(value, axis, route)


def paired(value):
    groups = [[i, i + 1] for i in range(0, lax.axis_size("cols"), 2)]
    return lax.all_gather(value, "cols", axis_index_groups=groups)


def both_rows(edge_a, edge_b):
    return swapped(edge_a, "rows", 0), swapped(edge_b, "rows", 1)


def summed(info, width, out_r, out_i, out_b, sums):
    extent = sums.shape[2]
    strip, piece = shaped(2, extent, HALF), shaped(2, width, HALF)
    far = swapped(out_b, "cols", 1)
    near = paired(out_r), paired(out_i)
    total_a, *edges = whole(functools.partial(join_near_body, width), (strip, piece, piece), (info,), (sums, *near))
    halos_a = both_rows(*edges)
    total_b, *edges = whole(functools.partial(join_far_body, width), (strip, piece, piece), (info,), (sums, far))
    halos_b = both_rows(*edges)
    return total_a, halos_a, total_b, halos_b


def on_device(object_field, probe, positions, counts, intensity):
    size = probe.shape[1]
    tile = object_field.shape[1]
    extent = tile + 2 * MARGIN
    row, col = lax.axis_index("rows"), lax.axis_index("cols")
    last = lax.axis_size("rows") - 1
    info = jnp.stack([row % 2, col % 2, row == 0, row == last]).astype(jnp.int32)
    tables = constants(size)
    order = jnp.asarray(split_order(size)).astype(jnp.bfloat16)
    positions, intensity = positions[0, 0], intensity[0, 0]
    plane, strip = shaped(extent, HALF), shaped(2, extent, HALF)
    corner = shaped(2, 2, MARGIN, HALF)

    edge, side = shaped(2, MARGIN, tile), shaped(2, tile, MARGIN)
    edge_a, edge_b, side_a, side_b = whole(cut_body, (edge, edge, side, side), (info,), (object_field,))
    halos = both_rows(edge_a, edge_b)
    far_edge, near_edge = swapped(side_b, "cols", 1), paired(side_a)
    *ext, corner_a, corner_b = whole(
        extend_body,
        (plane, plane, strip, corner, corner),
        (info,),
        (object_field, *halos),
        unread=(near_edge,),
    )
    measured, rolled = prepare(positions, intensity, probe, order, corner_a)
    far_corner = swapped(corner_b, "cols", 1)
    sides = near_edge, paired(corner_a), far_edge, far_corner
    parts = gradient(True, info, positions, counts, ext, sides, measured, rolled, tables)
    total_a, halos_a, total_b, halos_b = summed(info, extent // 2, *parts)
    near_ext = whole(update_near_body, (plane, plane), (info,), (*ext[:2], total_a, *halos_a))
    far_ext = whole(update_far_body, (strip,), (info,), (ext[2], total_b, *halos_b))
    ext = (*near_ext, *far_ext)
    sides = paired(ext[0]), paired(ext[1]), swapped(ext[2], "cols", 1)
    parts = gradient(False, info, positions, counts, ext, sides, measured, rolled, tables)
    total_a, halos_a, total_b, halos_b = summed(info, MARGIN, *parts)
    return whole(
        finish_body, (shaped(2, tile, tile),), (info,), (*ext, total_a, total_b, *halos_a, *halos_b)
    )[0]


def solution(mesh):
    placed = (
        P(None, "rows", "cols"),
        P(),
        P("rows", "cols", None, None),
        P("rows", "cols"),
        P("rows", "cols", None, None, None),
    )
    return jax.shard_map(
        on_device, mesh=mesh, in_specs=placed, out_specs=P(None, "rows", "cols"), check_vma=False
    )
```

```python
import functools

import jax
import jax.numpy as jnp
import numpy as np
from jax import lax
from jax.experimental import pallas as pl
from jax.experimental.pallas import tpu as pltpu
from jax.sharding import PartitionSpec as P

MARGIN = 128
HALF = 128
GROUP = 2


step_rate = 0.02
photon_unit = 0.001


def rotation_tables(length):
    half = length // 2
    index = np.arange(half, dtype=np.int64)
    angle = (index[:, None] * index[None, :] % half) * (2.0 * np.pi / half)
    norm = 1.0 / np.sqrt(length)
    cosine = np.cos(angle) * norm
    sine = np.sin(angle) * norm
    mixed = np.block([[cosine, -sine], [sine, cosine]]).astype(np.float32)
    turn = index * (2.0 * np.pi / length)
    twiddle = np.stack([np.cos(turn), -np.sin(turn)]).astype(np.float32)
    return mixed, twiddle


VMEM = pl.BlockSpec(memory_space=pltpu.VMEM)
SMEM = pl.BlockSpec(memory_space=pltpu.SMEM)
ANY = pl.BlockSpec(memory_space=pl.ANY)


def shaped(*dims):
    return jax.ShapeDtypeStruct(dims, jnp.float32)


def whole(body, outs, scalars, arrays, scratch=(), limit=16 << 20, flops=1 << 20, unread=()):
    return pl.pallas_call(
        body,
        out_shape=outs,
        in_specs=[SMEM] * len(scalars) + [VMEM] * len(arrays) + [ANY] * len(unread),
        out_specs=tuple(VMEM for _ in outs),
        scratch_shapes=scratch,
        compiler_params=pltpu.CompilerParams(vmem_limit_bytes=limit),
        cost_estimate=pl.CostEstimate(flops=flops, bytes_accessed=8 << 20, transcendentals=0),
    )(*scalars, *arrays, *unread)


def cut_body(info, tile, edge_a, edge_b, side_a, side_b):
    last = tile.shape[1] - MARGIN
    edge_a[...] = tile[:, pl.ds(pl.multiple_of((1 - info[0]) * last, 8), MARGIN), :]
    edge_b[...] = tile[:, pl.ds(pl.multiple_of(info[0] * last, 8), MARGIN), :]
    left, right = slice(0, MARGIN), slice(last, last + MARGIN)

    @pl.when(info[1] == 1)
    def _():
        side_a[...] = tile[:, :, left]
        side_b[...] = tile[:, :, right]

    @pl.when(info[1] == 0)
    def _():
        side_a[...] = tile[:, :, right]
        side_b[...] = tile[:, :, left]


def prepare_body(
    positions, intensity, probe, measured, rolled, held, wave, arrived
):
    slots, size = intensity.shape[0], probe.shape[1]
    half = size // 2
    copies = [pltpu.make_async_copy(probe, wave, arrived.at[0])]
    for block in range(2):
        columns = intensity.at[:, :, pl.ds(half * block, half)]
        copies.append(pltpu.make_async_copy(columns, held.at[block], arrived.at[1 + block]))
    for copy in copies:
        copy.start()
    copies[0].wait()

    def turn(slot, carry):
        shift = lax.rem(positions[0, 0, slot, 1], size)
        for part in range(2):
            rolled[slot, part] = pltpu.roll(wave[part], shift, 1)
        return carry

    lax.fori_loop(0, slots, turn, 0)
    source = lax.broadcasted_iota(jnp.int32, (half, size), 0)
    target = lax.broadcasted_iota(jnp.int32, (half, size), 1)
    wanted = jnp.where(target < half, 2 * target, 2 * (target - half) + 1)
    moves = [
        jnp.where(source + half * block == wanted, 1.0, 0.0).astype(jnp.bfloat16) for block in range(2)
    ]
    for copy in copies[1:]:
        copy.wait()

    def reorder(slot, carry):
        for parity in range(2):
            moved = jnp.zeros((half, size), jnp.float32)
            for block in range(2):
                counts = held[block, slot, pl.ds(parity, half, stride=2), :]
                upper = lax.shift_right_logical(counts, 8).astype(jnp.float32).astype(jnp.bfloat16)
                lower = lax.bitwise_and(counts, 255).astype(jnp.float32).astype(jnp.bfloat16)
                high = jnp.dot(upper, moves[block], preferred_element_type=jnp.float32)
                low = jnp.dot(lower, moves[block], preferred_element_type=jnp.float32)
                moved = moved + (256.0 * high + low)
            measured[slot, parity] = moved * photon_unit
        return carry

    lax.fori_loop(0, slots, reorder, 0)


def prepare(positions, intensity, probe):
    slots, size = intensity.shape[0], probe.shape[1]
    half = size // 2
    hbm = pl.BlockSpec(memory_space=pltpu.HBM)
    return pl.pallas_call(
        prepare_body,
        out_shape=(shaped(slots, 2, half, size), shaped(slots, 2, size, size)),
        in_specs=[SMEM, hbm, hbm],
        out_specs=(VMEM, VMEM),
        scratch_shapes=[
            pltpu.VMEM((2, slots, size, half), jnp.int32),
            pltpu.VMEM((2, size, size), jnp.float32),
            pltpu.SemaphoreType.DMA((3,)),
        ],
        compiler_params=pltpu.CompilerParams(vmem_limit_bytes=16 << 20),
        cost_estimate=pl.CostEstimate(flops=slots * 2**27, bytes_accessed=8 << 20, transcendentals=0),
    )(positions, intensity, probe)


def halves(value):
    upper = value.astype(jnp.bfloat16)
    lower = (value - upper.astype(jnp.float32)).astype(jnp.bfloat16)
    return upper, lower


def times_table(value, table):
    upper, lower = halves(value)
    packed = jnp.concatenate([upper, lower, upper], axis=1)
    return jnp.dot(packed, table, preferred_element_type=jnp.float32)


def table_times(table, value):
    upper, lower = halves(value)
    packed = jnp.concatenate([upper, lower, upper], axis=0)
    return jnp.dot(table, packed, preferred_element_type=jnp.float32)


def wide(left, right):
    return jnp.concatenate([left, right], axis=1)


def tall(upper, lower):
    return jnp.concatenate([upper, lower], axis=0)


def places(odd_col):
    return 3 - 3 * odd_col, 2 - odd_col, 1 + odd_col, 3 * odd_col


def gradient_body(
    first, info, positions, counts, ext_r, ext_i, ext_b, *refs
):
    if first:
        near_edge, near_corner, far_edge, far_corner, *refs = refs
    else:
        near_r, near_i, far_strip, *refs = refs
    measured, rolled, fore_lane, fore_row, back_row, back_lane, twist_lane, twist_row, *refs = refs
    out_r, out_i, out_b, in_a, in_b, field, sums = refs
    size = rolled.shape[2]
    half = size // 2
    extent = field.shape[2]
    odd_col = info[1]
    other = 1 - odd_col
    near_at, a_at, b_at, far_at = places(odd_col)
    lanes = lax.broadcasted_iota(jnp.int32, (1, half), 1)
    sums[...] = jnp.zeros_like(sums)
    field[a_at, 0] = ext_r[...]
    field[a_at, 1] = ext_i[...]
    field[b_at] = ext_b[...]
    if first:
        upper, middle, lower = slice(0, MARGIN), slice(MARGIN, extent - MARGIN), slice(extent - MARGIN, extent)
        field[near_at, :, middle] = near_edge[other]
        field[near_at, :, upper] = near_corner[other, 0]
        field[near_at, :, lower] = near_corner[other, 1]
        field[far_at, :, middle] = far_edge[...]
        field[far_at, :, upper] = far_corner[0]
        field[far_at, :, lower] = far_corner[1]
    else:
        field[near_at, 0] = near_r[other]
        field[near_at, 1] = near_i[other]
        field[far_at] = far_strip[...]
    lane_r, lane_i = twist_lane[0], twist_lane[1]
    row_r, row_i = twist_row[0], twist_row[1]

    def enter(slot):
        rows = pl.ds(positions[0, 0, slot, 0], size)
        waves = []
        for block in range(2):
            near = lanes + half * block >= positions[0, 0, slot, 1]
            cut = slice(half * block, half * (block + 1))
            p_r, p_i = rolled[slot, 0, :, cut], rolled[slot, 1, :, cut]
            o_r = jnp.where(near, field[block, 0, rows, :], field[block + 2, 0, rows, :])
            o_i = jnp.where(near, field[block, 1, rows, :], field[block + 2, 1, rows, :])
            waves.append((p_r * o_r - p_i * o_i, p_r * o_i + p_i * o_r))
        (r0, i0), (r1, i1) = waves
        d_r, d_i = r0 - r1, i0 - i1
        return [
            wide(r0 + r1, i0 + i1),
            wide(d_r * lane_r - d_i * lane_i, d_r * lane_i + d_i * lane_r),
        ]

    def cross(pair):
        even, odd = pair
        r_all = wide(even[:, :half], odd[:, :half])
        i_all = wide(even[:, half:], odd[:, half:])
        r0, r1 = r_all[:half], r_all[half:]
        i0, i1 = i_all[:half], i_all[half:]
        d_r, d_i = r0 - r1, i0 - i1
        return [
            tall(r0 + r1, i0 + i1),
            tall(d_r * row_r - d_i * row_i, d_r * row_i + d_i * row_r),
        ]

    def scale(slot, pair):
        scaled = []
        for parity, spectrum in enumerate(pair):
            s_r, s_i = spectrum[:half], spectrum[half:]
            misfit = s_r * s_r + s_i * s_i - measured[slot, parity]
            scaled.append(tall(misfit * s_r, misfit * s_i))
        return scaled

    def cross_back(pair):
        even, odd = pair
        e_r, e_i = even[:half], even[half:]
        o_r, o_i = odd[:half], odd[half:]
        t_r = o_r * row_r + o_i * row_i
        t_i = o_i * row_r - o_r * row_i
        full_r = tall(e_r + t_r, e_r - t_r)
        full_i = tall(e_i + t_i, e_i - t_i)
        return [
            wide(full_r[:, :half], full_i[:, :half]),
            wide(full_r[:, half:], full_i[:, half:]),
        ]

    def leave(slot, pair, keep):
        rows = pl.ds(positions[0, 0, slot, 0], size)
        even, odd = pair
        e_r, e_i = even[:, :half], even[:, half:]
        o_r, o_i = odd[:, :half], odd[:, half:]
        t_r = o_r * lane_r + o_i * lane_i
        t_i = o_i * lane_r - o_r * lane_i
        outs = [(e_r + t_r, e_i + t_i), (e_r - t_r, e_i - t_i)]
        for block, (b_r, b_i) in enumerate(outs):
            place = lanes + half * block
            near = place >= positions[0, 0, slot, 1]
            far = place < positions[0, 0, slot, 1]
            if keep is not None:
                near, far = near & keep, far & keep
            cut = slice(half * block, half * (block + 1))
            p_r, p_i = rolled[slot, 0, :, cut], rolled[slot, 1, :, cut]
            terms = (p_r * b_r + p_i * b_i, p_r * b_i - p_i * b_r)
            for part, term in enumerate(terms):
                sums[block, part, rows, :] += jnp.where(near, term, 0.0)
                sums[block + 2, part, rows, :] += jnp.where(far, term, 0.0)

    def one_group(group, carry):
        slots = [GROUP * group + i for i in range(GROUP)]
        live = [None] + [slot < counts[0, 0] for slot in slots[1:]]
        pairs = [enter(slot) for slot in slots]
        pairs = [[times_table(half_, fore_lane[...]) for half_ in pair] for pair in pairs]
        pairs = [cross(pair) for pair in pairs]
        pairs = [[table_times(fore_row[...], half_) for half_ in pair] for pair in pairs]
        pairs = [scale(slot, pair) for slot, pair in zip(slots, pairs)]
        pairs = [[table_times(back_row[...], half_) for half_ in pair] for pair in pairs]
        pairs = [cross_back(pair) for pair in pairs]
        pairs = [[times_table(half_, back_lane[...]) for half_ in pair] for pair in pairs]
        for slot, pair, keep in zip(slots, pairs, live):
            leave(slot, pair, keep)
        return carry

    lax.fori_loop(0, (counts[0, 0] + GROUP - 1) // GROUP, one_group, 0)
    out_r[...] = sums[near_at, 0]
    out_i[...] = sums[near_at, 1]
    out_b[...] = sums[far_at]
    in_a[...] = sums[a_at]
    in_b[...] = sums[b_at]


def gradient(first, info, positions, counts, ext, sides, measured, rolled, tables):
    extent = ext[0].shape[0]
    plane, strip = shaped(extent, HALF), shaped(2, extent, HALF)
    return whole(
        functools.partial(gradient_body, first),
        (plane, plane, strip, strip, strip),
        (info, positions, counts),
        (*ext, *sides, measured, rolled, *tables),
        [pltpu.VMEM((4, 2, extent, HALF), jnp.float32)] * 2,
        flops=6 * 8 * 3 * 2**25,
    )


def extend_body(info, tile, halo_a, halo_b, ready, ext_r, ext_i, ext_b, corner_a, corner_b):
    size = tile.shape[1]
    odd_row, odd_col = info[0], info[1]

    def fill(cut_a, cut_b):
        above = [jnp.where(odd_row == 1, halo_a[part], halo_b[part]) for part in range(2)]
        below = [jnp.where(odd_row == 1, halo_b[part], halo_a[part]) for part in range(2)]
        targets = [ext_r, ext_i]
        for part in range(2):
            corner_a[0, part] = above[part][:, cut_a]
            corner_a[1, part] = below[part][:, cut_a]
            corner_b[0, part] = above[part][:, cut_b]
            corner_b[1, part] = below[part][:, cut_b]
            targets[part][:MARGIN, :] = above[part][:, cut_a]
            targets[part][MARGIN : MARGIN + size, :] = tile[part, :, cut_a]
            targets[part][MARGIN + size :, :] = below[part][:, cut_a]
            ext_b[part, :MARGIN] = above[part][:, cut_b]
            ext_b[part, MARGIN : MARGIN + size] = tile[part, :, cut_b]
            ext_b[part, MARGIN + size :] = below[part][:, cut_b]

    left, right = slice(0, HALF), slice(HALF, 2 * HALF)

    @pl.when(odd_col == 1)
    def _():
        fill(left, right)

    @pl.when(odd_col == 0)
    def _():
        fill(right, left)


def outgoing(odd_row, total, width, out_a, out_b):
    extent = total.shape[1]
    out_a[...] = total[:, pl.ds(pl.multiple_of((1 - odd_row) * (extent - width), 8), width), :]
    out_b[...] = total[:, pl.ds(pl.multiple_of(odd_row * (extent - width), 8), width), :]


def join_near_body(width, info, inner, near_r, near_i, total, out_a, out_b):
    other = 1 - info[1]
    total[0] = inner[0] + near_r[other]
    total[1] = inner[1] + near_i[other]
    outgoing(info[0], total, width, out_a, out_b)


def join_far_body(width, info, inner, strip, total, out_a, out_b):
    total[...] = inner[...] + strip[...]
    outgoing(info[0], total, width, out_a, out_b)


def updated(info, part, ext, total, halo_a, halo_b):
    middle = total.shape[1] // 2
    above = total[part, :middle] + jnp.where(info[0] == 1, halo_a[part], halo_b[part])
    below = total[part, middle:] + jnp.where(info[0] == 1, halo_b[part], halo_a[part])
    row = lax.broadcasted_iota(jnp.int32, (middle, HALF), 0)
    above = jnp.where((info[2] == 1) & (row < MARGIN), 0.0, above)
    below = jnp.where((info[3] == 1) & (row >= middle - MARGIN), 0.0, below)
    return tall(ext[:middle] - step_rate * above, ext[middle:] - step_rate * below)


def update_near_body(info, ext_r, ext_i, total, halo_a, halo_b, out_r, out_i):
    out_r[...] = updated(info, 0, ext_r, total, halo_a, halo_b)
    out_i[...] = updated(info, 1, ext_i, total, halo_a, halo_b)


def update_far_body(info, ext_b, total, halo_a, halo_b, out):
    for part in range(2):
        out[part] = updated(info, part, ext_b.at[part], total, halo_a, halo_b)


def finish_body(info, ext_r, ext_i, ext_b, total_a, total_b, near_a, near_b, far_a, far_b, out):
    size = out.shape[1]
    half = size // 2
    upper, lower = slice(MARGIN, MARGIN + half), slice(MARGIN + half, MARGIN + size)

    def settle(cut, ext, total, halo_a, halo_b):
        for part in range(2):
            above = total[part, upper] + jnp.where(info[0] == 1, halo_a[part], halo_b[part])
            below = total[part, lower] + jnp.where(info[0] == 1, halo_b[part], halo_a[part])
            out[part, :half, cut] = ext[part][upper] - step_rate * above
            out[part, half:, cut] = ext[part][lower] - step_rate * below

    def place(cut_a, cut_b):
        settle(cut_a, [ext_r, ext_i], total_a, near_a, near_b)
        settle(cut_b, [ext_b.at[0], ext_b.at[1]], total_b, far_a, far_b)

    left, right = slice(0, HALF), slice(HALF, 2 * HALF)

    @pl.when(info[1] == 1)
    def _():
        place(left, right)

    @pl.when(info[1] == 0)
    def _():
        place(right, left)


def constants(size):
    half = size // 2
    mixed, twiddle = rotation_tables(size)
    upper = mixed.astype(jnp.bfloat16)
    lower = (mixed - upper.astype(np.float32)).astype(jnp.bfloat16)
    fore_lane = jnp.asarray(np.concatenate([upper, upper, lower], axis=0))
    back_row = jnp.asarray(np.concatenate([upper, upper, lower], axis=1))
    fore_row = jnp.asarray(np.concatenate([upper.T, upper.T, lower.T], axis=1))
    back_lane = jnp.asarray(np.concatenate([upper.T, upper.T, lower.T], axis=0))
    twist_lane = jnp.asarray(twiddle.reshape(2, 1, half))
    twist_row = jnp.asarray(np.ascontiguousarray(np.broadcast_to(twiddle[:, :, None], (2, half, size))))
    return fore_lane, fore_row, back_row, back_lane, twist_lane, twist_row


def swapped(value, axis, first):
    count = lax.axis_size(axis)
    route = []
    for i in range(first, count - 1, 2):
        route += [(i, i + 1), (i + 1, i)]
    return lax.ppermute(value, axis, route)


def paired(value):
    groups = [[i, i + 1] for i in range(0, lax.axis_size("cols"), 2)]
    return lax.all_gather(value, "cols", axis_index_groups=groups)


def both_rows(edge_a, edge_b):
    return swapped(edge_a, "rows", 0), swapped(edge_b, "rows", 1)


def summed(info, width, out_r, out_i, out_b, in_a, in_b):
    extent = in_a.shape[1]
    strip, piece = shaped(2, extent, HALF), shaped(2, width, HALF)
    far = swapped(out_b, "cols", 1)
    near = paired(out_r), paired(out_i)
    total_a, *edges = whole(functools.partial(join_near_body, width), (strip, piece, piece), (info,), (in_a, *near))
    halos_a = both_rows(*edges)
    total_b, *edges = whole(functools.partial(join_far_body, width), (strip, piece, piece), (info,), (in_b, far))
    halos_b = both_rows(*edges)
    return total_a, halos_a, total_b, halos_b


def on_device(object_field, probe, positions, counts, intensity):
    size = probe.shape[1]
    tile = object_field.shape[1]
    extent = tile + 2 * MARGIN
    row, col = lax.axis_index("rows"), lax.axis_index("cols")
    last = lax.axis_size("rows") - 1
    info = jnp.stack([row % 2, col % 2, row == 0, row == last]).astype(jnp.int32)
    tables = constants(size)
    intensity = intensity[0, 0]
    plane, strip = shaped(extent, HALF), shaped(2, extent, HALF)
    corner = shaped(2, 2, MARGIN, HALF)

    edge, side = shaped(2, MARGIN, tile), shaped(2, tile, MARGIN)
    edge_a, edge_b, side_a, side_b = whole(cut_body, (edge, edge, side, side), (info,), (object_field,))
    halos = both_rows(edge_a, edge_b)
    far_edge, near_edge = swapped(side_b, "cols", 1), paired(side_a)
    measured, rolled = prepare(positions, intensity, probe)
    *ext, corner_a, corner_b = whole(
        extend_body,
        (plane, plane, strip, corner, corner),
        (info,),
        (object_field, *halos),
        unread=(measured,),
    )
    far_corner = swapped(corner_b, "cols", 1)
    sides = near_edge, paired(corner_a), far_edge, far_corner
    parts = gradient(True, info, positions, counts, ext, sides, measured, rolled, tables)
    total_a, halos_a, total_b, halos_b = summed(info, extent // 2, *parts)
    near_ext = whole(update_near_body, (plane, plane), (info,), (*ext[:2], total_a, *halos_a))
    far_ext = whole(update_far_body, (strip,), (info,), (ext[2], total_b, *halos_b))
    ext = (*near_ext, *far_ext)
    sides = paired(ext[0]), paired(ext[1]), swapped(ext[2], "cols", 1)
    parts = gradient(False, info, positions, counts, ext, sides, measured, rolled, tables)
    total_a, halos_a, total_b, halos_b = summed(info, MARGIN, *parts)
    return whole(
        finish_body, (shaped(2, tile, tile),), (info,), (*ext, total_a, total_b, *halos_a, *halos_b)
    )[0]


def solution(mesh):
    placed = (
        P(None, "rows", "cols"),
        P(),
        P("rows", "cols", None, None),
        P("rows", "cols"),
        P("rows", "cols", None, None, None),
    )
    return jax.shard_map(
        on_device, mesh=mesh, in_specs=placed, out_specs=P(None, "rows", "cols"), check_vma=False
    )
```

```python
import functools

import jax
import jax.numpy as jnp
import numpy as np
from jax import lax
from jax.experimental import pallas as pl
from jax.experimental.pallas import tpu as pltpu
from jax.sharding import PartitionSpec as P

MARGIN = 128
HALF = 128
GROUP = 2


step_rate = 0.02
photon_unit = 0.001


def rotation_tables(length):
    half = length // 2
    index = np.arange(half, dtype=np.int64)
    angle = (index[:, None] * index[None, :] % half) * (2.0 * np.pi / half)
    norm = 1.0 / np.sqrt(length)
    cosine = np.cos(angle) * norm
    sine = np.sin(angle) * norm
    mixed = np.block([[cosine, -sine], [sine, cosine]]).astype(np.float32)
    turn = index * (2.0 * np.pi / length)
    twiddle = np.stack([np.cos(turn), -np.sin(turn)]).astype(np.float32)
    return mixed, twiddle


VMEM = pl.BlockSpec(memory_space=pltpu.VMEM)
SMEM = pl.BlockSpec(memory_space=pltpu.SMEM)
ANY = pl.BlockSpec(memory_space=pl.ANY)


def shaped(*dims):
    return jax.ShapeDtypeStruct(dims, jnp.float32)


def whole(body, outs, scalars, arrays, scratch=(), limit=16 << 20, flops=1 << 20, unread=()):
    return pl.pallas_call(
        body,
        out_shape=outs,
        in_specs=[SMEM] * len(scalars) + [VMEM] * len(arrays) + [ANY] * len(unread),
        out_specs=tuple(VMEM for _ in outs),
        scratch_shapes=scratch,
        compiler_params=pltpu.CompilerParams(vmem_limit_bytes=limit),
        cost_estimate=pl.CostEstimate(flops=flops, bytes_accessed=8 << 20, transcendentals=0),
    )(*scalars, *arrays, *unread)


def cut_body(info, tile, edge_a, edge_b, side_a, side_b):
    last = tile.shape[1] - MARGIN
    edge_a[...] = tile[:, pl.ds(pl.multiple_of((1 - info[0]) * last, 8), MARGIN), :]
    edge_b[...] = tile[:, pl.ds(pl.multiple_of(info[0] * last, 8), MARGIN), :]
    left, right = slice(0, MARGIN), slice(last, last + MARGIN)

    @pl.when(info[1] == 1)
    def _():
        side_a[...] = tile[:, :, left]
        side_b[...] = tile[:, :, right]

    @pl.when(info[1] == 0)
    def _():
        side_a[...] = tile[:, :, right]
        side_b[...] = tile[:, :, left]


def prepare_body(
    positions, intensity, probe, measured, rolled, held, wave, arrived
):
    slots, size = intensity.shape[0], probe.shape[1]
    half = size // 2
    copies = [pltpu.make_async_copy(probe, wave, arrived.at[0])]
    for block in range(2):
        columns = intensity.at[:, :, pl.ds(half * block, half)]
        copies.append(pltpu.make_async_copy(columns, held.at[block], arrived.at[1 + block]))
    for copy in copies:
        copy.start()
    copies[0].wait()

    def turn(slot, carry):
        shift = lax.rem(positions[0, 0, slot, 1], size)
        for part in range(2):
            rolled[slot, part] = pltpu.roll(wave[part], shift, 1)
        return carry

    lax.fori_loop(0, slots, turn, 0)
    source = lax.broadcasted_iota(jnp.int32, (size, size), 0)
    target = lax.broadcasted_iota(jnp.int32, (size, size), 1)
    wanted = jnp.where(target < half, 2 * target, 2 * (target - half) + 1)
    moves = jnp.where(source == wanted, 1.0, 0.0).astype(jnp.bfloat16)
    for copy in copies[1:]:
        copy.wait()

    def reorder(slot, carry):
        rows = [
            wide(*[held[block, slot, pl.ds(parity, half, stride=2), :] for block in range(2)])
            for parity in range(2)
        ]
        counts = tall(*rows)
        upper = lax.shift_right_logical(counts, 8).astype(jnp.float32).astype(jnp.bfloat16)
        lower = lax.bitwise_and(counts, 255).astype(jnp.float32).astype(jnp.bfloat16)
        moved = jnp.dot(tall(upper, lower), moves, preferred_element_type=jnp.float32)
        moved = (256.0 * moved[:size] + moved[size:]) * photon_unit
        measured[slot, 0] = moved[:half]
        measured[slot, 1] = moved[half:]
        return carry

    lax.fori_loop(0, slots, reorder, 0)


def prepare(positions, intensity, probe):
    slots, size = intensity.shape[0], probe.shape[1]
    half = size // 2
    hbm = pl.BlockSpec(memory_space=pltpu.HBM)
    return pl.pallas_call(
        prepare_body,
        out_shape=(shaped(slots, 2, half, size), shaped(slots, 2, size, size)),
        in_specs=[SMEM, hbm, hbm],
        out_specs=(VMEM, VMEM),
        scratch_shapes=[
            pltpu.VMEM((2, slots, size, half), jnp.int32),
            pltpu.VMEM((2, size, size), jnp.float32),
            pltpu.SemaphoreType.DMA((3,)),
        ],
        compiler_params=pltpu.CompilerParams(vmem_limit_bytes=16 << 20),
        cost_estimate=pl.CostEstimate(flops=slots * 2**27, bytes_accessed=8 << 20, transcendentals=0),
    )(positions, intensity, probe)


def halves(value):
    upper = value.astype(jnp.bfloat16)
    lower = (value - upper.astype(jnp.float32)).astype(jnp.bfloat16)
    return upper, lower


def times_table(value, table):
    upper, lower = halves(value)
    packed = jnp.concatenate([upper, lower, upper], axis=1)
    return jnp.dot(packed, table, preferred_element_type=jnp.float32)


def table_times(table, value):
    upper, lower = halves(value)
    packed = jnp.concatenate([upper, lower, upper], axis=0)
    return jnp.dot(table, packed, preferred_element_type=jnp.float32)


def wide(left, right):
    return jnp.concatenate([left, right], axis=1)


def tall(upper, lower):
    return jnp.concatenate([upper, lower], axis=0)


def places(odd_col):
    return 3 - 3 * odd_col, 2 - odd_col, 1 + odd_col, 3 * odd_col


def gradient_body(
    first, info, positions, counts, ext_r, ext_i, ext_b, *refs
):
    if first:
        near_edge, near_corner, far_edge, far_corner, *refs = refs
    else:
        near_r, near_i, far_strip, *refs = refs
    measured, rolled, fore_lane, fore_row, back_row, back_lane, twist_lane, twist_row, *refs = refs
    out_r, out_i, out_b, in_a, in_b, field, sums = refs
    size = rolled.shape[2]
    half = size // 2
    extent = field.shape[2]
    odd_col = info[1]
    other = 1 - odd_col
    near_at, a_at, b_at, far_at = places(odd_col)
    lanes = lax.broadcasted_iota(jnp.int32, (1, half), 1)
    sums[...] = jnp.zeros_like(sums)
    field[a_at, 0] = ext_r[...]
    field[a_at, 1] = ext_i[...]
    field[b_at] = ext_b[...]
    if first:
        upper, middle, lower = slice(0, MARGIN), slice(MARGIN, extent - MARGIN), slice(extent - MARGIN, extent)
        field[near_at, :, middle] = near_edge[other]
        field[near_at, :, upper] = near_corner[other, 0]
        field[near_at, :, lower] = near_corner[other, 1]
        field[far_at, :, middle] = far_edge[...]
        field[far_at, :, upper] = far_corner[0]
        field[far_at, :, lower] = far_corner[1]
    else:
        field[near_at, 0] = near_r[other]
        field[near_at, 1] = near_i[other]
        field[far_at] = far_strip[...]
    lane_r, lane_i = twist_lane[0], twist_lane[1]
    row_r, row_i = twist_row[0], twist_row[1]

    def enter(slot):
        rows = pl.ds(jnp.clip(positions[0, 0, slot, 0], 0, size), size)
        waves = []
        for block in range(2):
            near = lanes + half * block >= positions[0, 0, slot, 1]
            cut = slice(half * block, half * (block + 1))
            p_r, p_i = rolled[slot, 0, :, cut], rolled[slot, 1, :, cut]
            o_r = jnp.where(near, field[block, 0, rows, :], field[block + 2, 0, rows, :])
            o_i = jnp.where(near, field[block, 1, rows, :], field[block + 2, 1, rows, :])
            waves.append((p_r * o_r - p_i * o_i, p_r * o_i + p_i * o_r))
        (r0, i0), (r1, i1) = waves
        d_r, d_i = r0 - r1, i0 - i1
        return [
            wide(r0 + r1, i0 + i1),
            wide(d_r * lane_r - d_i * lane_i, d_r * lane_i + d_i * lane_r),
        ]

    def cross(pair):
        even, odd = pair
        r_all = wide(even[:, :half], odd[:, :half])
        i_all = wide(even[:, half:], odd[:, half:])
        r0, r1 = r_all[:half], r_all[half:]
        i0, i1 = i_all[:half], i_all[half:]
        d_r, d_i = r0 - r1, i0 - i1
        return [
            tall(r0 + r1, i0 + i1),
            tall(d_r * row_r - d_i * row_i, d_r * row_i + d_i * row_r),
        ]

    def scale(slot, pair):
        scaled = []
        for parity, spectrum in enumerate(pair):
            s_r, s_i = spectrum[:half], spectrum[half:]
            misfit = s_r * s_r + s_i * s_i - measured[slot, parity]
            scaled.append(tall(misfit * s_r, misfit * s_i))
        return scaled

    def cross_back(pair):
        even, odd = pair
        e_r, e_i = even[:half], even[half:]
        o_r, o_i = odd[:half], odd[half:]
        t_r = o_r * row_r + o_i * row_i
        t_i = o_i * row_r - o_r * row_i
        full_r = tall(e_r + t_r, e_r - t_r)
        full_i = tall(e_i + t_i, e_i - t_i)
        return [
            wide(full_r[:, :half], full_i[:, :half]),
            wide(full_r[:, half:], full_i[:, half:]),
        ]

    def leave(slot, pair, keep):
        rows = pl.ds(jnp.clip(positions[0, 0, slot, 0], 0, size), size)
        even, odd = pair
        e_r, e_i = even[:, :half], even[:, half:]
        o_r, o_i = odd[:, :half], odd[:, half:]
        t_r = o_r * lane_r + o_i * lane_i
        t_i = o_i * lane_r - o_r * lane_i
        outs = [(e_r + t_r, e_i + t_i), (e_r - t_r, e_i - t_i)]
        for block, (b_r, b_i) in enumerate(outs):
            place = lanes + half * block
            near = place >= positions[0, 0, slot, 1]
            far = place < positions[0, 0, slot, 1]
            if keep is not None:
                near, far = near & keep, far & keep
            cut = slice(half * block, half * (block + 1))
            p_r, p_i = rolled[slot, 0, :, cut], rolled[slot, 1, :, cut]
            terms = (p_r * b_r + p_i * b_i, p_r * b_i - p_i * b_r)
            for part, term in enumerate(terms):
                sums[block, part, rows, :] += jnp.where(near, term, 0.0)
                sums[block + 2, part, rows, :] += jnp.where(far, term, 0.0)

    def one_group(group, carry):
        slots = [GROUP * group + i for i in range(GROUP)]
        live = [None] + [slot < counts[0, 0] for slot in slots[1:]]
        pairs = [enter(slot) for slot in slots]
        pairs = [[times_table(half_, fore_lane[...]) for half_ in pair] for pair in pairs]
        pairs = [cross(pair) for pair in pairs]
        pairs = [[table_times(fore_row[...], half_) for half_ in pair] for pair in pairs]
        pairs = [scale(slot, pair) for slot, pair in zip(slots, pairs)]
        pairs = [[table_times(back_row[...], half_) for half_ in pair] for pair in pairs]
        pairs = [cross_back(pair) for pair in pairs]
        pairs = [[times_table(half_, back_lane[...]) for half_ in pair] for pair in pairs]
        for slot, pair, keep in zip(slots, pairs, live):
            leave(slot, pair, keep)
        return carry

    lax.fori_loop(0, (counts[0, 0] + GROUP - 1) // GROUP, one_group, 0)
    out_r[...] = sums[near_at, 0]
    out_i[...] = sums[near_at, 1]
    out_b[...] = sums[far_at]
    in_a[...] = sums[a_at]
    in_b[...] = sums[b_at]


def gradient(first, info, positions, counts, ext, sides, measured, rolled, tables):
    extent = ext[0].shape[0]
    plane, strip = shaped(extent, HALF), shaped(2, extent, HALF)
    return whole(
        functools.partial(gradient_body, first),
        (plane, plane, strip, strip, strip),
        (info, positions, counts),
        (*ext, *sides, measured, rolled, *tables),
        [pltpu.VMEM((4, 2, extent, HALF), jnp.float32)] * 2,
        flops=6 * 8 * 3 * 2**25,
    )


def extend_body(info, tile, halo_a, halo_b, ready, ext_r, ext_i, ext_b, corner_a, corner_b):
    size = tile.shape[1]
    odd_row, odd_col = info[0], info[1]

    def fill(cut_a, cut_b):
        above = [jnp.where(odd_row == 1, halo_a[part], halo_b[part]) for part in range(2)]
        below = [jnp.where(odd_row == 1, halo_b[part], halo_a[part]) for part in range(2)]
        targets = [ext_r, ext_i]
        for part in range(2):
            corner_a[0, part] = above[part][:, cut_a]
            corner_a[1, part] = below[part][:, cut_a]
            corner_b[0, part] = above[part][:, cut_b]
            corner_b[1, part] = below[part][:, cut_b]
            targets[part][:MARGIN, :] = above[part][:, cut_a]
            targets[part][MARGIN : MARGIN + size, :] = tile[part, :, cut_a]
            targets[part][MARGIN + size :, :] = below[part][:, cut_a]
            ext_b[part, :MARGIN] = above[part][:, cut_b]
            ext_b[part, MARGIN : MARGIN + size] = tile[part, :, cut_b]
            ext_b[part, MARGIN + size :] = below[part][:, cut_b]

    left, right = slice(0, HALF), slice(HALF, 2 * HALF)

    @pl.when(odd_col == 1)
    def _():
        fill(left, right)

    @pl.when(odd_col == 0)
    def _():
        fill(right, left)


def outgoing(odd_row, total, width, out_a, out_b):
    extent = total.shape[1]
    out_a[...] = total[:, pl.ds(pl.multiple_of((1 - odd_row) * (extent - width), 8), width), :]
    out_b[...] = total[:, pl.ds(pl.multiple_of(odd_row * (extent - width), 8), width), :]


def join_near_body(width, info, inner, near_r, near_i, total, out_a, out_b):
    other = 1 - info[1]
    total[0] = inner[0] + near_r[other]
    total[1] = inner[1] + near_i[other]
    outgoing(info[0], total, width, out_a, out_b)


def join_far_body(width, info, inner, strip, total, out_a, out_b):
    total[...] = inner[...] + strip[...]
    outgoing(info[0], total, width, out_a, out_b)


def updated(info, part, ext, total, halo_a, halo_b):
    middle = total.shape[1] // 2
    above = total[part, :middle] + jnp.where(info[0] == 1, halo_a[part], halo_b[part])
    below = total[part, middle:] + jnp.where(info[0] == 1, halo_b[part], halo_a[part])
    row = lax.broadcasted_iota(jnp.int32, (middle, HALF), 0)
    above = jnp.where((info[2] == 1) & (row < MARGIN), 0.0, above)
    below = jnp.where((info[3] == 1) & (row >= middle - MARGIN), 0.0, below)
    return tall(ext[:middle] - step_rate * above, ext[middle:] - step_rate * below)


def update_near_body(info, ext_r, ext_i, total, halo_a, halo_b, out_r, out_i):
    out_r[...] = updated(info, 0, ext_r, total, halo_a, halo_b)
    out_i[...] = updated(info, 1, ext_i, total, halo_a, halo_b)


def update_far_body(info, ext_b, total, halo_a, halo_b, out):
    for part in range(2):
        out[part] = updated(info, part, ext_b.at[part], total, halo_a, halo_b)


def finish_body(
    info, ext_r, ext_i, ext_b, total_a, total_b, near_a, near_b, far_a, far_b, out, ready, sent
):
    size = ready.shape[1]
    half = size // 2
    upper, lower = slice(MARGIN, MARGIN + half), slice(MARGIN + half, MARGIN + size)
    copies = [pltpu.make_async_copy(ready.at[part], out.at[part], sent.at[part]) for part in range(2)]

    def settle(part, cut, ext, total, halo_a, halo_b):
        above = total[part, upper] + jnp.where(info[0] == 1, halo_a[part], halo_b[part])
        below = total[part, lower] + jnp.where(info[0] == 1, halo_b[part], halo_a[part])
        ready[part, :half, cut] = ext[upper] - step_rate * above
        ready[part, half:, cut] = ext[lower] - step_rate * below

    def place(part, cut_a, cut_b):
        settle(part, cut_a, [ext_r, ext_i][part], total_a, near_a, near_b)
        settle(part, cut_b, ext_b.at[part], total_b, far_a, far_b)

    left, right = slice(0, HALF), slice(HALF, 2 * HALF)
    for part in range(2):

        @pl.when(info[1] == 1)
        def _():
            place(part, left, right)

        @pl.when(info[1] == 0)
        def _():
            place(part, right, left)

        copies[part].start()
    for copy in copies:
        copy.wait()


def finished(info, tile, arrays):
    whole_tile = shaped(2, tile, tile)
    return pl.pallas_call(
        finish_body,
        out_shape=whole_tile,
        in_specs=[SMEM] + [VMEM] * len(arrays),
        out_specs=ANY,
        scratch_shapes=[pltpu.VMEM(whole_tile.shape, jnp.float32), pltpu.SemaphoreType.DMA((2,))],
        compiler_params=pltpu.CompilerParams(vmem_limit_bytes=16 << 20),
        cost_estimate=pl.CostEstimate(flops=1 << 20, bytes_accessed=4 << 20, transcendentals=0),
    )(info, *arrays)


def constants(size):
    half = size // 2
    mixed, twiddle = rotation_tables(size)
    upper = mixed.astype(jnp.bfloat16)
    lower = (mixed - upper.astype(np.float32)).astype(jnp.bfloat16)
    fore_lane = jnp.asarray(np.concatenate([upper, upper, lower], axis=0))
    back_row = jnp.asarray(np.concatenate([upper, upper, lower], axis=1))
    fore_row = jnp.asarray(np.concatenate([upper.T, upper.T, lower.T], axis=1))
    back_lane = jnp.asarray(np.concatenate([upper.T, upper.T, lower.T], axis=0))
    twist_lane = jnp.asarray(twiddle.reshape(2, 1, half))
    twist_row = jnp.asarray(np.ascontiguousarray(np.broadcast_to(twiddle[:, :, None], (2, half, size))))
    return fore_lane, fore_row, back_row, back_lane, twist_lane, twist_row


def swapped(value, axis, first):
    count = lax.axis_size(axis)
    route = []
    for i in range(first, count - 1, 2):
        route += [(i, i + 1), (i + 1, i)]
    return lax.ppermute(value, axis, route)


def paired(value):
    groups = [[i, i + 1] for i in range(0, lax.axis_size("cols"), 2)]
    return lax.all_gather(value, "cols", axis_index_groups=groups)


def both_rows(edge_a, edge_b):
    return swapped(edge_a, "rows", 0), swapped(edge_b, "rows", 1)


def summed(info, width, out_r, out_i, out_b, in_a, in_b):
    extent = in_a.shape[1]
    strip, piece = shaped(2, extent, HALF), shaped(2, width, HALF)
    far = swapped(out_b, "cols", 1)
    near = paired(out_r), paired(out_i)
    total_a, *edges = whole(functools.partial(join_near_body, width), (strip, piece, piece), (info,), (in_a, *near))
    halos_a = both_rows(*edges)
    total_b, *edges = whole(functools.partial(join_far_body, width), (strip, piece, piece), (info,), (in_b, far))
    halos_b = both_rows(*edges)
    return total_a, halos_a, total_b, halos_b


def on_device(object_field, probe, positions, counts, intensity):
    size = probe.shape[1]
    tile = object_field.shape[1]
    extent = tile + 2 * MARGIN
    row, col = lax.axis_index("rows"), lax.axis_index("cols")
    last = lax.axis_size("rows") - 1
    info = jnp.stack([row % 2, col % 2, row == 0, row == last]).astype(jnp.int32)
    tables = constants(size)
    intensity = intensity[0, 0]
    plane, strip = shaped(extent, HALF), shaped(2, extent, HALF)
    corner = shaped(2, 2, MARGIN, HALF)

    edge, side = shaped(2, MARGIN, tile), shaped(2, tile, MARGIN)
    edge_a, edge_b, side_a, side_b = whole(cut_body, (edge, edge, side, side), (info,), (object_field,))
    halos = both_rows(edge_a, edge_b)
    far_edge, near_edge = swapped(side_b, "cols", 1), paired(side_a)
    measured, rolled = prepare(positions, intensity, probe)
    *ext, corner_a, corner_b = whole(
        extend_body,
        (plane, plane, strip, corner, corner),
        (info,),
        (object_field, *halos),
        unread=(measured,),
    )
    far_corner = swapped(corner_b, "cols", 1)
    sides = near_edge, paired(corner_a), far_edge, far_corner
    parts = gradient(True, info, positions, counts, ext, sides, measured, rolled, tables)
    total_a, halos_a, total_b, halos_b = summed(info, extent // 2, *parts)
    near_ext = whole(update_near_body, (plane, plane), (info,), (*ext[:2], total_a, *halos_a))
    far_ext = whole(update_far_body, (strip,), (info,), (ext[2], total_b, *halos_b))
    ext = (*near_ext, *far_ext)
    sides = paired(ext[0]), paired(ext[1]), swapped(ext[2], "cols", 1)
    parts = gradient(False, info, positions, counts, ext, sides, measured, rolled, tables)
    total_a, halos_a, total_b, halos_b = summed(info, MARGIN, *parts)
    return finished(info, tile, (*ext, total_a, total_b, *halos_a, *halos_b))


def solution(mesh):
    placed = (
        P(None, "rows", "cols"),
        P(),
        P("rows", "cols", None, None),
        P("rows", "cols"),
        P("rows", "cols", None, None, None),
    )
    return jax.shard_map(
        on_device, mesh=mesh, in_specs=placed, out_specs=P(None, "rows", "cols"), check_vma=False
    )
```

```python
import functools

import jax
import jax.numpy as jnp
import numpy as np
from jax import lax
from jax.experimental import pallas as pl
from jax.experimental.pallas import tpu as pltpu
from jax.sharding import PartitionSpec as P

MARGIN = 128
HALF = 128
GROUP = 2


step_rate = 0.02
photon_unit = 0.001


def rotation_tables(length):
    half = length // 2
    index = np.arange(half, dtype=np.int64)
    angle = (index[:, None] * index[None, :] % half) * (2.0 * np.pi / half)
    norm = 1.0 / np.sqrt(length)
    cosine = np.cos(angle) * norm
    sine = np.sin(angle) * norm
    mixed = np.block([[cosine, -sine], [sine, cosine]]).astype(np.float32)
    turn = index * (2.0 * np.pi / length)
    twiddle = np.stack([np.cos(turn), -np.sin(turn)]).astype(np.float32)
    return mixed, twiddle


VMEM = pl.BlockSpec(memory_space=pltpu.VMEM)
SMEM = pl.BlockSpec(memory_space=pltpu.SMEM)
ANY = pl.BlockSpec(memory_space=pl.ANY)


def shaped(*dims):
    return jax.ShapeDtypeStruct(dims, jnp.float32)


def whole(body, outs, scalars, arrays, scratch=(), limit=16 << 20, flops=1 << 20, unread=()):
    return pl.pallas_call(
        body,
        out_shape=outs,
        in_specs=[SMEM] * len(scalars) + [VMEM] * len(arrays) + [ANY] * len(unread),
        out_specs=tuple(VMEM for _ in outs),
        scratch_shapes=scratch,
        compiler_params=pltpu.CompilerParams(vmem_limit_bytes=limit),
        cost_estimate=pl.CostEstimate(flops=flops, bytes_accessed=8 << 20, transcendentals=0),
    )(*scalars, *arrays, *unread)


def cut_body(info, tile, edge_a, edge_b, side_a, side_b):
    last = tile.shape[1] - MARGIN
    edge_a[...] = tile[:, pl.ds(pl.multiple_of((1 - info[0]) * last, 8), MARGIN), :]
    edge_b[...] = tile[:, pl.ds(pl.multiple_of(info[0] * last, 8), MARGIN), :]
    left, right = slice(0, MARGIN), slice(last, last + MARGIN)

    @pl.when(info[1] == 1)
    def _():
        side_a[...] = tile[:, :, left]
        side_b[...] = tile[:, :, right]

    @pl.when(info[1] == 0)
    def _():
        side_a[...] = tile[:, :, right]
        side_b[...] = tile[:, :, left]


def prepare_body(
    positions, intensity, probe, measured, rolled, held, wave, arrived
):
    slots, size = intensity.shape[0], probe.shape[1]
    half = size // 2
    copies = [pltpu.make_async_copy(probe, wave, arrived.at[0])]
    for block in range(2):
        columns = intensity.at[:, :, pl.ds(half * block, half)]
        copies.append(pltpu.make_async_copy(columns, held.at[block], arrived.at[1 + block]))
    for copy in copies:
        copy.start()
    copies[0].wait()

    def turn(slot, carry):
        shift = lax.rem(positions[0, 0, slot, 1], size)
        for part in range(2):
            rolled[slot, part] = pltpu.roll(wave[part], shift, 1)
        return carry

    lax.fori_loop(0, slots, turn, 0)
    source = lax.broadcasted_iota(jnp.int32, (size, size), 0)
    target = lax.broadcasted_iota(jnp.int32, (size, size), 1)
    wanted = jnp.where(target < half, 2 * target, 2 * (target - half) + 1)
    moves = jnp.where(source == wanted, 1.0, 0.0).astype(jnp.bfloat16)
    for copy in copies[1:]:
        copy.wait()

    def reorder(slot, carry):
        rows = [
            wide(*[held[block, slot, pl.ds(parity, half, stride=2), :] for block in range(2)])
            for parity in range(2)
        ]
        counts = tall(*rows)
        upper = lax.shift_right_logical(counts, 8).astype(jnp.float32).astype(jnp.bfloat16)
        lower = lax.bitwise_and(counts, 255).astype(jnp.float32).astype(jnp.bfloat16)
        moved = jnp.dot(tall(upper, lower), moves, preferred_element_type=jnp.float32)
        moved = (256.0 * moved[:size] + moved[size:]) * photon_unit
        measured[slot, 0] = moved[:half]
        measured[slot, 1] = moved[half:]
        return carry

    lax.fori_loop(0, slots, reorder, 0)


def prepare(positions, intensity, probe):
    slots, size = intensity.shape[0], probe.shape[1]
    half = size // 2
    hbm = pl.BlockSpec(memory_space=pltpu.HBM)
    return pl.pallas_call(
        prepare_body,
        out_shape=(shaped(slots, 2, half, size), shaped(slots, 2, size, size)),
        in_specs=[SMEM, hbm, hbm],
        out_specs=(VMEM, VMEM),
        scratch_shapes=[
            pltpu.VMEM((2, slots, size, half), jnp.int32),
            pltpu.VMEM((2, size, size), jnp.float32),
            pltpu.SemaphoreType.DMA((3,)),
        ],
        compiler_params=pltpu.CompilerParams(vmem_limit_bytes=16 << 20),
        cost_estimate=pl.CostEstimate(flops=slots * 2**27, bytes_accessed=8 << 20, transcendentals=0),
    )(positions, intensity, probe)


def halves(value):
    upper = value.astype(jnp.bfloat16)
    lower = (value - upper.astype(jnp.float32)).astype(jnp.bfloat16)
    return upper, lower


def times_table(value, table):
    upper, lower = halves(value)
    packed = jnp.concatenate([upper, lower, upper], axis=1)
    return jnp.dot(packed, table, preferred_element_type=jnp.float32)


def table_times(table, value):
    upper, lower = halves(value)
    packed = jnp.concatenate([upper, lower, upper], axis=0)
    return jnp.dot(table, packed, preferred_element_type=jnp.float32)


def wide(left, right):
    return jnp.concatenate([left, right], axis=1)


def tall(upper, lower):
    return jnp.concatenate([upper, lower], axis=0)


def places(odd_col):
    return 3 - 3 * odd_col, 2 - odd_col, 1 + odd_col, 3 * odd_col


def gradient_body(
    first, info, positions, counts, ext_r, ext_i, ext_b, *refs
):
    if first:
        near_edge, near_corner, far_edge, far_corner, *refs = refs
    else:
        near_r, near_i, far_strip, *refs = refs
    measured, rolled, fore_lane, fore_row, back_row, back_lane, twist_lane, twist_row, *refs = refs
    out_r, out_i, out_b, in_a, in_b, field, sums = refs
    size = rolled.shape[2]
    half = size // 2
    extent = field.shape[2]
    odd_col = info[1]
    other = 1 - odd_col
    near_at, a_at, b_at, far_at = places(odd_col)
    lanes = lax.broadcasted_iota(jnp.int32, (1, half), 1)
    sums[...] = jnp.zeros_like(sums)
    field[a_at, 0] = ext_r[...]
    field[a_at, 1] = ext_i[...]
    field[b_at] = ext_b[...]
    if first:
        upper, middle, lower = slice(0, MARGIN), slice(MARGIN, extent - MARGIN), slice(extent - MARGIN, extent)
        field[near_at, :, middle] = near_edge[other]
        field[near_at, :, upper] = near_corner[other, 0]
        field[near_at, :, lower] = near_corner[other, 1]
        field[far_at, :, middle] = far_edge[...]
        field[far_at, :, upper] = far_corner[0]
        field[far_at, :, lower] = far_corner[1]
    else:
        field[near_at, 0] = near_r[other]
        field[near_at, 1] = near_i[other]
        field[far_at] = far_strip[...]
    lane_r, lane_i = twist_lane[0], twist_lane[1]
    row_r, row_i = twist_row[0], twist_row[1]

    def enter(slot):
        rows = pl.ds(jnp.clip(positions[0, 0, slot, 0], 0, size), size)
        waves = []
        for block in range(2):
            near = lanes + half * block >= positions[0, 0, slot, 1]
            cut = slice(half * block, half * (block + 1))
            p_r, p_i = rolled[slot, 0, :, cut], rolled[slot, 1, :, cut]
            o_r = jnp.where(near, field[block, 0, rows, :], field[block + 2, 0, rows, :])
            o_i = jnp.where(near, field[block, 1, rows, :], field[block + 2, 1, rows, :])
            waves.append((p_r * o_r - p_i * o_i, p_r * o_i + p_i * o_r))
        (r0, i0), (r1, i1) = waves
        d_r, d_i = r0 - r1, i0 - i1
        return [
            wide(r0 + r1, i0 + i1),
            wide(d_r * lane_r - d_i * lane_i, d_r * lane_i + d_i * lane_r),
        ]

    def cross(pair):
        even, odd = pair
        r_all = wide(even[:, :half], odd[:, :half])
        i_all = wide(even[:, half:], odd[:, half:])
        r0, r1 = r_all[:half], r_all[half:]
        i0, i1 = i_all[:half], i_all[half:]
        d_r, d_i = r0 - r1, i0 - i1
        return [
            tall(r0 + r1, i0 + i1),
            tall(d_r * row_r - d_i * row_i, d_r * row_i + d_i * row_r),
        ]

    def scale(slot, pair):
        scaled = []
        for parity, spectrum in enumerate(pair):
            s_r, s_i = spectrum[:half], spectrum[half:]
            misfit = s_r * s_r + s_i * s_i - measured[slot, parity]
            scaled.append(tall(misfit * s_r, misfit * s_i))
        return scaled

    def cross_back(pair):
        even, odd = pair
        e_r, e_i = even[:half], even[half:]
        o_r, o_i = odd[:half], odd[half:]
        t_r = o_r * row_r + o_i * row_i
        t_i = o_i * row_r - o_r * row_i
        full_r = tall(e_r + t_r, e_r - t_r)
        full_i = tall(e_i + t_i, e_i - t_i)
        return [
            wide(full_r[:, :half], full_i[:, :half]),
            wide(full_r[:, half:], full_i[:, half:]),
        ]

    def leave(slot, pair, keep):
        rows = pl.ds(jnp.clip(positions[0, 0, slot, 0], 0, size), size)
        even, odd = pair
        e_r, e_i = even[:, :half], even[:, half:]
        o_r, o_i = odd[:, :half], odd[:, half:]
        t_r = o_r * lane_r + o_i * lane_i
        t_i = o_i * lane_r - o_r * lane_i
        outs = [(e_r + t_r, e_i + t_i), (e_r - t_r, e_i - t_i)]
        for block, (b_r, b_i) in enumerate(outs):
            place = lanes + half * block
            near = place >= positions[0, 0, slot, 1]
            far = place < positions[0, 0, slot, 1]
            if keep is not None:
                near, far = near & keep, far & keep
            cut = slice(half * block, half * (block + 1))
            p_r, p_i = rolled[slot, 0, :, cut], rolled[slot, 1, :, cut]
            terms = (p_r * b_r + p_i * b_i, p_r * b_i - p_i * b_r)
            for part, term in enumerate(terms):
                sums[block, part, rows, :] += jnp.where(near, term, 0.0)
                sums[block + 2, part, rows, :] += jnp.where(far, term, 0.0)

    def one_group(group, carry):
        slots = [GROUP * group + i for i in range(GROUP)]
        live = [None] + [slot < counts[0, 0] for slot in slots[1:]]
        pairs = [enter(slot) for slot in slots]
        pairs = [[times_table(half_, fore_lane[...]) for half_ in pair] for pair in pairs]
        pairs = [cross(pair) for pair in pairs]
        pairs = [[table_times(fore_row[...], half_) for half_ in pair] for pair in pairs]
        pairs = [scale(slot, pair) for slot, pair in zip(slots, pairs)]
        pairs = [[table_times(back_row[...], half_) for half_ in pair] for pair in pairs]
        pairs = [cross_back(pair) for pair in pairs]
        pairs = [[times_table(half_, back_lane[...]) for half_ in pair] for pair in pairs]
        for slot, pair, keep in zip(slots, pairs, live):
            leave(slot, pair, keep)
        return carry

    lax.fori_loop(0, (counts[0, 0] + GROUP - 1) // GROUP, one_group, 0)
    out_r[...] = sums[near_at, 0]
    out_i[...] = sums[near_at, 1]
    out_b[...] = sums[far_at]
    in_a[...] = sums[a_at]
    in_b[...] = sums[b_at]


def gradient(first, info, positions, counts, ext, sides, measured, rolled, tables):
    extent = ext[0].shape[0]
    plane, strip = shaped(extent, HALF), shaped(2, extent, HALF)
    return whole(
        functools.partial(gradient_body, first),
        (plane, plane, strip, strip, strip),
        (info, positions, counts),
        (*ext, *sides, measured, rolled, *tables),
        [pltpu.VMEM((4, 2, extent, HALF), jnp.float32)] * 2,
        flops=6 * 8 * 3 * 2**25,
    )


def extend_body(info, tile, halo_a, halo_b, ready, ext_r, ext_i, ext_b, corner_a, corner_b):
    size = tile.shape[1]
    odd_row, odd_col = info[0], info[1]

    def fill(cut_a, cut_b):
        above = [jnp.where(odd_row == 1, halo_a[part], halo_b[part]) for part in range(2)]
        below = [jnp.where(odd_row == 1, halo_b[part], halo_a[part]) for part in range(2)]
        targets = [ext_r, ext_i]
        for part in range(2):
            corner_a[0, part] = above[part][:, cut_a]
            corner_a[1, part] = below[part][:, cut_a]
            corner_b[0, part] = above[part][:, cut_b]
            corner_b[1, part] = below[part][:, cut_b]
            targets[part][:MARGIN, :] = above[part][:, cut_a]
            targets[part][MARGIN : MARGIN + size, :] = tile[part, :, cut_a]
            targets[part][MARGIN + size :, :] = below[part][:, cut_a]
            ext_b[part, :MARGIN] = above[part][:, cut_b]
            ext_b[part, MARGIN : MARGIN + size] = tile[part, :, cut_b]
            ext_b[part, MARGIN + size :] = below[part][:, cut_b]

    left, right = slice(0, HALF), slice(HALF, 2 * HALF)

    @pl.when(odd_col == 1)
    def _():
        fill(left, right)

    @pl.when(odd_col == 0)
    def _():
        fill(right, left)


def outgoing(odd_row, total, width, out_a, out_b):
    extent = total.shape[1]
    out_a[...] = total[:, pl.ds(pl.multiple_of((1 - odd_row) * (extent - width), 8), width), :]
    out_b[...] = total[:, pl.ds(pl.multiple_of(odd_row * (extent - width), 8), width), :]


def join_near_body(width, info, inner, near_r, near_i, total, out_a, out_b):
    other = 1 - info[1]
    total[0] = inner[0] + near_r[other]
    total[1] = inner[1] + near_i[other]
    outgoing(info[0], total, width, out_a, out_b)


def join_far_body(width, info, inner, strip, earlier, total, out_a, out_b):
    total[...] = inner[...] + strip[...]
    outgoing(info[0], total, width, out_a, out_b)


def updated(info, part, ext, total, halo_a, halo_b):
    middle = total.shape[1] // 2
    above = total[part, :middle] + jnp.where(info[0] == 1, halo_a[part], halo_b[part])
    below = total[part, middle:] + jnp.where(info[0] == 1, halo_b[part], halo_a[part])
    row = lax.broadcasted_iota(jnp.int32, (middle, HALF), 0)
    above = jnp.where((info[2] == 1) & (row < MARGIN), 0.0, above)
    below = jnp.where((info[3] == 1) & (row >= middle - MARGIN), 0.0, below)
    return tall(ext[:middle] - step_rate * above, ext[middle:] - step_rate * below)


def update_near_body(info, ext_r, ext_i, total, halo_a, halo_b, out_r, out_i):
    out_r[...] = updated(info, 0, ext_r, total, halo_a, halo_b)
    out_i[...] = updated(info, 1, ext_i, total, halo_a, halo_b)


def update_far_body(info, ext_b, total, halo_a, halo_b, out):
    for part in range(2):
        out[part] = updated(info, part, ext_b.at[part], total, halo_a, halo_b)


def finish_body(
    info, ext_r, ext_i, ext_b, total_a, total_b, near_a, near_b, far_a, far_b, out, ready, sent
):
    size = ready.shape[1]
    half = size // 2
    upper, lower = slice(MARGIN, MARGIN + half), slice(MARGIN + half, MARGIN + size)
    copies = [pltpu.make_async_copy(ready.at[part], out.at[part], sent.at[part]) for part in range(2)]

    def settle(part, cut, ext, total, halo_a, halo_b):
        above = total[part, upper] + jnp.where(info[0] == 1, halo_a[part], halo_b[part])
        below = total[part, lower] + jnp.where(info[0] == 1, halo_b[part], halo_a[part])
        ready[part, :half, cut] = ext[upper] - step_rate * above
        ready[part, half:, cut] = ext[lower] - step_rate * below

    def place(part, cut_a, cut_b):
        settle(part, cut_a, [ext_r, ext_i][part], total_a, near_a, near_b)
        settle(part, cut_b, ext_b.at[part], total_b, far_a, far_b)

    left, right = slice(0, HALF), slice(HALF, 2 * HALF)
    for part in range(2):

        @pl.when(info[1] == 1)
        def _():
            place(part, left, right)

        @pl.when(info[1] == 0)
        def _():
            place(part, right, left)

        copies[part].start()
    for copy in copies:
        copy.wait()


def finished(info, tile, arrays):
    whole_tile = shaped(2, tile, tile)
    return pl.pallas_call(
        finish_body,
        out_shape=whole_tile,
        in_specs=[SMEM] + [VMEM] * len(arrays),
        out_specs=ANY,
        scratch_shapes=[pltpu.VMEM(whole_tile.shape, jnp.float32), pltpu.SemaphoreType.DMA((2,))],
        compiler_params=pltpu.CompilerParams(vmem_limit_bytes=16 << 20),
        cost_estimate=pl.CostEstimate(flops=1 << 20, bytes_accessed=4 << 20, transcendentals=0),
    )(info, *arrays)


def constants(size):
    half = size // 2
    mixed, twiddle = rotation_tables(size)
    upper = mixed.astype(jnp.bfloat16)
    lower = (mixed - upper.astype(np.float32)).astype(jnp.bfloat16)
    fore_lane = jnp.asarray(np.concatenate([upper, upper, lower], axis=0))
    back_row = jnp.asarray(np.concatenate([upper, upper, lower], axis=1))
    fore_row = jnp.asarray(np.concatenate([upper.T, upper.T, lower.T], axis=1))
    back_lane = jnp.asarray(np.concatenate([upper.T, upper.T, lower.T], axis=0))
    twist_lane = jnp.asarray(twiddle.reshape(2, 1, half))
    twist_row = jnp.asarray(np.ascontiguousarray(np.broadcast_to(twiddle[:, :, None], (2, half, size))))
    return fore_lane, fore_row, back_row, back_lane, twist_lane, twist_row


def swapped(value, axis, first):
    count = lax.axis_size(axis)
    route = []
    for i in range(first, count - 1, 2):
        route += [(i, i + 1), (i + 1, i)]
    return lax.ppermute(value, axis, route)


def paired(value):
    groups = [[i, i + 1] for i in range(0, lax.axis_size("cols"), 2)]
    return lax.all_gather(value, "cols", axis_index_groups=groups)


def both_rows(edge_a, edge_b):
    return swapped(edge_a, "rows", 0), swapped(edge_b, "rows", 1)


def summed(info, width, out_r, out_i, out_b, in_a, in_b):
    extent = in_a.shape[1]
    strip, piece = shaped(2, extent, HALF), shaped(2, width, HALF)
    far = swapped(out_b, "cols", 1)
    near = paired(out_r), paired(out_i)
    total_a, *edges = whole(functools.partial(join_near_body, width), (strip, piece, piece), (info,), (in_a, *near))
    halos_a = both_rows(*edges)
    total_b, *edges = whole(
        functools.partial(join_far_body, width),
        (strip, piece, piece),
        (info,),
        (in_b, far),
        unread=edges[:1],
    )
    halos_b = both_rows(*edges)
    return total_a, halos_a, total_b, halos_b


def on_device(object_field, probe, positions, counts, intensity):
    size = probe.shape[1]
    tile = object_field.shape[1]
    extent = tile + 2 * MARGIN
    row, col = lax.axis_index("rows"), lax.axis_index("cols")
    last = lax.axis_size("rows") - 1
    info = jnp.stack([row % 2, col % 2, row == 0, row == last]).astype(jnp.int32)
    tables = constants(size)
    intensity = intensity[0, 0]
    plane, strip = shaped(extent, HALF), shaped(2, extent, HALF)
    corner = shaped(2, 2, MARGIN, HALF)

    edge, side = shaped(2, MARGIN, tile), shaped(2, tile, MARGIN)
    edge_a, edge_b, side_a, side_b = whole(cut_body, (edge, edge, side, side), (info,), (object_field,))
    halos = both_rows(edge_a, edge_b)
    far_edge, near_edge = swapped(side_b, "cols", 1), paired(side_a)
    measured, rolled = prepare(positions, intensity, probe)
    *ext, corner_a, corner_b = whole(
        extend_body,
        (plane, plane, strip, corner, corner),
        (info,),
        (object_field, *halos),
        unread=(measured,),
    )
    far_corner = swapped(corner_b, "cols", 1)
    sides = near_edge, paired(corner_a), far_edge, far_corner
    parts = gradient(True, info, positions, counts, ext, sides, measured, rolled, tables)
    total_a, halos_a, total_b, halos_b = summed(info, extent // 2, *parts)
    near_ext = whole(update_near_body, (plane, plane), (info,), (*ext[:2], total_a, *halos_a))
    far_ext = whole(update_far_body, (strip,), (info,), (ext[2], total_b, *halos_b))
    ext = (*near_ext, *far_ext)
    sides = paired(ext[0]), paired(ext[1]), swapped(ext[2], "cols", 1)
    parts = gradient(False, info, positions, counts, ext, sides, measured, rolled, tables)
    total_a, halos_a, total_b, halos_b = summed(info, MARGIN, *parts)
    return finished(info, tile, (*ext, total_a, total_b, *halos_a, *halos_b))


def solution(mesh):
    placed = (
        P(None, "rows", "cols"),
        P(),
        P("rows", "cols", None, None),
        P("rows", "cols"),
        P("rows", "cols", None, None, None),
    )
    return jax.shard_map(
        on_device, mesh=mesh, in_specs=placed, out_specs=P(None, "rows", "cols"), check_vma=False
    )
```

```python
import functools

import jax
import jax.numpy as jnp
import numpy as np
from jax import lax
from jax.experimental import pallas as pl
from jax.experimental.pallas import tpu as pltpu
from jax.sharding import PartitionSpec as P

MARGIN = 128
HALF = 128
GROUP = 2


step_rate = 0.02
photon_unit = 0.001


def rotation_tables(length):
    half = length // 2
    index = np.arange(half, dtype=np.int64)
    angle = (index[:, None] * index[None, :] % half) * (2.0 * np.pi / half)
    norm = 1.0 / np.sqrt(length)
    cosine = np.cos(angle) * norm
    sine = np.sin(angle) * norm
    mixed = np.block([[cosine, -sine], [sine, cosine]]).astype(np.float32)
    turn = index * (2.0 * np.pi / length)
    twiddle = np.stack([np.cos(turn), -np.sin(turn)]).astype(np.float32)
    return mixed, twiddle


VMEM = pl.BlockSpec(memory_space=pltpu.VMEM)
SMEM = pl.BlockSpec(memory_space=pltpu.SMEM)
ANY = pl.BlockSpec(memory_space=pl.ANY)


def shaped(*dims):
    return jax.ShapeDtypeStruct(dims, jnp.float32)


def whole(body, outs, scalars, arrays, scratch=(), limit=16 << 20, flops=1 << 20, unread=()):
    return pl.pallas_call(
        body,
        out_shape=outs,
        in_specs=[SMEM] * len(scalars) + [VMEM] * len(arrays) + [ANY] * len(unread),
        out_specs=tuple(VMEM for _ in outs),
        scratch_shapes=scratch,
        compiler_params=pltpu.CompilerParams(vmem_limit_bytes=limit),
        cost_estimate=pl.CostEstimate(flops=flops, bytes_accessed=8 << 20, transcendentals=0),
    )(*scalars, *arrays, *unread)


def cut_body(info, tile, edge_a, edge_b, side_a, side_b):
    last = tile.shape[1] - MARGIN
    edge_a[...] = tile[:, pl.ds(pl.multiple_of((1 - info[0]) * last, 8), MARGIN), :]
    edge_b[...] = tile[:, pl.ds(pl.multiple_of(info[0] * last, 8), MARGIN), :]
    left, right = slice(0, MARGIN), slice(last, last + MARGIN)

    @pl.when(info[1] == 1)
    def _():
        side_a[...] = tile[:, :, left]
        side_b[...] = tile[:, :, right]

    @pl.when(info[1] == 0)
    def _():
        side_a[...] = tile[:, :, right]
        side_b[...] = tile[:, :, left]


def prepare_body(
    positions, intensity, probe, measured, rolled, held, arrived
):
    slots, size = intensity.shape[0], probe.shape[1]
    half = size // 2
    copies = []
    for block in range(2):
        columns = intensity.at[:, :, pl.ds(half * block, half)]
        copies.append(pltpu.make_async_copy(columns, held.at[block], arrived.at[block]))
    for copy in copies:
        copy.start()

    def turn(slot, carry):
        shift = lax.rem(positions[0, 0, slot, 1], size)
        for part in range(2):
            rolled[slot, part] = pltpu.roll(probe[part], shift, 1)
        return carry

    lax.fori_loop(0, slots, turn, 0)
    source = lax.broadcasted_iota(jnp.int32, (size, size), 0)
    target = lax.broadcasted_iota(jnp.int32, (size, size), 1)
    wanted = jnp.where(target < half, 2 * target, 2 * (target - half) + 1)
    moves = jnp.where(source == wanted, 1.0, 0.0).astype(jnp.bfloat16)
    for copy in copies:
        copy.wait()

    def reorder(slot, carry):
        rows = [
            wide(*[held[block, slot, pl.ds(parity, half, stride=2), :] for block in range(2)])
            for parity in range(2)
        ]
        counts = tall(*rows)
        upper = lax.shift_right_logical(counts, 8).astype(jnp.float32).astype(jnp.bfloat16)
        lower = lax.bitwise_and(counts, 255).astype(jnp.float32).astype(jnp.bfloat16)
        moved = jnp.dot(tall(upper, lower), moves, preferred_element_type=jnp.float32)
        moved = (256.0 * moved[:size] + moved[size:]) * photon_unit
        measured[slot, 0] = moved[:half]
        measured[slot, 1] = moved[half:]
        return carry

    lax.fori_loop(0, slots, reorder, 0)


def prepare(positions, intensity, probe):
    slots, size = intensity.shape[0], probe.shape[1]
    half = size // 2
    hbm = pl.BlockSpec(memory_space=pltpu.HBM)
    return pl.pallas_call(
        prepare_body,
        out_shape=(shaped(slots, 2, half, size), shaped(slots, 2, size, size)),
        in_specs=[SMEM, hbm, VMEM],
        out_specs=(VMEM, VMEM),
        scratch_shapes=[
            pltpu.VMEM((2, slots, size, half), jnp.int32),
            pltpu.SemaphoreType.DMA((2,)),
        ],
        compiler_params=pltpu.CompilerParams(vmem_limit_bytes=16 << 20),
        cost_estimate=pl.CostEstimate(flops=slots * 2**27, bytes_accessed=8 << 20, transcendentals=0),
    )(positions, intensity, probe)


def halves(value):
    upper = value.astype(jnp.bfloat16)
    lower = (value - upper.astype(jnp.float32)).astype(jnp.bfloat16)
    return upper, lower


def times_table(value, table):
    upper, lower = halves(value)
    packed = jnp.concatenate([upper, lower, upper], axis=1)
    return jnp.dot(packed, table, preferred_element_type=jnp.float32)


def table_times(table, value):
    upper, lower = halves(value)
    packed = jnp.concatenate([upper, lower, upper], axis=0)
    return jnp.dot(table, packed, preferred_element_type=jnp.float32)


def wide(left, right):
    return jnp.concatenate([left, right], axis=1)


def tall(upper, lower):
    return jnp.concatenate([upper, lower], axis=0)


def places(odd_col):
    return 3 - 3 * odd_col, 2 - odd_col, 1 + odd_col, 3 * odd_col


def gradient_body(
    first, info, positions, counts, ext_r, ext_i, ext_b, *refs
):
    if first:
        near_edge, near_corner, far_edge, far_corner, *refs = refs
    else:
        near_r, near_i, far_strip, *refs = refs
    measured, rolled, fore_lane, fore_row, back_row, back_lane, twist_lane, twist_row, *refs = refs
    out_r, out_i, out_b, in_a, in_b, field, sums = refs
    size = rolled.shape[2]
    half = size // 2
    extent = field.shape[2]
    odd_col = info[1]
    other = 1 - odd_col
    near_at, a_at, b_at, far_at = places(odd_col)
    lanes = lax.broadcasted_iota(jnp.int32, (1, half), 1)
    sums[...] = jnp.zeros_like(sums)
    field[a_at, 0] = ext_r[...]
    field[a_at, 1] = ext_i[...]
    field[b_at] = ext_b[...]
    if first:
        upper, middle, lower = slice(0, MARGIN), slice(MARGIN, extent - MARGIN), slice(extent - MARGIN, extent)
        field[near_at, :, middle] = near_edge[other]
        field[near_at, :, upper] = near_corner[other, 0]
        field[near_at, :, lower] = near_corner[other, 1]
        field[far_at, :, middle] = far_edge[...]
        field[far_at, :, upper] = far_corner[0]
        field[far_at, :, lower] = far_corner[1]
    else:
        field[near_at, 0] = near_r[other]
        field[near_at, 1] = near_i[other]
        field[far_at] = far_strip[...]
    lane_r, lane_i = twist_lane[0], twist_lane[1]
    row_r, row_i = twist_row[0], twist_row[1]

    def enter(slot):
        rows = pl.ds(jnp.clip(positions[0, 0, slot, 0], 0, size), size)
        waves = []
        for block in range(2):
            near = lanes + half * block >= positions[0, 0, slot, 1]
            cut = slice(half * block, half * (block + 1))
            p_r, p_i = rolled[slot, 0, :, cut], rolled[slot, 1, :, cut]
            o_r = jnp.where(near, field[block, 0, rows, :], field[block + 2, 0, rows, :])
            o_i = jnp.where(near, field[block, 1, rows, :], field[block + 2, 1, rows, :])
            waves.append((p_r * o_r - p_i * o_i, p_r * o_i + p_i * o_r))
        (r0, i0), (r1, i1) = waves
        d_r, d_i = r0 - r1, i0 - i1
        return [
            wide(r0 + r1, i0 + i1),
            wide(d_r * lane_r - d_i * lane_i, d_r * lane_i + d_i * lane_r),
        ]

    def cross(pair):
        even, odd = pair
        r_all = wide(even[:, :half], odd[:, :half])
        i_all = wide(even[:, half:], odd[:, half:])
        r0, r1 = r_all[:half], r_all[half:]
        i0, i1 = i_all[:half], i_all[half:]
        d_r, d_i = r0 - r1, i0 - i1
        return [
            tall(r0 + r1, i0 + i1),
            tall(d_r * row_r - d_i * row_i, d_r * row_i + d_i * row_r),
        ]

    def scale(slot, pair):
        scaled = []
        for parity, spectrum in enumerate(pair):
            s_r, s_i = spectrum[:half], spectrum[half:]
            misfit = s_r * s_r + s_i * s_i - measured[slot, parity]
            scaled.append(tall(misfit * s_r, misfit * s_i))
        return scaled

    def cross_back(pair):
        even, odd = pair
        e_r, e_i = even[:half], even[half:]
        o_r, o_i = odd[:half], odd[half:]
        t_r = o_r * row_r + o_i * row_i
        t_i = o_i * row_r - o_r * row_i
        full_r = tall(e_r + t_r, e_r - t_r)
        full_i = tall(e_i + t_i, e_i - t_i)
        return [
            wide(full_r[:, :half], full_i[:, :half]),
            wide(full_r[:, half:], full_i[:, half:]),
        ]

    def leave(slot, pair, keep):
        rows = pl.ds(jnp.clip(positions[0, 0, slot, 0], 0, size), size)
        even, odd = pair
        e_r, e_i = even[:, :half], even[:, half:]
        o_r, o_i = odd[:, :half], odd[:, half:]
        t_r = o_r * lane_r + o_i * lane_i
        t_i = o_i * lane_r - o_r * lane_i
        outs = [(e_r + t_r, e_i + t_i), (e_r - t_r, e_i - t_i)]
        for block, (b_r, b_i) in enumerate(outs):
            place = lanes + half * block
            near = place >= positions[0, 0, slot, 1]
            far = place < positions[0, 0, slot, 1]
            if keep is not None:
                near, far = near & keep, far & keep
            cut = slice(half * block, half * (block + 1))
            p_r, p_i = rolled[slot, 0, :, cut], rolled[slot, 1, :, cut]
            terms = (p_r * b_r + p_i * b_i, p_r * b_i - p_i * b_r)
            for part, term in enumerate(terms):
                sums[block, part, rows, :] += jnp.where(near, term, 0.0)
                sums[block + 2, part, rows, :] += jnp.where(far, term, 0.0)

    def one_group(group, carry):
        slots = [GROUP * group + i for i in range(GROUP)]
        live = [None] + [slot < counts[0, 0] for slot in slots[1:]]
        pairs = [enter(slot) for slot in slots]
        pairs = [[times_table(half_, fore_lane[...]) for half_ in pair] for pair in pairs]
        pairs = [cross(pair) for pair in pairs]
        pairs = [[table_times(fore_row[...], half_) for half_ in pair] for pair in pairs]
        pairs = [scale(slot, pair) for slot, pair in zip(slots, pairs)]
        pairs = [[table_times(back_row[...], half_) for half_ in pair] for pair in pairs]
        pairs = [cross_back(pair) for pair in pairs]
        pairs = [[times_table(half_, back_lane[...]) for half_ in pair] for pair in pairs]
        for slot, pair, keep in zip(slots, pairs, live):
            leave(slot, pair, keep)
        return carry

    lax.fori_loop(0, (counts[0, 0] + GROUP - 1) // GROUP, one_group, 0)
    out_r[...] = sums[near_at, 0]
    out_i[...] = sums[near_at, 1]
    out_b[...] = sums[far_at]
    in_a[...] = sums[a_at]
    in_b[...] = sums[b_at]


def gradient(first, info, positions, counts, ext, sides, measured, rolled, tables):
    extent = ext[0].shape[0]
    plane, strip = shaped(extent, HALF), shaped(2, extent, HALF)
    return whole(
        functools.partial(gradient_body, first),
        (plane, plane, strip, strip, strip),
        (info, positions, counts),
        (*ext, *sides, measured, rolled, *tables),
        [pltpu.VMEM((4, 2, extent, HALF), jnp.float32)] * 2,
        flops=6 * 8 * 3 * 2**25,
    )


def extend_body(info, tile, halo_a, halo_b, ready, ext_r, ext_i, ext_b, corner_a, corner_b):
    size = tile.shape[1]
    odd_row, odd_col = info[0], info[1]

    def fill(cut_a, cut_b):
        above = [jnp.where(odd_row == 1, halo_a[part], halo_b[part]) for part in range(2)]
        below = [jnp.where(odd_row == 1, halo_b[part], halo_a[part]) for part in range(2)]
        targets = [ext_r, ext_i]
        for part in range(2):
            corner_a[0, part] = above[part][:, cut_a]
            corner_a[1, part] = below[part][:, cut_a]
            corner_b[0, part] = above[part][:, cut_b]
            corner_b[1, part] = below[part][:, cut_b]
            targets[part][:MARGIN, :] = above[part][:, cut_a]
            targets[part][MARGIN : MARGIN + size, :] = tile[part, :, cut_a]
            targets[part][MARGIN + size :, :] = below[part][:, cut_a]
            ext_b[part, :MARGIN] = above[part][:, cut_b]
            ext_b[part, MARGIN : MARGIN + size] = tile[part, :, cut_b]
            ext_b[part, MARGIN + size :] = below[part][:, cut_b]

    left, right = slice(0, HALF), slice(HALF, 2 * HALF)

    @pl.when(odd_col == 1)
    def _():
        fill(left, right)

    @pl.when(odd_col == 0)
    def _():
        fill(right, left)


def outgoing(odd_row, total, width, out_a, out_b):
    extent = total.shape[1]
    out_a[...] = total[:, pl.ds(pl.multiple_of((1 - odd_row) * (extent - width), 8), width), :]
    out_b[...] = total[:, pl.ds(pl.multiple_of(odd_row * (extent - width), 8), width), :]


def join_near_body(width, info, inner, near_r, near_i, total, out_a, out_b):
    other = 1 - info[1]
    total[0] = inner[0] + near_r[other]
    total[1] = inner[1] + near_i[other]
    outgoing(info[0], total, width, out_a, out_b)


def join_far_body(width, info, inner, strip, earlier, total, out_a, out_b):
    total[...] = inner[...] + strip[...]
    outgoing(info[0], total, width, out_a, out_b)


def updated(info, part, ext, total, halo_a, halo_b):
    middle = total.shape[1] // 2
    above = total[part, :middle] + jnp.where(info[0] == 1, halo_a[part], halo_b[part])
    below = total[part, middle:] + jnp.where(info[0] == 1, halo_b[part], halo_a[part])
    row = lax.broadcasted_iota(jnp.int32, (middle, HALF), 0)
    above = jnp.where((info[2] == 1) & (row < MARGIN), 0.0, above)
    below = jnp.where((info[3] == 1) & (row >= middle - MARGIN), 0.0, below)
    return tall(ext[:middle] - step_rate * above, ext[middle:] - step_rate * below)


def update_near_body(info, ext_r, ext_i, total, halo_a, halo_b, out_r, out_i):
    out_r[...] = updated(info, 0, ext_r, total, halo_a, halo_b)
    out_i[...] = updated(info, 1, ext_i, total, halo_a, halo_b)


def update_far_body(info, ext_b, total, halo_a, halo_b, out):
    for part in range(2):
        out[part] = updated(info, part, ext_b.at[part], total, halo_a, halo_b)


def finish_body(
    info, ext_r, ext_i, ext_b, total_a, total_b, near_a, near_b, far_a, far_b, out, ready, sent
):
    size = ready.shape[1]
    half = size // 2
    upper, lower = slice(MARGIN, MARGIN + half), slice(MARGIN + half, MARGIN + size)
    copies = [pltpu.make_async_copy(ready.at[part], out.at[part], sent.at[part]) for part in range(2)]

    def settle(part, cut, ext, total, halo_a, halo_b):
        above = total[part, upper] + jnp.where(info[0] == 1, halo_a[part], halo_b[part])
        below = total[part, lower] + jnp.where(info[0] == 1, halo_b[part], halo_a[part])
        ready[part, :half, cut] = ext[upper] - step_rate * above
        ready[part, half:, cut] = ext[lower] - step_rate * below

    def place(part, cut_a, cut_b):
        settle(part, cut_a, [ext_r, ext_i][part], total_a, near_a, near_b)
        settle(part, cut_b, ext_b.at[part], total_b, far_a, far_b)

    left, right = slice(0, HALF), slice(HALF, 2 * HALF)
    for part in range(2):

        @pl.when(info[1] == 1)
        def _():
            place(part, left, right)

        @pl.when(info[1] == 0)
        def _():
            place(part, right, left)

        copies[part].start()
    for copy in copies:
        copy.wait()


def finished(info, tile, arrays):
    whole_tile = shaped(2, tile, tile)
    return pl.pallas_call(
        finish_body,
        out_shape=whole_tile,
        in_specs=[SMEM] + [VMEM] * len(arrays),
        out_specs=ANY,
        scratch_shapes=[pltpu.VMEM(whole_tile.shape, jnp.float32), pltpu.SemaphoreType.DMA((2,))],
        compiler_params=pltpu.CompilerParams(vmem_limit_bytes=16 << 20),
        cost_estimate=pl.CostEstimate(flops=1 << 20, bytes_accessed=4 << 20, transcendentals=0),
    )(info, *arrays)


def constants(size):
    half = size // 2
    mixed, twiddle = rotation_tables(size)
    upper = mixed.astype(jnp.bfloat16)
    lower = (mixed - upper.astype(np.float32)).astype(jnp.bfloat16)
    fore_lane = jnp.asarray(np.concatenate([upper, upper, lower], axis=0))
    back_row = jnp.asarray(np.concatenate([upper, upper, lower], axis=1))
    fore_row = jnp.asarray(np.concatenate([upper.T, upper.T, lower.T], axis=1))
    back_lane = jnp.asarray(np.concatenate([upper.T, upper.T, lower.T], axis=0))
    twist_lane = jnp.asarray(twiddle.reshape(2, 1, half))
    twist_row = jnp.asarray(np.ascontiguousarray(np.broadcast_to(twiddle[:, :, None], (2, half, size))))
    return fore_lane, fore_row, back_row, back_lane, twist_lane, twist_row


def swapped(value, axis, first):
    count = lax.axis_size(axis)
    route = []
    for i in range(first, count - 1, 2):
        route += [(i, i + 1), (i + 1, i)]
    return lax.ppermute(value, axis, route)


def paired(value):
    groups = [[i, i + 1] for i in range(0, lax.axis_size("cols"), 2)]
    return lax.all_gather(value, "cols", axis_index_groups=groups)


def both_rows(edge_a, edge_b):
    return swapped(edge_a, "rows", 0), swapped(edge_b, "rows", 1)


def summed(info, width, out_r, out_i, out_b, in_a, in_b):
    extent = in_a.shape[1]
    strip, piece = shaped(2, extent, HALF), shaped(2, width, HALF)
    far = swapped(out_b, "cols", 1)
    near = paired(out_r), paired(out_i)
    total_a, *edges = whole(functools.partial(join_near_body, width), (strip, piece, piece), (info,), (in_a, *near))
    halos_a = both_rows(*edges)
    total_b, *edges = whole(
        functools.partial(join_far_body, width),
        (strip, piece, piece),
        (info,),
        (in_b, far),
        unread=edges[:1],
    )
    halos_b = both_rows(*edges)
    return total_a, halos_a, total_b, halos_b


def on_device(object_field, probe, positions, counts, intensity):
    size = probe.shape[1]
    tile = object_field.shape[1]
    extent = tile + 2 * MARGIN
    row, col = lax.axis_index("rows"), lax.axis_index("cols")
    last = lax.axis_size("rows") - 1
    info = jnp.stack([row % 2, col % 2, row == 0, row == last]).astype(jnp.int32)
    tables = constants(size)
    intensity = intensity[0, 0]
    plane, strip = shaped(extent, HALF), shaped(2, extent, HALF)
    corner = shaped(2, 2, MARGIN, HALF)

    edge, side = shaped(2, MARGIN, tile), shaped(2, tile, MARGIN)
    edge_a, edge_b, side_a, side_b = whole(cut_body, (edge, edge, side, side), (info,), (object_field,))
    halos = both_rows(edge_a, edge_b)
    far_edge, near_edge = swapped(side_b, "cols", 1), paired(side_a)
    measured, rolled = prepare(positions, intensity, probe)
    *ext, corner_a, corner_b = whole(
        extend_body,
        (plane, plane, strip, corner, corner),
        (info,),
        (object_field, *halos),
        unread=(measured,),
    )
    far_corner = swapped(corner_b, "cols", 1)
    sides = near_edge, paired(corner_a), far_edge, far_corner
    parts = gradient(True, info, positions, counts, ext, sides, measured, rolled, tables)
    total_a, halos_a, total_b, halos_b = summed(info, extent // 2, *parts)
    near_ext = whole(update_near_body, (plane, plane), (info,), (*ext[:2], total_a, *halos_a))
    far_ext = whole(update_far_body, (strip,), (info,), (ext[2], total_b, *halos_b))
    ext = (*near_ext, *far_ext)
    sides = paired(ext[0]), paired(ext[1]), swapped(ext[2], "cols", 1)
    parts = gradient(False, info, positions, counts, ext, sides, measured, rolled, tables)
    total_a, halos_a, total_b, halos_b = summed(info, MARGIN, *parts)
    return finished(info, tile, (*ext, total_a, total_b, *halos_a, *halos_b))


def solution(mesh):
    placed = (
        P(None, "rows", "cols"),
        P(),
        P("rows", "cols", None, None),
        P("rows", "cols"),
        P("rows", "cols", None, None, None),
    )
    return jax.shard_map(
        on_device, mesh=mesh, in_specs=placed, out_specs=P(None, "rows", "cols"), check_vma=False
    )
```
